32 devices in a mesh: dp: 16 (over z, x, core), ctx: 2 (over y).
Axes of the slice: x: 2, y: 2, z: 4, core: 2. Of those that a mesh axis runs over, the one named last changes fastest.
Arguments:
- block_in: bfloat16 [16, 256, 1088], P('dp', 'ctx'), may hold values from -6 to 6
- cotangent: bfloat16 [16, 256, 1088], P('dp', 'ctx'), may hold values from -6 to 6
- block_order: int32 [4], replicated, may hold values from 0 to 3, each once
- ln1_gain: bfloat16 [1088], P('dp'), may hold values from 0.25 to 1.75
- ln1_bias: bfloat16 [1088], P('dp'), may hold values from -2 to 2
- w_qkv: bfloat16 [1088, 3264], P('dp'), may hold values from -1 to 1
- b_query: bfloat16 [1088], P('dp'), may hold values from -2 to 2
- b_value: bfloat16 [1088], P('dp'), may hold values from -2 to 2
- w_out: bfloat16 [1088, 1088], P('dp'), may hold values from -1 to 1
- b_out: bfloat16 [1088], P('dp'), may hold values from -2 to 2
- ln2_gain: bfloat16 [1088], P('dp'), may hold values from 0.25 to 1.75
- ln2_bias: bfloat16 [1088], P('dp'), may hold values from -2 to 2
- w_up: bfloat16 [1088, 4352], P(None, 'dp'), may hold values from -0.1875 to 0.1875
- b_up: bfloat16 [4352], P('dp'), may hold values from -2 to 2
- w_down: bfloat16 [4352, 1088], P('dp'), may hold values from -0.09375 to 0.09375
- b_down: bfloat16 [1088], P('dp'), may hold values from -2 to 2
Outputs:
- block_out: bfloat16 [16, 256, 1088], P('dp', 'ctx')
- input_grad: float32 [16, 256, 1088], P('dp', 'ctx')
- g_ln1_gain: float32 [1088], P('dp')
- g_ln1_bias: float32 [1088], P('dp')
- g_w_qkv: float32 [1088, 3264], P('dp', 'ctx')
- g_b_query: float32 [1088], P('dp')
- g_b_value: float32 [1088], P('dp')
- g_w_out: float32 [1088, 1088], P('dp', 'ctx')
- g_b_out: float32 [1088], P('dp')
- g_ln2_gain: float32 [1088], P('dp')
- g_ln2_bias: float32 [1088], P('dp')
- g_w_up: float32 [1088, 4352], P('ctx', 'dp')
- g_b_up: float32 [4352], P('dp')
- g_w_down: float32 [4352, 1088], P('dp', 'ctx')
- g_b_down: float32 [1088], P('dp')
The draws below stay inside these ranges and needn't reach their ends.
Inputs may be any that keep to these rules, and one draw needn't show every extreme that they name: `block_order`: each block number appears once.
All inputs are finite; a program needn't handle non-finite values.
Results may differ from the reference program's by a relative error of at most 0.011.
Values may be sent and summed in bfloat16 or wider, within the bound.
A program may use at most 192 MiB of HBM per device.

```python
import math
import jax
import jax.numpy as jnp
from jax import lax

D = 1088
HEADS = 17
HD = 64
FF = 4352
BL = 64
SEQS = 16
BLOCKS = 4
SEQ = 256


def draw_w_qkv(key, part):
    scale = 1.0 / math.sqrt(D)
    drawn = jax.random.normal(jax.random.fold_in(key, 1), (D, 3 * D), jnp.float32) * scale
    return jnp.clip(drawn, -0.99, 0.99).astype(jnp.bfloat16)


def steps_of(stream_key, extent, cuts, smallest, high):
    loudness = 1.0
    for position, shards_of in cuts:
        steps = jax.random.uniform(jax.random.fold_in(jax.random.fold_in(stream_key, 6), position), (shards_of,), jnp.float32, smallest / len(cuts), high / len(cuts))
        loudness = loudness * jnp.repeat(jnp.exp(steps), extent[position] // shards_of).reshape((-1,) + (1,) * (len(extent) - 1 - position))
    return loudness


def scatter_about(rng, dims, width, reach, shards=(), held_as=jnp.bfloat16):
    values = jax.random.normal(rng, dims, jnp.float32) * width
    if len(shards) > 0:
        values = steps_of(rng, dims, shards, -0.22, 0.18) * values
    return jnp.clip(values, min=-reach, max=reach).astype(held_as)


def setup_inputs(seed: int = 0) -> dict:
    keys = jax.random.split(jax.random.key(seed), 17)
    block_in = scatter_about(keys[0], (SEQS, SEQ, D), 1.0, 6.0, ((0, 16), (1, 2)))
    cotangent = scatter_about(keys[1], (SEQS, SEQ, D), 1.0, 6.0, ((0, 16), (1, 2)))
    block_order = jax.random.permutation(keys[2], BLOCKS).astype(jnp.int32)
    ln1_gain = jnp.clip(1.0 + 0.15 * jax.random.normal(keys[3], (D,), jnp.float32), 0.25, 1.75).astype(jnp.bfloat16)
    ln1_bias = scatter_about(keys[4], (D,), 0.3, 2.0, ((0, 16),))
    w_qkv = draw_w_qkv(jax.random.fold_in(keys[16], 71), 0)
    b_query = scatter_about(keys[6], (D,), 0.3, 2.0, ((0, 16),))
    b_value = scatter_about(keys[7], (D,), 0.3, 2.0, ((0, 16),))
    w_out = scatter_about(keys[8], (D, D), (D // 32) ** -0.5, 1.0, ((0, 16),))
    b_out = scatter_about(keys[9], (D,), 0.3, 2.0, ((0, 16),))
    ln2_gain = jnp.clip(1.0 + 0.15 * jax.random.normal(keys[10], (D,), jnp.float32), 0.25, 1.75).astype(jnp.bfloat16)
    ln2_bias = scatter_about(keys[11], (D,), 0.3, 2.0, ((0, 16),))
    w_up = scatter_about(keys[12], (D, FF), D ** -0.5, 0.1875, ((1, 16),))
    b_up = scatter_about(keys[13], (FF,), 0.3, 2.0, ((0, 16),))
    w_down = scatter_about(keys[14], (FF, D), FF ** -0.5, 0.09375, ((0, 16),))
    b_down = scatter_about(keys[15], (D,), 0.3, 2.0, ((0, 16),))
    return {"block_in": block_in, "cotangent": cotangent, "block_order": block_order, "ln1_gain": ln1_gain, "ln1_bias": ln1_bias, "w_qkv": w_qkv, "b_query": b_query, "b_value": b_value, "w_out": w_out, "b_out": b_out, "ln2_gain": ln2_gain, "ln2_bias": ln2_bias, "w_up": w_up, "b_up": b_up, "w_down": w_down, "b_down": b_down}


def rounded(values):
    return lax.optimization_barrier(values.astype(jnp.bfloat16))

def norm_parts(values, gain_values, shift_values):
    average = lax.optimization_barrier(jnp.mean(values, axis=-1, keepdims=True))
    centered = values - average
    inverse = lax.rsqrt(lax.optimization_barrier(jnp.mean(centered * centered, axis=-1, keepdims=True)) + 1e-05)
    normed = centered * inverse
    return (normed * gain_values.astype(jnp.float32) + shift_values.astype(jnp.float32), normed, inverse)

def norm_back(upstream, normed, inverse, gain_values):
    scaled = upstream * gain_values.astype(jnp.float32)
    return inverse * (scaled - lax.optimization_barrier(jnp.mean(scaled, axis=-1, keepdims=True)) - normed * lax.optimization_barrier(jnp.mean(scaled * normed, axis=-1, keepdims=True)))

def gelu_slope(values):
    return 0.5 * (1.0 + lax.erf(values * 0.7071067811865476)) + values * jnp.exp(-0.5 * values * values) * 0.3989422804014327

def sequence_pass(inputs, upstream_b, positions, params):
    ln1_gain, ln1_bias, w_qkv, b_query, b_value, w_out, b_out, ln2_gain, ln2_bias, w_up, b_up, w_down, b_down = params
    length = inputs.shape[0]
    residual = inputs.astype(jnp.float32)
    normed_in_f, normed_one, inverse_one = norm_parts(residual, ln1_gain, ln1_bias)
    normed_in = rounded(normed_in_f)
    projected = jnp.dot(normed_in, w_qkv, preferred_element_type=jnp.float32)
    queries = rounded(projected[:, :D] + b_query.astype(jnp.float32))
    key_rows = rounded(projected[:, D:2 * D])
    value_rows = rounded(projected[:, 2 * D:] + b_value.astype(jnp.float32))
    query_f = queries.astype(jnp.float32).reshape(length, HEADS, HD)
    key_f = key_rows.astype(jnp.float32).reshape(length, HEADS, HD)
    value_f = value_rows.astype(jnp.float32).reshape(length, HEADS, HD)
    allowed = positions[:, None] >= positions[None, :]
    scores = jnp.where(allowed, jnp.einsum('qhd,khd->hqk', query_f, key_f) * 0.125, -1e+30)
    largest = lax.optimization_barrier(jnp.max(scores, axis=-1, keepdims=True))
    exponent = jnp.where(allowed, jnp.exp(scores - largest), 0.0)
    totals = lax.optimization_barrier(jnp.sum(exponent, axis=-1, keepdims=True))
    logsum = largest + jnp.log(totals)
    context = jnp.einsum('hqk,khd->qhd', exponent / totals, value_f, precision=lax.Precision.HIGHEST)
    attended = rounded(context.reshape(length, D))
    hidden_one = residual + jnp.dot(attended, w_out, preferred_element_type=jnp.float32) + b_out.astype(jnp.float32)
    normed_mid_f, normed_two, inverse_two = norm_parts(hidden_one, ln2_gain, ln2_bias)
    normed_mid = rounded(normed_mid_f)
    pre_act = jnp.dot(normed_mid, w_up, preferred_element_type=jnp.float32) + b_up.astype(jnp.float32)
    activated = rounded(jax.nn.gelu(pre_act, approximate=False))
    block_out = (hidden_one + jnp.dot(activated, w_down, preferred_element_type=jnp.float32) + b_down.astype(jnp.float32)).astype(jnp.bfloat16)
    upstream = upstream_b.astype(jnp.float32)
    grad_down = jnp.dot(activated.T, upstream_b, preferred_element_type=jnp.float32)
    grad_pre = jnp.dot(upstream_b, w_down.T, preferred_element_type=jnp.float32) * gelu_slope(pre_act)
    grad_pre_b = rounded(grad_pre)
    grad_up = jnp.dot(normed_mid.T, grad_pre_b, preferred_element_type=jnp.float32)
    grad_mid = jnp.dot(grad_pre_b, w_up.T, preferred_element_type=jnp.float32)
    grad_hidden = upstream + norm_back(grad_mid, normed_two, inverse_two, ln2_gain)
    grad_hidden_b = rounded(grad_hidden)
    grad_out_w = jnp.dot(attended.T, grad_hidden_b, preferred_element_type=jnp.float32)
    grad_context = rounded(jnp.dot(grad_hidden_b, w_out.T, preferred_element_type=jnp.float32))
    grad_ctx_f = grad_context.astype(jnp.float32).reshape(length, HEADS, HD)
    attended_f = attended.astype(jnp.float32).reshape(length, HEADS, HD)
    row_delta = jnp.einsum('qhd,qhd->hq', grad_ctx_f, attended_f)
    probability = jnp.where(allowed, jnp.exp(scores - logsum), 0.0)
    prob_b = rounded(probability).astype(jnp.float32)
    grad_value = jnp.einsum('hqk,qhd->khd', prob_b, grad_ctx_f)
    grad_prob = jnp.einsum('qhd,khd->hqk', grad_ctx_f, value_f)
    grad_score = rounded(probability * (grad_prob - row_delta[:, :, None])).astype(jnp.float32)
    grad_query = jnp.einsum('hqk,khd->qhd', grad_score, key_f) * 0.125
    grad_key = jnp.einsum('hqk,qhd->khd', grad_score, query_f) * 0.125
    grad_qkv = rounded(jnp.concatenate([grad_query.reshape(length, D), grad_key.reshape(length, D), grad_value.reshape(length, D)], axis=1))
    grad_qkv_w = jnp.dot(normed_in.T, grad_qkv, preferred_element_type=jnp.float32)
    grad_in_norm = jnp.dot(grad_qkv, w_qkv.T, preferred_element_type=jnp.float32)
    grad_input = grad_hidden + norm_back(grad_in_norm, normed_one, inverse_one, ln1_gain)
    grads = (lax.optimization_barrier(jnp.sum(grad_in_norm * normed_one, axis=0)), lax.optimization_barrier(jnp.sum(grad_in_norm, axis=0)), grad_qkv_w, lax.optimization_barrier(jnp.sum(grad_query, axis=0)).reshape(D), lax.optimization_barrier(jnp.sum(grad_value, axis=0)).reshape(D), grad_out_w, lax.optimization_barrier(jnp.sum(grad_hidden, axis=0)), lax.optimization_barrier(jnp.sum(grad_mid * normed_two, axis=0)), lax.optimization_barrier(jnp.sum(grad_mid, axis=0)), grad_up, lax.optimization_barrier(jnp.sum(grad_pre, axis=0)), grad_down, lax.optimization_barrier(jnp.sum(upstream, axis=0)))
    return (block_out, grad_input, grads)

def reference(block_in, cotangent, block_order, ln1_gain, ln1_bias, w_qkv, b_query, b_value, w_out, b_out, ln2_gain, ln2_bias, w_up, b_up, w_down, b_down):
    params = (ln1_gain, ln1_bias, w_qkv, b_query, b_value, w_out, b_out, ln2_gain, ln2_bias, w_up, b_up, w_down, b_down)
    slot_index = jnp.arange(SEQ, dtype=jnp.int32)
    positions = (block_order[slot_index // BL] * BL + slot_index % BL).astype(jnp.int32)
    empty_grads = tuple((jnp.zeros(member.shape, jnp.float32) for member in params))

    def visit(running, sequence_pair):
        out_rows, grad_rows, grads = sequence_pass(sequence_pair[0], sequence_pair[1], positions, params)
        return (tuple((left + right for left, right in zip(running, grads))), (out_rows, grad_rows))
    totals, outputs = lax.scan(visit, empty_grads, (block_in, cotangent))
    return (outputs[0], outputs[1], totals[0], totals[1], totals[2], totals[3], totals[4], totals[5], totals[6], totals[7], totals[8], totals[9], totals[10], totals[11], totals[12])
```

```python
import functools

import jax
import jax.numpy as jnp
from jax import lax
from jax.experimental import pallas as pl
from jax.experimental.pallas import tpu as pltpu
from jax.sharding import PartitionSpec as P

HD = 64
SCALE = 0.125


def norm_parts(values, gain_values, shift_values):
    average = jnp.mean(values, axis=-1, keepdims=True)
    centered = values - average
    inverse = lax.rsqrt(jnp.mean(centered * centered, axis=-1, keepdims=True) + 1e-05)
    normed = centered * inverse
    return normed * gain_values + shift_values, normed, inverse


def norm_back(upstream, normed, inverse, gain_values):
    scaled = upstream * gain_values
    return inverse * (
        scaled
        - jnp.mean(scaled, axis=-1, keepdims=True)
        - normed * jnp.mean(scaled * normed, axis=-1, keepdims=True)
    )


def gelu_slope(values):
    return (
        0.5 * (1.0 + lax.erf(values * 0.7071067811865476))
        + values * jnp.exp(-0.5 * values * values) * 0.3989422804014327
    )


def contract_first(left, right):
    return lax.dot_general(
        left, right, (((0,), (0,)), ((), ())), preferred_element_type=jnp.float32
    )


def contract_last(left, right):
    return lax.dot_general(
        left, right, (((1,), (1,)), ((), ())), preferred_element_type=jnp.float32
    )


def head_groups(width):
    groups = [(start, 128) for start in range(0, width - width % 128, 128)]
    if width % 128:
        groups.append((width - width % 128, width % 128))
    return groups


def head_masks(lanes):
    if lanes == HD:
        return [None]
    lane = lax.broadcasted_iota(jnp.int32, (1, lanes), 1)
    return [
        jnp.where((lane >= first) & (lane < first + HD), 1.0, 0.0).astype(jnp.bfloat16)
        for first in range(0, lanes, HD)
    ]


def keep(array, mask):
    return array if mask is None else array * mask


def visible_bias(query_pos_ref, key_pos_ref):
    return jnp.where(query_pos_ref[...] >= key_pos_ref[...], 0.0, -1e30)


def attend_kernel(query_pos_ref, key_pos_ref, q_ref, k_ref, v_ref, o_ref):
    bias = visible_bias(query_pos_ref, key_pos_ref)
    for start, lanes in head_groups(q_ref.shape[1]):
        block = slice(start, start + lanes)
        q, k, v = q_ref[:, block], k_ref[:, block], v_ref[:, block]
        total = None
        for mask in head_masks(lanes):
            scores = contract_last(keep(q, mask), k) * SCALE + bias
            largest = jnp.max(scores, axis=-1, keepdims=True)
            exponent = jnp.exp(scores - largest)
            inverse = 1.0 / jnp.sum(exponent, axis=-1, keepdims=True)
            part = (
                jnp.dot(
                    exponent.astype(jnp.bfloat16),
                    keep(v, mask),
                    preferred_element_type=jnp.float32,
                )
                * inverse
            )
            total = part if total is None else total + part
        o_ref[:, block] = total.astype(o_ref.dtype)


def attend_back_kernel(
    query_pos_ref,
    key_pos_ref,
    q_ref,
    k_ref,
    v_ref,
    do_ref,
    o_ref,
    dq_ref,
    dk_ref,
    dv_ref,
    dq_sum_ref,
    dv_sum_ref,
):
    bias = visible_bias(query_pos_ref, key_pos_ref)
    for start, lanes in head_groups(q_ref.shape[1]):
        block = slice(start, start + lanes)
        q, k, v = q_ref[:, block], k_ref[:, block], v_ref[:, block]
        do, o = do_ref[:, block], o_ref[:, block]
        product = do.astype(jnp.float32) * o.astype(jnp.float32)
        dq = dk = dv = None
        for mask in head_masks(lanes):
            q_h, k_h, do_h = keep(q, mask), keep(k, mask), keep(do, mask)
            product_h = product if mask is None else product * mask.astype(jnp.float32)
            delta = jnp.sum(product_h, axis=-1, keepdims=True)
            scores = contract_last(q_h, k) * SCALE + bias
            largest = jnp.max(scores, axis=-1, keepdims=True)
            exponent = jnp.exp(scores - largest)
            p = exponent * (1.0 / jnp.sum(exponent, axis=-1, keepdims=True))
            dp = contract_last(do_h, v)
            ds = (p * (dp - delta)).astype(jnp.bfloat16)
            dv_h = contract_first(p.astype(jnp.bfloat16), do_h)
            dq_h = jnp.dot(ds, k_h, preferred_element_type=jnp.float32)
            dk_h = contract_first(ds, q_h)
            dq = dq_h if dq is None else dq + dq_h
            dk = dk_h if dk is None else dk + dk_h
            dv = dv_h if dv is None else dv + dv_h
        dq = dq * SCALE
        dq_ref[:, block] = dq.astype(dq_ref.dtype)
        dk_ref[:, block] = (dk * SCALE).astype(dk_ref.dtype)
        dv_ref[:, block] = dv.astype(dv_ref.dtype)
        dq_sum_ref[:, block] = jnp.sum(dq, axis=0, keepdims=True)
        dv_sum_ref[:, block] = jnp.sum(dv, axis=0, keepdims=True)


def whole_vmem(count):
    return [pl.BlockSpec(memory_space=pltpu.VMEM)] * count


def attend(query_pos, key_pos, q, k, v):
    rows, width = q.shape
    keys = k.shape[0]
    return pl.pallas_call(
        attend_kernel,
        out_shape=jax.ShapeDtypeStruct((rows, width), jnp.bfloat16),
        in_specs=whole_vmem(5),
        out_specs=pl.BlockSpec(memory_space=pltpu.VMEM),
        cost_estimate=pl.CostEstimate(
            flops=8 * rows * keys * width,
            bytes_accessed=4 * (rows + keys) * width,
            transcendentals=rows * keys * (width // HD),
        ),
    )(query_pos, key_pos, q, k, v)


def attend_back(query_pos, key_pos, q, k, v, do, o):
    rows, width = q.shape
    keys = k.shape[0]
    return pl.pallas_call(
        attend_back_kernel,
        out_shape=(
            jax.ShapeDtypeStruct((rows, width), jnp.bfloat16),
            jax.ShapeDtypeStruct((keys, width), jnp.bfloat16),
            jax.ShapeDtypeStruct((keys, width), jnp.bfloat16),
            jax.ShapeDtypeStruct((1, width), jnp.float32),
            jax.ShapeDtypeStruct((1, width), jnp.float32),
        ),
        in_specs=whole_vmem(7),
        out_specs=tuple(whole_vmem(5)),
        cost_estimate=pl.CostEstimate(
            flops=20 * rows * keys * width,
            bytes_accessed=8 * (rows + keys) * width,
            transcendentals=rows * keys * (width // HD),
        ),
    )(query_pos, key_pos, q, k, v, do, o)


MESH = pl.DeviceIdType.MESH
CORES = 2
COLUMNS = 2
VMEM_LIMIT = 63 * 1024 * 1024
SIDES = ((1, 2), (-1, 3))


def place():
    index = lax.axis_index("dp")
    lines = lax.axis_size("dp") // (CORES * COLUMNS)
    core = index % CORES
    column = (index // CORES) % COLUMNS
    return index // (CORES * COLUMNS), column, core, lines


def device_at(line, column, core):
    return (line * COLUMNS + column) * CORES + core


def on_line(line, lines):
    return (line >= 0) & (line < lines)


def greet():
    line, column, core, lines = place()
    barrier = pltpu.get_barrier_semaphore()
    peers = [device_at((line + by) % lines, column, core) for by in range(1, lines)]
    peers += [device_at(line, 1 - column, core), device_at(line, column, 1 - core)]
    for peer in peers:
        pl.semaphore_signal(barrier, inc=1, device_id={"dp": peer}, device_id_type=MESH)
    pl.semaphore_wait(barrier, len(peers))


def gather_kernel(count, *refs):
    ins, outs = refs[:count], refs[count : 2 * count]
    send_sem, recv_sem, local_sem = refs[2 * count :]
    line, column, core, lines = place()
    me = device_at(line, column, core)
    greet()

    def describe(a, shard, target, way, slot, own=False):
        return pltpu.make_async_remote_copy(
            src_ref=ins[a] if own else outs[a].at[shard],
            dst_ref=outs[a].at[shard],
            send_sem=send_sem.at[a, way, slot],
            recv_sem=recv_sem.at[a, shard],
            device_id={"dp": target},
            device_id_type=MESH,
        )

    def push(*what, own=False):
        describe(*what, own=own).start()

    def arrived(a, shard):
        describe(a, shard, partner, 0, 0).wait_recv()

    def sent(a, way, slot):
        describe(a, me, partner, way, slot).wait_send()

    beside = device_at(line, 1 - column, core)
    partner = device_at(line, column, 1 - core)

    def along(step):
        return device_at(line + step, column, core)

    for a in range(count):
        push(a, me, beside, 1, 0, own=True)
        for step, way in SIDES:

            @pl.when(on_line(line + step, lines))
            def _():
                push(a, me, along(step), way, 0, own=True)

        push(a, me, partner, 4, 0, own=True)
    for a in range(count):
        pltpu.make_async_copy(ins[a], outs[a].at[me], local_sem.at[a]).start()
    for by in range(1, lines):
        for a in range(count):
            for step, way in SIDES:

                @pl.when(on_line(line - step * by, lines))
                def _():
                    shard = along(-step * by)
                    arrived(a, shard)

                    @pl.when(on_line(line + step, lines))
                    def _():
                        push(a, shard, along(step), way, by)

                    push(a, shard, beside, 1, lines + step * by)
                    push(a, shard, partner, 4, lines + step * by)

    for a in range(count):
        arrived(a, device_at(line, 1 - column, core))
        push(a, device_at(line, 1 - column, core), partner, 4, 2 * lines)
    for by in range(1, lines):
        for a in range(count):
            for step, _ in SIDES:

                @pl.when(on_line(line - step * by, lines))
                def _():
                    shard = device_at(line - step * by, 1 - column, core)
                    arrived(a, shard)
                    push(a, shard, partner, 4, 3 * lines + step * by)

    for a in range(count):
        for by in range(lines):
            for across in range(COLUMNS):
                arrived(a, device_at(by, across, 1 - core))
    for a in range(count):
        sent(a, 1, 0)
        sent(a, 4, 0)
        sent(a, 4, 2 * lines)
        for step, way in SIDES:

            @pl.when(on_line(line + step, lines))
            def _():
                sent(a, way, 0)

            for by in range(1, lines):

                @pl.when(on_line(line - step * by, lines))
                def _():
                    @pl.when(on_line(line + step, lines))
                    def _():
                        sent(a, way, by)

                    sent(a, 1, lines + step * by)
                    sent(a, 4, lines + step * by)
                    sent(a, 4, 3 * lines + step * by)

        pltpu.make_async_copy(ins[a], outs[a].at[me], local_sem.at[a]).wait()


def gather_dp(arrays, collective_id):
    peers = lax.axis_size("dp")
    count = len(arrays)
    lines = peers // (CORES * COLUMNS)
    return pl.pallas_call(
        functools.partial(gather_kernel, count),
        out_shape=tuple(jax.ShapeDtypeStruct((peers,) + a.shape, a.dtype) for a in arrays),
        in_specs=whole_vmem(count),
        out_specs=tuple([pl.BlockSpec(memory_space=pl.ANY)] * count),
        scratch_shapes=[
            pltpu.SemaphoreType.DMA((count, 5, 4 * lines)),
            pltpu.SemaphoreType.DMA((count, peers)),
            pltpu.SemaphoreType.DMA((count,)),
        ],
        compiler_params=pltpu.CompilerParams(
            collective_id=collective_id, has_side_effects=True, vmem_limit_bytes=VMEM_LIMIT
        ),
    )(*arrays)


def reduce_kernel(count, *refs):
    ins, outs = refs[:count], refs[count : 2 * count]
    core_bufs, side_bufs, up_bufs, down_bufs, side_sends, line_sends = [
        refs[(2 + i) * count : (3 + i) * count] for i in range(6)
    ]
    send_sem, recv_sem = refs[8 * count :]
    line, column, core, lines = place()
    beside = device_at(line, 1 - column, core)
    partner = device_at(line, column, 1 - core)
    greet()

    def describe(a, source, landing, target, way, slot):
        return pltpu.make_async_remote_copy(
            src_ref=source,
            dst_ref=landing,
            send_sem=send_sem.at[a, way, slot],
            recv_sem=recv_sem.at[a, way, slot],
            device_id={"dp": target},
            device_id_type=MESH,
        )

    def arrived(a, landing, way, slot):
        describe(a, landing, landing, partner, way, slot).wait_recv()
        return landing[...].astype(jnp.float32)

    def for_lines(visit):
        for by in range(lines - 1, 0, -1):
            for a in range(count):
                for step, _ in SIDES:

                    @pl.when(on_line(line + step * by, lines))
                    def _():
                        visit(a, line + step * by, step, by)

        for a in range(count):
            visit(a, line, 0, 0)

    def to_partner(across):
        def visit(a, target, step, by):
            slot = target if across is beside else lines + target
            shard = device_at(target, 1 - column if across is beside else column, 1 - core)
            describe(a, ins[a].at[shard], core_bufs[a].at[slot], partner, 0, slot).start()

        return visit

    def to_beside(a, target, step, by):
        total = arrived(a, core_bufs[a].at[target], 0, target)
        total = total + ins[a][device_at(target, 1 - column, core)].astype(jnp.float32)
        side_sends[a][target] = total.astype(side_sends[a].dtype)
        describe(
            a, side_sends[a].at[target], side_bufs[a].at[target], beside, 1, target
        ).start()

    def along(a, target, step, by):
        total = arrived(a, core_bufs[a].at[lines + target], 0, lines + target)
        total = total + ins[a][device_at(target, column, core)].astype(jnp.float32)
        total = total + arrived(a, side_bufs[a].at[target], 1, target)
        if step == 0:
            outs[a][...] = total
        else:
            way, landing = (2, up_bufs[a]) if step > 0 else (3, down_bufs[a])
            line_sends[a][target] = total.astype(line_sends[a].dtype)

            @pl.when(on_line(line - step, lines))
            def _():
                more = arrived(a, landing.at[target], way, target)
                line_sends[a][target] = (total + more).astype(line_sends[a].dtype)

            describe(
                a,
                line_sends[a].at[target],
                landing.at[target],
                device_at(line + step, column, core),
                way,
                target,
            ).start()

    for_lines(to_partner(beside))
    for_lines(to_partner(None))
    for_lines(to_beside)
    for_lines(along)
    for a in range(count):
        for step, way, landing in ((1, 2, up_bufs[a]), (-1, 3, down_bufs[a])):

            @pl.when(on_line(line - step, lines))
            def _():
                outs[a][...] += arrived(a, landing.at[line], way, line)

    def sent(a, target, step, by):
        buffer = line_sends[a].at[target]
        describe(a, buffer, buffer, partner, 0, target).wait_send()
        describe(a, buffer, buffer, partner, 0, lines + target).wait_send()
        describe(a, buffer, buffer, partner, 1, target).wait_send()
        if step:
            describe(a, buffer, buffer, partner, 2 if step > 0 else 3, target).wait_send()

    for_lines(sent)


def reduce_dp(arrays, collective_id):
    peers = lax.axis_size("dp")
    count = len(arrays)
    lines = peers // (CORES * COLUMNS)
    buffers = []
    for size in (2 * lines, lines, lines, lines, lines, lines):
        buffers += [pltpu.VMEM((size,) + a.shape[1:], a.dtype) for a in arrays]
    return pl.pallas_call(
        functools.partial(reduce_kernel, count),
        out_shape=tuple(jax.ShapeDtypeStruct(a.shape[1:], jnp.float32) for a in arrays),
        in_specs=whole_vmem(count),
        out_specs=tuple(whole_vmem(count)),
        scratch_shapes=buffers
        + [
            pltpu.SemaphoreType.DMA((count, 4, 2 * lines)),
            pltpu.SemaphoreType.DMA((count, 4, 2 * lines)),
        ],
        compiler_params=pltpu.CompilerParams(
            collective_id=collective_id, has_side_effects=True, vmem_limit_bytes=VMEM_LIMIT
        ),
    )(*arrays)


UP, DOWN, ACROSS, PARTNER = range(4)


def ffn_kernel(
    mid_ref,
    ups_ref,
    w_up_ref,
    w_up_t_ref,
    w_down_ref,
    w_down_t_ref,
    b_up_ref,
    gm_ref,
    br_ref,
    gup_ref,
    gdown_ref,
    gb_ref,
    mids,
    parts,
    acts,
    grads,
    core_buf,
    side_buf,
    up_buf,
    down_buf,
    side_send,
    line_send,
    g_send,
    g_recv,
    r_send,
    r_recv,
):
    line, column, core, lines = place()
    rows, width = mid_ref.shape
    me = device_at(line, column, core)
    beside = device_at(line, 1 - column, core)
    partner = device_at(line, column, 1 - core)
    greet()

    def copy(source, landing, send, recv, target):
        return pltpu.make_async_remote_copy(
            src_ref=source,
            dst_ref=landing,
            send_sem=send,
            recv_sem=recv,
            device_id={"dp": target},
            device_id_type=MESH,
        )

    def push(shard, way, target, own=False):
        source = mid_ref if own else mids.at[shard]
        copy(source, mids.at[shard], g_send.at[way, shard], g_recv.at[shard], target).start()

    def arrived(shard):
        buffer = mids.at[shard]
        copy(buffer, buffer, g_send.at[PARTNER, shard], g_recv.at[shard], partner).wait_recv()

    def sent(shard, way):
        buffer = mids.at[shard]
        copy(buffer, buffer, g_send.at[way, shard], g_recv.at[shard], partner).wait_send()

    sides = ((1, UP), (-1, DOWN))
    push(me, ACROSS, beside, own=True)
    for step, way in sides:

        @pl.when(on_line(line + step, lines))
        def _():
            push(me, way, device_at(line + step, column, core), own=True)

    push(me, PARTNER, partner, own=True)
    mids[me] = mid_ref[...]
    gb_ref[...] = jnp.zeros_like(gb_ref)

    def relay(by):
        for step, way in sides:

            @pl.when(on_line(line - step * by, lines))
            def _():
                shard = device_at(line - step * by, column, core)
                arrived(shard)

                @pl.when(on_line(line + step, lines))
                def _():
                    push(shard, way, device_at(line + step, column, core))

                push(shard, ACROSS, beside)
                push(shard, PARTNER, partner)

    toward = 1 - 2 * ((2 * line) // lines)

    def feed(chip):
        pair = pl.ds(chip * CORES, CORES)
        mid = mids[pair].reshape(CORES * rows, width)
        ups = ups_ref[pair].reshape(CORES * rows, width)
        pre = jnp.dot(mid, w_up_ref[...], preferred_element_type=jnp.float32) + b_up_ref[...]
        grad = jnp.dot(ups, w_down_t_ref[...], preferred_element_type=jnp.float32)
        half = 0.5 * (1.0 + lax.erf(pre * 0.7071067811865476))
        act = (pre * half).astype(jnp.bfloat16)
        grad = grad * (half + pre * jnp.exp(-0.5 * pre * pre) * 0.3989422804014327)
        gb_ref[...] += jnp.sum(grad, axis=0, keepdims=True)
        grad = grad.astype(jnp.bfloat16)
        acts[chip] = act
        grads[chip] = grad
        part = jnp.dot(grad, w_up_t_ref[...], preferred_element_type=jnp.float32)
        parts[pair] = part.astype(jnp.bfloat16).reshape(CORES, rows, width)
        copy(
            parts.at[chip * CORES + 1 - core],
            core_buf.at[chip],
            r_send.at[0, chip],
            r_recv.at[0, chip],
            partner,
        ).start()
        branch = jnp.dot(act, w_down_ref[...], preferred_element_type=jnp.float32)
        br_ref[pair] = branch.astype(jnp.bfloat16).reshape(CORES, rows, width)

    def visit(d, carry):
        @pl.when(d + 1 < lines)
        def _():
            relay(d + 1)

        at = (line + toward * d + lines) % lines
        arrived(device_at(at, column, 1 - core))
        feed(at * COLUMNS + column)
        far = device_at(at, 1 - column, core)
        arrived(far)
        push(far, PARTNER, partner)
        arrived(device_at(at, 1 - column, 1 - core))
        feed(at * COLUMNS + 1 - column)
        return carry

    lax.fori_loop(0, lines, visit, 0)

    def landed(buffer, way, slot):
        copy(buffer, buffer, r_send.at[way, slot], r_recv.at[way, slot], partner).wait_recv()
        return buffer[...].astype(jnp.float32)

    def for_lines(act):
        for by in range(lines - 1, 0, -1):
            for step in (1, -1):

                @pl.when(on_line(line + step * by, lines))
                def _():
                    act(line + step * by, step)

        act(line, 0)

    def to_beside(target, step):
        chip = target * COLUMNS + 1 - column
        total = landed(core_buf.at[chip], 0, chip)
        total = total + parts[chip * CORES + core].astype(jnp.float32)
        side_send[target] = total.astype(side_send.dtype)
        copy(
            side_send.at[target],
            side_buf.at[target],
            r_send.at[1, target],
            r_recv.at[1, target],
            beside,
        ).start()

    def along(target, step):
        chip = target * COLUMNS + column
        total = landed(core_buf.at[chip], 0, chip)
        total = total + parts[chip * CORES + core].astype(jnp.float32)
        total = total + landed(side_buf.at[target], 1, target)
        if step == 0:
            gm_ref[...] = total
        else:
            way, landing = (2, up_buf) if step > 0 else (3, down_buf)
            line_send[target] = total.astype(line_send.dtype)

            @pl.when(on_line(line - step, lines))
            def _():
                more = landed(landing.at[target], way, target)
                line_send[target] = (total + more).astype(line_send.dtype)

            copy(
                line_send.at[target],
                landing.at[target],
                r_send.at[way, target],
                r_recv.at[way, target],
                device_at(line + step, column, core),
            ).start()

    for_lines(to_beside)
    gup_ref[...] = jnp.zeros_like(gup_ref)
    gdown_ref[...] = jnp.zeros_like(gdown_ref)

    def weigh(chip, carry):
        pair = pl.ds(chip * CORES, CORES)
        gup_ref[...] += contract_first(grads[chip], mids[pair].reshape(CORES * rows, width))
        gdown_ref[...] += contract_first(acts[chip], ups_ref[pair].reshape(CORES * rows, width))
        return carry

    lax.fori_loop(0, lines * COLUMNS, weigh, 0)
    for_lines(along)
    for step, way, landing in ((1, 2, up_buf), (-1, 3, down_buf)):

        @pl.when(on_line(line - step, lines))
        def _():
            gm_ref[...] += landed(landing.at[line], way, line)

    def reduce_sent(target, step):
        buffer = line_send.at[target]
        slots = [(0, target * COLUMNS), (0, target * COLUMNS + 1), (1, target)]
        if step:
            slots.append((2 if step > 0 else 3, target))
        for way, slot in slots:
            copy(buffer, buffer, r_send.at[way, slot], r_recv.at[way, slot], partner).wait_send()

    for_lines(reduce_sent)

    def gather_sent(target, step):
        shard = device_at(target, column, core)
        sent(shard, ACROSS)
        sent(shard, PARTNER)
        sent(device_at(target, 1 - column, core), PARTNER)
        for way_step, way in sides:
            if step in (0, -way_step):

                @pl.when(on_line(line + way_step, lines))
                def _():
                    sent(shard, way)

    for_lines(gather_sent)


def feed_forward(mid, ups, w_up, w_down, b_up, collective_id):
    peers = lax.axis_size("dp")
    lines = peers // (CORES * COLUMNS)
    chips = lines * COLUMNS
    rows, width = mid.shape
    hidden = w_up.shape[1]

    def slabs(count):
        return pltpu.VMEM((count, rows, width), jnp.bfloat16)

    return pl.pallas_call(
        ffn_kernel,
        out_shape=(
            jax.ShapeDtypeStruct((rows, width), jnp.float32),
            jax.ShapeDtypeStruct((peers, rows, width), jnp.bfloat16),
            jax.ShapeDtypeStruct((hidden, width), jnp.float32),
            jax.ShapeDtypeStruct((hidden, width), jnp.float32),
            jax.ShapeDtypeStruct((1, hidden), jnp.float32),
        ),
        in_specs=whole_vmem(7),
        out_specs=tuple(whole_vmem(5)),
        scratch_shapes=[
            slabs(peers),
            slabs(peers),
            pltpu.VMEM((chips, CORES * rows, hidden), jnp.bfloat16),
            pltpu.VMEM((chips, CORES * rows, hidden), jnp.bfloat16),
            slabs(chips),
            slabs(lines),
            slabs(lines),
            slabs(lines),
            slabs(lines),
            slabs(lines),
            pltpu.SemaphoreType.DMA((4, peers)),
            pltpu.SemaphoreType.DMA((peers,)),
            pltpu.SemaphoreType.DMA((4, chips)),
            pltpu.SemaphoreType.DMA((4, chips)),
        ],
        compiler_params=pltpu.CompilerParams(
            collective_id=collective_id, has_side_effects=True, vmem_limit_bytes=VMEM_LIMIT
        ),
    )(mid, ups, w_up, w_up.T, w_down, w_down.T, b_up.astype(jnp.float32)[None, :])


def shift(array, axis, by):
    peers = lax.axis_size(axis)
    return lax.ppermute(array, axis, [(i, (i + by) % peers) for i in range(peers)])


def gather_direct(array, axis):
    peers = lax.axis_size(axis)
    mine = lax.axis_index(axis)
    held = [array] + [shift(array, axis, by) for by in range(1, peers)]
    stacked = jnp.zeros((peers,) + array.shape, array.dtype)
    for by in range(peers):
        stacked = lax.dynamic_update_index_in_dim(stacked, held[by], (mine - by) % peers, 0)
    return stacked


def scatter_direct(array, axis, dim):
    peers = lax.axis_size(axis)
    mine = lax.axis_index(axis)
    size = array.shape[dim] // peers

    def piece(owner):
        return lax.dynamic_slice_in_dim(array, owner * size, size, dim)

    total = piece(mine).astype(jnp.float32)
    for by in range(1, peers):
        sent = piece((mine + by) % peers).astype(jnp.bfloat16)
        total = total + shift(sent, axis, by).astype(jnp.float32)
    return total


def per_device(
    block_in,
    cotangent,
    block_order,
    ln1_gain,
    ln1_bias,
    w_qkv,
    b_query,
    b_value,
    w_out,
    b_out,
    ln2_gain,
    ln2_bias,
    w_up,
    b_up,
    w_down,
    b_down,
):
    inputs = block_in[0]
    row_count, width = inputs.shape
    peers = lax.axis_size("dp")
    cycle_size = lax.axis_size("ctx")
    owner_index = lax.axis_index("ctx")
    all_rows = row_count * cycle_size
    shard = width // peers

    vectors = jnp.stack(
        [ln1_gain, ln1_bias, b_query, b_value, b_out, ln2_gain, ln2_bias, b_down]
    )
    upstream_b = cotangent[0]
    vectors, qkv_full, out_full, upstream_all = gather_dp(
        [vectors, w_qkv, w_out, upstream_b], 0
    )
    qkv_full = qkv_full.reshape(width, 3 * width)
    out_full = out_full.reshape(width, width)

    vectors = jnp.transpose(vectors, (1, 0, 2)).reshape(8, width).astype(jnp.float32)
    gain_one, shift_one, bias_query, bias_value, bias_out, gain_two, shift_two, bias_down = [
        vectors[i] for i in range(8)
    ]

    slots = jnp.arange(all_rows, dtype=jnp.int32)
    block_rows = all_rows // block_order.shape[0]
    positions = block_order[slots // block_rows] * block_rows + slots % block_rows
    key_pos = positions[None, :]
    query_pos = lax.dynamic_slice_in_dim(positions, owner_index * row_count, row_count)[:, None]

    residual = inputs.astype(jnp.float32)
    normed_in_f, normed_one, inverse_one = norm_parts(residual, gain_one, shift_one)
    normed_in = normed_in_f.astype(jnp.bfloat16)
    projected = jnp.dot(normed_in, qkv_full, preferred_element_type=jnp.float32)
    bias_qkv = jnp.concatenate([bias_query, jnp.zeros((width,), jnp.float32), bias_value])
    projected_b = (projected + bias_qkv).astype(jnp.bfloat16)
    query_b = projected_b[:, :width]
    keys_values = gather_direct(projected_b[:, width:], "ctx").reshape(all_rows, 2 * width)
    key_all, value_all = keys_values[:, :width], keys_values[:, width:]
    attended = attend(query_pos, key_pos, query_b, key_all, value_all)

    hidden_one = (
        residual
        + jnp.dot(attended, out_full, preferred_element_type=jnp.float32)
        + bias_out
    )
    normed_mid_f, normed_two, inverse_two = norm_parts(hidden_one, gain_two, shift_two)
    normed_mid = normed_mid_f.astype(jnp.bfloat16)
    upstream = upstream_b.astype(jnp.float32)
    grad_mid, branch_parts, grad_up, grad_down, grad_bias_up = feed_forward(
        normed_mid, upstream_all, w_up, w_down, b_up, 1
    )
    grad_bias_up = grad_bias_up[0]
    g_up = scatter_direct(grad_up, "ctx", 1).T
    g_down = scatter_direct(grad_down, "ctx", 1)

    grad_hidden = upstream + norm_back(grad_mid, normed_two, inverse_two, gain_two)
    grad_hidden_b = grad_hidden.astype(jnp.bfloat16)
    grad_ctx_b = contract_last(grad_hidden_b, out_full).astype(jnp.bfloat16)
    grad_query, grad_key, grad_value, query_sum, value_sum = attend_back(
        query_pos, key_pos, query_b, key_all, value_all, grad_ctx_b, attended
    )
    grad_kv = scatter_direct(jnp.concatenate([grad_key, grad_value], axis=1), "ctx", 0)
    grad_qkv = jnp.concatenate([grad_query, grad_kv.astype(jnp.bfloat16)], axis=1)

    def by_owner(left, right):
        left = left.reshape(row_count, peers, shard)
        return jnp.einsum("tnd,tc->ndc", left, right, preferred_element_type=jnp.float32).astype(
            jnp.bfloat16
        )

    grad_in_norm = contract_last(grad_qkv, qkv_full)
    grad_input = grad_hidden + norm_back(grad_in_norm, normed_one, inverse_one, gain_one)

    sums = jnp.stack(
        [
            jnp.sum(grad_in_norm * normed_one, axis=0),
            jnp.sum(grad_in_norm, axis=0),
            query_sum[0],
            value_sum[0],
            jnp.sum(grad_hidden, axis=0),
            jnp.sum(grad_mid * normed_two, axis=0),
            jnp.sum(grad_mid, axis=0),
            jnp.sum(upstream, axis=0),
        ]
    )
    sums = jnp.transpose(sums.reshape(8, peers, shard), (1, 0, 2))
    qkv_dp, out_dp, sums, branch_out = reduce_dp(
        [
            by_owner(normed_in, grad_qkv),
            by_owner(attended, grad_hidden_b),
            sums,
            branch_parts,
        ],
        3,
    )
    block_out = (hidden_one + branch_out + bias_down).astype(jnp.bfloat16)
    g_out = scatter_direct(out_dp, "ctx", 1)
    g_qkv = scatter_direct(qkv_dp, "ctx", 1)
    sums = jnp.sum(gather_direct(sums, "ctx"), axis=0)
    g_bias_up = jnp.sum(gather_direct(grad_bias_up, "ctx"), axis=0)
    return (
        block_out[None],
        grad_input[None],
        sums[0],
        sums[1],
        g_qkv,
        sums[2],
        sums[3],
        g_out,
        sums[4],
        sums[5],
        sums[6],
        g_up,
        g_bias_up,
        g_down,
        sums[7],
    )


def solution(mesh):
    in_specs = (
        P("dp", "ctx", None),
        P("dp", "ctx", None),
        P(),
        P("dp"),
        P("dp"),
        P("dp", None),
        P("dp"),
        P("dp"),
        P("dp", None),
        P("dp"),
        P("dp"),
        P("dp"),
        P(None, "dp"),
        P("dp"),
        P("dp", None),
        P("dp"),
    )
    out_specs = (
        P("dp", "ctx", None),
        P("dp", "ctx", None),
        P("dp"),
        P("dp"),
        P("dp", "ctx"),
        P("dp"),
        P("dp"),
        P("dp", "ctx"),
        P("dp"),
        P("dp"),
        P("dp"),
        P("ctx", "dp"),
        P("dp"),
        P("dp", "ctx"),
        P("dp"),
    )
    return jax.shard_map(
        per_device, mesh=mesh, in_specs=in_specs, out_specs=out_specs, check_vma=False
    )
```

```python
import functools
import types

import jax
import jax.numpy as jnp
from jax import lax
from jax.experimental import pallas as pl
from jax.experimental.pallas import tpu as pltpu
from jax.sharding import PartitionSpec as P

HD = 64
SCALE = 0.125


def norm_parts(values, gain_values, shift_values):
    average = jnp.mean(values, axis=-1, keepdims=True)
    centered = values - average
    inverse = lax.rsqrt(jnp.mean(centered * centered, axis=-1, keepdims=True) + 1e-05)
    normed = centered * inverse
    return normed * gain_values + shift_values, normed, inverse


def norm_back(upstream, normed, inverse, gain_values):
    scaled = upstream * gain_values
    return inverse * (
        scaled
        - jnp.mean(scaled, axis=-1, keepdims=True)
        - normed * jnp.mean(scaled * normed, axis=-1, keepdims=True)
    )


def contract_first(left, right):
    return lax.dot_general(
        left, right, (((0,), (0,)), ((), ())), preferred_element_type=jnp.float32
    )


def contract_last(left, right):
    return lax.dot_general(
        left, right, (((1,), (1,)), ((), ())), preferred_element_type=jnp.float32
    )


def head_groups(width):
    groups = [(start, 128) for start in range(0, width - width % 128, 128)]
    if width % 128:
        groups.append((width - width % 128, width % 128))
    return groups


def head_masks(lanes):
    if lanes == HD:
        return [None]
    lane = lax.broadcasted_iota(jnp.int32, (1, lanes), 1)
    return [
        jnp.where((lane >= first) & (lane < first + HD), 1.0, 0.0).astype(jnp.bfloat16)
        for first in range(0, lanes, HD)
    ]


def keep(array, mask):
    return array if mask is None else array * mask


MESH = pl.DeviceIdType.MESH
CORES = 2
COLUMNS = 2
VMEM_LIMIT = 63 * 1024 * 1024
UP, DOWN, ACROSS, PARTNER = range(4)
SIDES = ((1, UP), (-1, DOWN))
GROUP = 8
FUSED_LIMIT = 14 * 1024 * 1024


def place():
    index = lax.axis_index("dp")
    lines = lax.axis_size("dp") // (CORES * COLUMNS)
    core = index % CORES
    column = (index // CORES) % COLUMNS
    return index // (CORES * COLUMNS), column, core, lines


def device_at(line, column, core):
    return (line * COLUMNS + column) * CORES + core


def on_line(line, lines):
    return (line >= 0) & (line < lines)


def greet():
    line, column, core, lines = place()
    cycle = lax.axis_size("ctx")
    mine = lax.axis_index("ctx")
    barrier = pltpu.get_barrier_semaphore()
    peers = [{"dp": device_at((line + by) % lines, column, core)} for by in range(1, lines)]
    peers += [{"dp": device_at(line, 1 - column, core)}, {"dp": device_at(line, column, 1 - core)}]
    peers += [{"ctx": (mine + by) % cycle} for by in range(1, cycle)]
    for peer in peers:
        pl.semaphore_signal(barrier, inc=1, device_id=peer, device_id_type=MESH)
    pl.semaphore_wait(barrier, len(peers))


def remote(source, landing, send, recv, target):
    return pltpu.make_async_remote_copy(
        src_ref=source,
        dst_ref=landing,
        send_sem=send,
        recv_sem=recv,
        device_id=target,
        device_id_type=MESH,
    )


def on_distance(by, act):
    line, _, _, lines = place()
    if by == 0:
        act(line, 0)
        return
    for step in (1, -1):

        @pl.when(on_line(line + step * by, lines))
        def _():
            act(line + step * by, step)


def nearest(d):
    line, _, _, lines = place()
    toward = 1 - 2 * ((2 * line) // lines)
    return (line + toward * d + lines) % lines


def gather_stream(own, land, send, recv, balanced):
    line, column, core, lines = place()
    me = device_at(line, column, core)
    beside = device_at(line, 1 - column, core)
    partner = device_at(line, column, 1 - core)

    def push(shard, way, target, source=None):
        source = land(shard) if source is None else source
        remote(source, land(shard), send(way, shard), recv(shard), {"dp": target}).start()

    def arrived(shard):
        buffer = land(shard)
        remote(buffer, buffer, send(PARTNER, shard), recv(shard), {"dp": partner}).wait_recv()

    def sent(shard, way):
        buffer = land(shard)
        remote(buffer, buffer, send(way, shard), recv(shard), {"dp": partner}).wait_send()

    def start():
        push(me, ACROSS, beside, own)
        for step, way in SIDES:

            @pl.when(on_line(line + step, lines))
            def _():
                push(me, way, device_at(line + step, column, core), own)

        push(me, PARTNER, partner, own)

    def crosses(source, act):
        if balanced:

            @pl.when((source != 0) & (source != lines - 1))
            def _():
                act()

        else:
            act()

    def relay(by, seen=None):
        for step, way in SIDES:

            @pl.when(on_line(line - step * by, lines))
            def _():
                shard = device_at(line - step * by, column, core)
                arrived(shard)

                @pl.when(on_line(line + step, lines))
                def _():
                    push(shard, way, device_at(line + step, column, core))

                crosses(line - step * by, lambda: push(shard, ACROSS, beside))
                push(shard, PARTNER, partner)
                if seen is not None:
                    seen(shard)

    def through(source, act):
        if balanced:
            for step, way in SIDES:
                end = 0 if step > 0 else lines - 1

                @pl.when((source == end) & on_line(line + step, lines))
                def _():
                    act(way, device_at(line + step, column, core))

    def cross(source, seen=None):
        shard = device_at(source, 1 - column, core)
        arrived(shard)
        through(source, lambda way, target: push(shard, way, target))
        push(shard, PARTNER, partner)
        if seen is not None:
            seen(shard)

    def finish():
        def visit(source, step):
            shard = device_at(source, column, core)
            far = device_at(source, 1 - column, core)
            sent(shard, PARTNER)
            sent(far, PARTNER)
            if step:
                crosses(source, lambda: sent(shard, ACROSS))
            else:
                sent(shard, ACROSS)
            through(source, lambda way, target: sent(far, way))
            for along, way in SIDES:
                if step in (0, -along):

                    @pl.when(on_line(line + along, lines))
                    def _():
                        sent(shard, way)

        for by in range(lines):
            on_distance(by, visit)

    return types.SimpleNamespace(
        start=start, relay=relay, cross=cross, arrived=arrived, finish=finish
    )


def reduce_stream(have, buffers, send, recv, settle):
    line, column, core, lines = place()
    side_buf, up_buf, down_buf, stash = buffers
    beside = device_at(line, 1 - column, core)

    def landed(buffer, way, slot):
        copy = remote(buffer, buffer, send.at[way, slot], recv.at[way, slot], {"dp": beside})
        copy.wait_recv()
        return buffer[...].astype(jnp.float32)

    def to_beside(target, step):
        chip = target * COLUMNS + 1 - column
        buffer = stash(chip)
        buffer[...] = have(chip).astype(buffer.dtype)
        remote(
            buffer,
            side_buf.at[target],
            send.at[1, target],
            recv.at[1, target],
            {"dp": beside},
        ).start()

    def along(target, step):
        chip = target * COLUMNS + column
        total = have(chip)
        total = total + landed(side_buf.at[target], 1, target)
        if step == 0:
            for by, way, landing in ((1, 2, up_buf), (-1, 3, down_buf)):
                settle_from(total, by, way, landing)
            return
        way, landing = (2, up_buf) if step > 0 else (3, down_buf)
        buffer = stash(chip)
        buffer[...] = total.astype(buffer.dtype)

        @pl.when(on_line(line - step, lines))
        def _():
            more = landed(landing.at[target], way, target)
            buffer[...] = (total + more).astype(buffer.dtype)

        remote(
            buffer,
            landing.at[target],
            send.at[way, target],
            recv.at[way, target],
            {"dp": device_at(line + step, column, core)},
        ).start()

    def settle_from(total, by, way, landing):
        if way == 2:
            settle(total, True)

        @pl.when(on_line(line - by, lines))
        def _():
            settle(landed(landing.at[line], way, line), False)

    def finish():
        def visit(target, step):
            buffer = side_buf.at[target]
            slots = [(1, target)]
            if step:
                slots.append((2 if step > 0 else 3, target))
            for way, slot in slots:
                remote(
                    buffer, buffer, send.at[way, slot], recv.at[way, slot], {"dp": beside}
                ).wait_send()

        for by in range(lines):
            on_distance(by, visit)

    return types.SimpleNamespace(to_beside=to_beside, along=along, finish=finish)


def load_kernel(
    w_ref, u_ref, x_ref, w_all, u_all, x_all,
    w_send, w_recv, part_send, cycle_send, u_send, u_recv, x_send, x_recv, local,
):
    line, column, core, lines = place()
    cycle = lax.axis_size("ctx")
    mine = lax.axis_index("ctx")
    me = device_at(line, column, core)
    partner = device_at(line, column, 1 - core)
    others = [(mine + by) % cycle for by in range(1, cycle)]
    greet()

    weights = gather_stream(
        w_ref.at[mine],
        lambda shard: w_all.at[mine, shard],
        lambda way, shard: w_send.at[way, shard],
        lambda shard: w_recv.at[mine, shard],
        False,
    )
    ups = gather_stream(
        u_ref,
        lambda shard: u_all.at[shard],
        lambda way, shard: u_send.at[way, shard],
        lambda shard: u_recv.at[shard],
        True,
    )

    def part(c, shard, send, target, source=None):
        landing = w_all.at[c, shard]
        source = landing if source is None else source
        return remote(source, landing, send, w_recv.at[c, shard], target)

    def to_cycle(shard):
        for c in others:
            part(mine, shard, cycle_send.at[c, shard], {"ctx": c}).start()

    def from_cycle(shard):
        for c in others:
            copy = part(c, shard, part_send.at[c, shard], {"dp": partner})
            copy.wait_recv()
            copy.start()

    def swap(c, source):
        return remote(x_ref, x_all.at[source], x_send.at[c], x_recv.at[source], {"ctx": c})

    copies = [
        pltpu.make_async_copy(w_ref.at[c], w_all.at[c, me], local.at[c]) for c in range(cycle)
    ]
    copies.append(pltpu.make_async_copy(u_ref, u_all.at[me], local.at[cycle]))
    copies.append(pltpu.make_async_copy(x_ref, x_all.at[mine], local.at[cycle + 1]))
    weights.start()
    for c in others:
        swap(c, mine).start()
    ups.start()
    for c in others:
        part(c, me, part_send.at[c, me], {"dp": partner}, w_ref.at[c]).start()
    for copy in copies:
        copy.start()

    for d in range(lines):
        if d + 1 < lines:
            weights.relay(d + 1, to_cycle)
            ups.relay(d + 1)
        on_distance(d, lambda source, step: weights.cross(source, to_cycle))
        on_distance(d, lambda source, step: ups.cross(source))
        if d > 0:
            on_distance(d, lambda source, step: from_cycle(device_at(source, column, core)))
            on_distance(d - 1, lambda source, step: from_cycle(device_at(source, 1 - column, core)))
    on_distance(
        lines - 1, lambda source, step: from_cycle(device_at(source, 1 - column, core))
    )
    for chip in range(lines * COLUMNS):
        shard = chip * CORES + 1 - core
        weights.arrived(shard)
        ups.arrived(shard)
        for c in others:
            part(c, shard, part_send.at[c, shard], {"dp": partner}).wait_recv()
    weights.finish()
    ups.finish()
    for c in others:
        swap(c, c).wait_recv()
        swap(c, mine).wait_send()
        part(c, me, part_send.at[c, me], {"dp": partner}).wait_send()
    for d in range(lines):
        for across in (column, 1 - column):
            if d == 0 and across is column:
                continue
            shard = device_at(nearest(d), across, core)
            for c in others:
                part(c, shard, part_send.at[c, shard], {"dp": partner}).wait_send()
                part(mine, shard, cycle_send.at[c, shard], {"ctx": c}).wait_send()
    for copy in copies:
        copy.wait()


def load(weights, ups, rows, collective_id):
    peers = lax.axis_size("dp")
    cycle = lax.axis_size("ctx")
    dma = pltpu.SemaphoreType.DMA
    return pl.pallas_call(
        load_kernel,
        out_shape=(
            jax.ShapeDtypeStruct((cycle, peers) + weights.shape[1:], weights.dtype),
            jax.ShapeDtypeStruct((peers,) + ups.shape, ups.dtype),
            jax.ShapeDtypeStruct((cycle,) + rows.shape, rows.dtype),
        ),
        in_specs=whole_vmem(3),
        out_specs=tuple([pl.BlockSpec(memory_space=pl.ANY)] * 3),
        scratch_shapes=[
            dma((4, peers)),
            dma((cycle, peers)),
            dma((cycle, peers)),
            dma((cycle, peers)),
            dma((4, peers)),
            dma((peers,)),
            dma((cycle,)),
            dma((cycle,)),
            dma((cycle + 2,)),
        ],
        compiler_params=pltpu.CompilerParams(collective_id=collective_id, has_side_effects=True),
    )(weights, ups, rows)


def spreader(width, shard, padded):
    source = lax.broadcasted_iota(jnp.int32, (width, 1), 0).astype(jnp.float32)
    block = jnp.floor((source + 0.5) * (1.0 / shard))
    target = source + block * float(padded - shard)
    lanes = lax.broadcasted_iota(jnp.int32, (1, width // shard * padded), 1).astype(jnp.float32)
    return jnp.where(target == lanes, 1.0, 0.0).astype(jnp.bfloat16)


def visible_bias(query_pos_ref, key_pos_ref):
    return jnp.where(query_pos_ref[...] >= key_pos_ref[...], 0.0, -1e30)


def parts_over(first, last, size, count):
    return [c for c in range(count) if c * size < last and (c + 1) * size > first]


def forward_kernel(
    query_pos_ref, key_pos_ref, x_ref, w_ref, vec_ref,
    spread_ref, normed_ref, q_ref, k_ref, v_ref, o_ref, o_spread_ref, h_ref, mid_ref,
    projected,
):
    cycle, rows, width = x_ref.shape
    shard = width // lax.axis_size("dp")
    mine = lax.axis_index("ctx")
    size = w_ref.shape[2]
    padded = w_ref.shape[1] // lax.axis_size("dp")
    spread_ref[...] = spreader(width, shard, padded)
    gain_one, shift_one, bias_q, bias_v, bias_o, gain_two, shift_two = [
        vec_ref[i : i + 1, :] for i in range(7)
    ]

    def project(left, first, last):
        for c in parts_over(first, last, size, cycle):
            projected[:, c * size : (c + 1) * size] = jnp.dot(
                left, w_ref[c], preferred_element_type=jnp.float32
            )

    def visit(c, carry):
        block = pl.ds(pl.multiple_of(c * rows, rows), rows)
        values, _, _ = norm_parts(x_ref[c].astype(jnp.float32), gain_one, shift_one)
        spread = jnp.dot(
            values.astype(jnp.bfloat16), spread_ref[...], preferred_element_type=jnp.float32
        ).astype(jnp.bfloat16)
        normed_ref[block, :] = spread
        project(spread, 0, 3 * width)
        k_ref[block, :] = projected[:, width : 2 * width].astype(jnp.bfloat16)
        v_ref[block, :] = (projected[:, 2 * width : 3 * width] + bias_v).astype(jnp.bfloat16)

        @pl.when(c == mine)
        def _():
            q_ref[...] = (projected[:, :width] + bias_q).astype(jnp.bfloat16)

        return carry

    lax.fori_loop(0, cycle, visit, 0)
    bias = visible_bias(query_pos_ref, key_pos_ref)
    for start, lanes in head_groups(width):
        block = slice(start, start + lanes)
        q, k, v = q_ref[:, block], k_ref[:, block], v_ref[:, block]
        total = None
        for mask in head_masks(lanes):
            scores = contract_last(keep(q, mask), k) * SCALE + bias
            largest = jnp.max(scores, axis=-1, keepdims=True)
            exponent = jnp.exp(scores - largest)
            inverse = 1.0 / jnp.sum(exponent, axis=-1, keepdims=True)
            part = jnp.dot(
                exponent.astype(jnp.bfloat16), keep(v, mask), preferred_element_type=jnp.float32
            )
            part = part * inverse
            total = part if total is None else total + part
        o_ref[:, block] = total.astype(jnp.bfloat16)
    o_spread = jnp.dot(
        o_ref[...], spread_ref[...], preferred_element_type=jnp.float32
    ).astype(jnp.bfloat16)
    o_spread_ref[...] = o_spread
    project(o_spread, 3 * width, 4 * width)
    hidden = x_ref[mine].astype(jnp.float32) + projected[:, 3 * width : 4 * width] + bias_o
    h_ref[...] = hidden
    mid_ref[...] = norm_parts(hidden, gain_two, shift_two)[0].astype(jnp.bfloat16)


def forward(query_pos, key_pos, x, w, vectors):
    cycle, rows, width = x.shape
    full = w.shape[1]

    def bf(*shape):
        return jax.ShapeDtypeStruct(shape, jnp.bfloat16)

    return pl.pallas_call(
        forward_kernel,
        out_shape=(
            bf(width, full),
            bf(cycle * rows, full),
            bf(rows, width),
            bf(cycle * rows, width),
            bf(cycle * rows, width),
            bf(rows, width),
            bf(rows, full),
            jax.ShapeDtypeStruct((rows, width), jnp.float32),
            bf(rows, width),
        ),
        in_specs=whole_vmem(5),
        out_specs=tuple(whole_vmem(9)),
        scratch_shapes=[pltpu.VMEM((rows, 4 * width), jnp.float32)],
        compiler_params=pltpu.CompilerParams(vmem_limit_bytes=VMEM_LIMIT),
    )(query_pos, key_pos, x, w, vectors)


def weigh_slabs(slab_ref, normed_ref, wide, o_spread_ref, head_wide):
    cycle, peers, padded, _ = slab_ref.shape
    width = wide.shape[1] // 4
    tall, thin = 3 * width // cycle, width // cycle
    for c in range(cycle):
        grads = contract_first(normed_ref[...], wide[:, c * tall : (c + 1) * tall])
        for s in range(peers):
            slab_ref[c, s, :, :tall] = grads[s * padded : (s + 1) * padded].astype(jnp.bfloat16)
        start = 3 * width + c * thin
        grads = contract_first(o_spread_ref[...], head_wide[:, start : start + thin])
        for s in range(peers):
            slab_ref[c, s, :, tall:] = grads[s * padded : (s + 1) * padded].astype(jnp.bfloat16)


def weigh_kernel(normed_ref, wide_ref, o_spread_ref, head_wide_ref, slab_ref):
    weigh_slabs(slab_ref, normed_ref, wide_ref, o_spread_ref, head_wide_ref)


def backward_kernel(
    whole, query_pos_ref, key_pos_ref, x_ref, w_ref, vec_ref, spread_ref, normed_ref,
    q_ref, k_ref, v_ref, o_ref, o_spread_ref, h_ref, up_ref, gm_ref,
    sums_ref, da_ref, da_own_ref, dh_ref, *rest
):
    if whole:
        slab_ref, wide, head_wide, do_ref = rest
    else:
        wide, head_wide, do_ref = rest
    cycle, rows, width = x_ref.shape
    peers = lax.axis_size("dp")
    mine = lax.axis_index("ctx")
    size = w_ref.shape[2]
    padded = w_ref.shape[1] // peers
    gain_one, shift_one, _, _, _, gain_two, shift_two = [vec_ref[i : i + 1, :] for i in range(7)]

    def column_sum(values):
        return jnp.sum(values, axis=0, keepdims=True)

    _, normed, inverse = norm_parts(h_ref[...], gain_two, shift_two)
    upstream = up_ref[...].astype(jnp.float32)
    grad_mid = gm_ref[...]
    sums_ref[0:2, :] = jnp.zeros((2, width), jnp.float32)
    sums_ref[5:6, :] = column_sum(grad_mid * normed)
    sums_ref[6:7, :] = column_sum(grad_mid)
    sums_ref[7:8, :] = column_sum(upstream)
    grad_hidden = upstream + norm_back(grad_mid, normed, inverse, gain_two)
    dh_ref[...] = grad_hidden
    sums_ref[4:5, :] = column_sum(grad_hidden)
    grad_hidden_b = grad_hidden.astype(jnp.bfloat16)
    head_wide[...] = jnp.zeros_like(head_wide)
    head_wide[:, 3 * width : 4 * width] = grad_hidden_b
    grad_ctx = None
    for c in parts_over(3 * width, 4 * width, size, cycle):
        more = contract_last(head_wide[:, c * size : (c + 1) * size], w_ref[c])
        grad_ctx = more if grad_ctx is None else grad_ctx + more
    do_ref[...] = contract_last(grad_ctx.astype(jnp.bfloat16), spread_ref[...]).astype(
        jnp.bfloat16
    )

    wide[...] = jnp.zeros_like(wide)
    own = pl.ds(pl.multiple_of(mine * rows, rows), rows)
    bias = visible_bias(query_pos_ref, key_pos_ref)
    for start, lanes in head_groups(width):
        block = slice(start, start + lanes)
        q, k, v = q_ref[:, block], k_ref[:, block], v_ref[:, block]
        do, o = do_ref[:, block], o_ref[:, block]
        product = do.astype(jnp.float32) * o.astype(jnp.float32)
        dq = dk = dv = None
        for mask in head_masks(lanes):
            q_h, k_h, do_h = keep(q, mask), keep(k, mask), keep(do, mask)
            product_h = product if mask is None else product * mask.astype(jnp.float32)
            delta = jnp.sum(product_h, axis=-1, keepdims=True)
            scores = contract_last(q_h, k) * SCALE + bias
            largest = jnp.max(scores, axis=-1, keepdims=True)
            exponent = jnp.exp(scores - largest)
            p = exponent * (1.0 / jnp.sum(exponent, axis=-1, keepdims=True))
            dp = contract_last(do_h, v)
            ds = (p * (dp - delta)).astype(jnp.bfloat16)
            dv_h = contract_first(p.astype(jnp.bfloat16), do_h)
            dq_h = jnp.dot(ds, k_h, preferred_element_type=jnp.float32)
            dk_h = contract_first(ds, q_h)
            dq = dq_h if dq is None else dq + dq_h
            dk = dk_h if dk is None else dk + dk_h
            dv = dv_h if dv is None else dv + dv_h
        dq = dq * SCALE
        wide[own, start : start + lanes] = dq.astype(jnp.bfloat16)
        wide[:, width + start : width + start + lanes] = (dk * SCALE).astype(jnp.bfloat16)
        wide[:, 2 * width + start : 2 * width + start + lanes] = dv.astype(jnp.bfloat16)
        sums_ref[2:3, block] = column_sum(dq)
        sums_ref[3:4, block] = column_sum(dv)

    if whole:
        weigh_slabs(slab_ref, normed_ref, wide, o_spread_ref, head_wide)

    def visit(block, carry):
        span = pl.ds(pl.multiple_of(block * rows, rows), rows)
        total = None
        for c in parts_over(0, 3 * width, size, cycle):
            more = contract_last(wide[span, c * size : (c + 1) * size], w_ref[c])
            total = more if total is None else total + more
        high = total.astype(jnp.bfloat16)
        low = (total - high.astype(jnp.float32)).astype(jnp.bfloat16)
        grad = contract_last(high, spread_ref[...]) + contract_last(low, spread_ref[...])
        _, normed, _ = norm_parts(x_ref[block].astype(jnp.float32), gain_one, shift_one)
        sums_ref[0:1, :] += column_sum(grad * normed)
        sums_ref[1:2, :] += column_sum(grad)
        da_ref[block] = grad.astype(jnp.bfloat16)

        @pl.when(block == mine)
        def _():
            da_own_ref[...] = grad

        return carry

    lax.fori_loop(0, cycle, visit, 0)


def backward(*arrays):
    x, w = arrays[2], arrays[3]
    cycle, rows, width = x.shape
    peers = lax.axis_size("dp")
    size = w.shape[2]
    slabs = jax.ShapeDtypeStruct((cycle, peers, w.shape[1] // peers, size), jnp.bfloat16)
    kept = [((cycle * rows, 4 * width), jnp.bfloat16), ((rows, 4 * width), jnp.bfloat16)]
    whole = slabs.size + w.size + kept[0][0][0] * kept[0][0][1] < FUSED_LIMIT
    params = pltpu.CompilerParams(vmem_limit_bytes=VMEM_LIMIT)
    outs = [
        jax.ShapeDtypeStruct((8, width), jnp.float32),
        jax.ShapeDtypeStruct((cycle, rows, width), jnp.bfloat16),
        jax.ShapeDtypeStruct((rows, width), jnp.float32),
        jax.ShapeDtypeStruct((rows, width), jnp.float32),
    ]
    scratch = [pltpu.VMEM((rows, width), jnp.bfloat16)]
    if whole:
        outs += [slabs]
        scratch = [pltpu.VMEM(*entry) for entry in kept] + scratch
    else:
        outs += [jax.ShapeDtypeStruct(*entry) for entry in kept]
    sums, da, da_own, dh, *rest = pl.pallas_call(
        functools.partial(backward_kernel, whole),
        out_shape=tuple(outs),
        in_specs=whole_vmem(len(arrays)),
        out_specs=tuple(whole_vmem(len(outs))),
        scratch_shapes=scratch,
        compiler_params=params,
    )(*arrays)
    if not whole:
        normed, o_spread = arrays[6], arrays[11]
        rest = [
            pl.pallas_call(
                weigh_kernel,
                out_shape=slabs,
                in_specs=whole_vmem(4),
                out_specs=whole_vmem(1)[0],
                compiler_params=params,
            )(normed, rest[0], o_spread, rest[1])
        ]
    return rest[0], sums, da, da_own, dh


def whole_vmem(count):
    return [pl.BlockSpec(memory_space=pltpu.VMEM)] * count


def ffn_kernel(
    mid_ref, ups_ref, w_up_ref, w_up_t_ref, w_down_ref, w_down_t_ref, b_up_ref,
    gm_ref, br_ref, gup_ref, gdown_ref, gb_ref,
    mids, parts, acts, grads, up_total, down_total, give, take, bias_part, bias_all,
    core_buf, side_buf, up_buf, down_buf,
    g_send, g_recv, c_send, c_recv, r_send, r_recv, y_send, y_recv, b_send, b_recv,
):
    line, column, core, lines = place()
    rows, width = mid_ref.shape
    cycle = lax.axis_size("ctx")
    mine = lax.axis_index("ctx")
    me = device_at(line, column, core)
    partner = device_at(line, column, 1 - core)
    greet()

    gather = gather_stream(
        mid_ref,
        lambda shard: mids.at[shard],
        lambda way, shard: g_send.at[way, shard],
        lambda shard: g_recv.at[shard],
        False,
    )
    gather.start()
    mids[me] = mid_ref[...]
    bias_part[...] = jnp.zeros_like(bias_part)

    def to_core(chip):
        return remote(
            parts.at[chip * CORES + 1 - core],
            core_buf.at[chip],
            c_send.at[chip],
            c_recv.at[chip],
            {"dp": partner},
        )

    def feed(chip):
        pair = pl.ds(chip * CORES, CORES)
        mid = mids[pair].reshape(CORES * rows, width)
        ups = ups_ref[pair].reshape(CORES * rows, width)
        pre = jnp.dot(mid, w_up_ref[...], preferred_element_type=jnp.float32) + b_up_ref[...]
        grad = jnp.dot(ups, w_down_t_ref[...], preferred_element_type=jnp.float32)
        half = 0.5 * (1.0 + lax.erf(pre * 0.7071067811865476))
        act = (pre * half).astype(jnp.bfloat16)
        grad = grad * (half + pre * jnp.exp(-0.5 * pre * pre) * 0.3989422804014327)
        bias_part[...] += jnp.sum(grad, axis=0, keepdims=True)
        grad = grad.astype(jnp.bfloat16)
        acts[chip] = act
        grads[chip] = grad
        part = jnp.dot(grad, w_up_t_ref[...], preferred_element_type=jnp.float32)
        parts[pair] = part.astype(jnp.bfloat16).reshape(CORES, rows, width)
        to_core(chip).start()
        branch = jnp.dot(act, w_down_ref[...], preferred_element_type=jnp.float32)
        br_ref[pair] = branch.astype(jnp.bfloat16).reshape(CORES, rows, width)

    def visit(d, carry):
        @pl.when(d + 1 < lines)
        def _():
            gather.relay(d + 1)

        at = nearest(d)
        gather.arrived(device_at(at, column, 1 - core))
        feed(at * COLUMNS + column)
        gather.cross(at)
        gather.arrived(device_at(at, 1 - column, 1 - core))
        feed(at * COLUMNS + 1 - column)
        return carry

    lax.fori_loop(0, lines, visit, 0)

    def have(chip):
        to_core(chip).wait_recv()
        return core_buf[chip].astype(jnp.float32) + parts[chip * CORES + core].astype(jnp.float32)

    def settle(total, first):
        gm_ref[...] = total if first else gm_ref[...] + total

    reduce = reduce_stream(
        have,
        (side_buf, up_buf, down_buf, lambda chip: parts.at[chip * CORES + core]),
        r_send,
        r_recv,
        settle,
    )
    for by in range(lines - 1, -1, -1):
        on_distance(by, reduce.to_beside)

    def swap(c, source):
        return remote(give.at[c], take.at[source], y_send.at[c], y_recv.at[source], {"ctx": c})

    def swap_bias(c, source):
        landing = bias_all.at[source]
        return remote(bias_part, landing, b_send.at[c], b_recv.at[source], {"ctx": c})

    bias_all[mine] = bias_part[...]
    others = [(mine + by) % cycle for by in range(1, cycle)]
    for c in others:
        swap_bias(c, mine).start()
    up_total[...] = jnp.zeros_like(up_total)
    down_total[...] = jnp.zeros_like(down_total)

    def weigh(chip, carry):
        pair = pl.ds(chip * CORES, CORES)
        up_total[...] += contract_first(grads[chip], mids[pair].reshape(CORES * rows, width))
        down_total[...] += contract_first(acts[chip], ups_ref[pair].reshape(CORES * rows, width))
        return carry

    lax.fori_loop(0, lines * COLUMNS, weigh, 0)
    size = width // cycle
    for c in range(cycle):
        up_part = up_total[:, c * size : (c + 1) * size]
        down_part = down_total[:, c * size : (c + 1) * size]

        @pl.when(c == mine)
        def _():
            gup_ref[...] = up_part
            gdown_ref[...] = down_part

        @pl.when(c != mine)
        def _():
            give[c, 0] = up_part.astype(give.dtype)
            give[c, 1] = down_part.astype(give.dtype)
            swap(c, mine).start()

    for by in range(lines - 1, -1, -1):
        on_distance(by, reduce.along)
    for c in others:
        swap(c, c).wait_recv()
        gup_ref[...] += take[c, 0].astype(jnp.float32)
        gdown_ref[...] += take[c, 1].astype(jnp.float32)
        swap_bias(c, c).wait_recv()
    total = bias_all[0]
    for c in range(1, cycle):
        total = total + bias_all[c]
    gb_ref[...] = total
    for c in others:
        swap(c, mine).wait_send()
        swap_bias(c, mine).wait_send()
    for chip in range(lines * COLUMNS):
        to_core(chip).wait_send()
    reduce.finish()
    gather.finish()


def feed_forward(mid, ups, w_up, w_down, b_up, collective_id):
    peers = lax.axis_size("dp")
    cycle = lax.axis_size("ctx")
    lines = peers // (CORES * COLUMNS)
    chips = lines * COLUMNS
    rows, width = mid.shape
    hidden = w_up.shape[1]
    dma = pltpu.SemaphoreType.DMA

    def slabs(count):
        return pltpu.VMEM((count, rows, width), jnp.bfloat16)

    return pl.pallas_call(
        ffn_kernel,
        out_shape=(
            jax.ShapeDtypeStruct((rows, width), jnp.float32),
            jax.ShapeDtypeStruct((peers, rows, width), jnp.bfloat16),
            jax.ShapeDtypeStruct((hidden, width // cycle), jnp.float32),
            jax.ShapeDtypeStruct((hidden, width // cycle), jnp.float32),
            jax.ShapeDtypeStruct((1, hidden), jnp.float32),
        ),
        in_specs=whole_vmem(7),
        out_specs=tuple(whole_vmem(5)),
        scratch_shapes=[
            slabs(peers),
            slabs(peers),
            pltpu.VMEM((chips, CORES * rows, hidden), jnp.bfloat16),
            pltpu.VMEM((chips, CORES * rows, hidden), jnp.bfloat16),
            pltpu.VMEM((hidden, width), jnp.float32),
            pltpu.VMEM((hidden, width), jnp.float32),
            pltpu.VMEM((cycle, 2, hidden, width // cycle), jnp.bfloat16),
            pltpu.VMEM((cycle, 2, hidden, width // cycle), jnp.bfloat16),
            pltpu.VMEM((1, hidden), jnp.float32),
            pltpu.VMEM((cycle, 1, hidden), jnp.float32),
            slabs(chips),
            slabs(lines),
            slabs(lines),
            slabs(lines),
            dma((4, peers)),
            dma((peers,)),
            dma((chips,)),
            dma((chips,)),
            dma((4, lines)),
            dma((4, lines)),
            dma((cycle,)),
            dma((cycle,)),
            dma((cycle,)),
            dma((cycle,)),
        ],
        compiler_params=pltpu.CompilerParams(
            collective_id=collective_id, has_side_effects=True, vmem_limit_bytes=VMEM_LIMIT
        ),
    )(mid, ups, w_up, w_up.T, w_down, w_down.T, b_up.astype(jnp.float32)[None, :])


def settle_kernel(
    slab_ref, br_ref, sums_ref, da_ref, da_own_ref, dh_ref, h_ref, x_ref, vec_ref,
    out_ref, ing_ref, gq_ref, go_ref, total_ref,
    slab_core, slab_cycle, slab_side, slab_up, slab_down,
    slab_sum,
    br_core, br_side, br_up, br_down,
    da_all, stage, sums_core, sums_cycle, sums_side, sums_line,
    sc_send, sc_recv, sy_send, sy_recv, sr_send, sr_recv, bc_send, bc_recv, br_send, br_recv,
    a_send, a_recv, one_send, one_recv, cyc_send, cyc_recv, lin_send, lin_recv,
):
    line, column, core, lines = place()
    rows, width = dh_ref.shape
    shard = gq_ref.shape[0]
    cycle = lax.axis_size("ctx")
    mine = lax.axis_index("ctx")
    beside = device_at(line, 1 - column, core)
    partner = device_at(line, column, 1 - core)
    others = [(mine + by) % cycle for by in range(1, cycle)]
    greet()

    def slab_to_core(c, chip):
        return remote(
            slab_ref.at[c, chip * CORES + 1 - core],
            slab_core.at[c, chip],
            sc_send.at[c, chip],
            sc_recv.at[c, chip],
            {"dp": partner},
        )

    def slab_to_cycle(c, chip, source):
        return remote(
            slab_core.at[c, chip],
            slab_cycle.at[source, chip],
            sy_send.at[c, chip],
            sy_recv.at[source, chip],
            {"ctx": c},
        )

    def br_to_core(chip):
        return remote(
            br_ref.at[chip * CORES + 1 - core],
            br_core.at[chip],
            bc_send.at[chip],
            bc_recv.at[chip],
            {"dp": partner},
        )

    def da_swap(c, source):
        return remote(da_ref.at[c], da_all.at[source], a_send.at[c], a_recv.at[source], {"ctx": c})

    def both(act):
        def visit(target, step):
            act(target * COLUMNS + 1 - column)
            act(target * COLUMNS + column)

        return visit

    def far_first(act):
        for by in range(lines - 1, -1, -1):
            on_distance(by, act)

    sums_to_core = remote(sums_ref, sums_core, one_send.at[0], one_recv.at[0], {"dp": partner})
    sums_to_side = remote(stage.at[1], sums_side, one_send.at[1], one_recv.at[1], {"dp": beside})

    def sums_to_cycle(c, source):
        landing = sums_cycle.at[source]
        return remote(stage.at[0], landing, cyc_send.at[c], cyc_recv.at[source], {"ctx": c})

    def sums_to_line(to, source):
        target = {"dp": device_at(to, column, core)}
        return remote(
            stage.at[2], sums_line.at[source], lin_send.at[to], lin_recv.at[source], target
        )

    sums_to_core.start()

    def send_parts(chip):
        for c in others:
            slab_to_core(c, chip).start()

    far_first(both(send_parts))
    far_first(both(lambda chip: br_to_core(chip).start()))
    far_first(both(lambda chip: slab_to_core(mine, chip).start()))

    def cycle_sums(chip):
        for c in others:
            slab_to_core(c, chip).wait_recv()
            total = slab_core[c, chip].astype(jnp.float32)
            total = total + slab_ref[c, chip * CORES + core].astype(jnp.float32)
            slab_core[c, chip] = total.astype(slab_core.dtype)
            slab_to_cycle(c, chip, mine).start()

    def br_have(chip):
        br_to_core(chip).wait_recv()
        return br_core[chip].astype(jnp.float32) + br_ref[chip * CORES + core].astype(jnp.float32)

    def br_settle(total, first):
        if first:
            ing_ref[...] = total
        else:
            ing_ref[...] += total

    def slab_have(chip):
        slab_to_core(mine, chip).wait_recv()
        total = slab_core[mine, chip].astype(jnp.float32)
        total = total + slab_ref[mine, chip * CORES + core].astype(jnp.float32)
        for c in others:
            slab_to_cycle(c, chip, c).wait_recv()
            total = total + slab_cycle[c, chip].astype(jnp.float32)
        return total

    def slab_settle(total, first):
        slab_sum[...] = total if first else slab_sum[...] + total

    branch = reduce_stream(
        br_have, (br_side, br_up, br_down, lambda chip: br_core.at[chip]), br_send, br_recv, br_settle
    )
    slabs = reduce_stream(
        slab_have,
        (slab_side, slab_up, slab_down, lambda chip: slab_core.at[mine, chip]),
        sr_send,
        sr_recv,
        slab_settle,
    )

    def first_hop(target, step):
        both(cycle_sums)(target, step)
        branch.to_beside(target, step)

    far_first(first_hop)
    for c in others:
        da_swap(c, mine).start()
    sums_to_core.wait_recv()
    stage[0] = sums_ref[...] + sums_core[...]
    sums_cycle[mine] = stage[0]
    for c in others:
        sums_to_cycle(c, mine).start()

    for by in range(lines - 1, -1, -1):
        on_distance(by, slabs.to_beside)
        on_distance(by, branch.along)
        if by + 1 < lines:
            on_distance(by + 1, slabs.along)
        if by == lines - 1:
            for c in others:
                sums_to_cycle(c, c).wait_recv()
            total = sums_cycle[0]
            for c in range(1, cycle):
                total = total + sums_cycle[c]
            stage[1] = total
            sums_to_side.start()
        if by == lines - 2:
            sums_to_side.wait_recv()
            stage[2] = stage[1] + sums_side[...]
            sums_line[line] = stage[2]
            for away in range(1, lines):
                sums_to_line((line + away) % lines, line).start()
    out_ref[...] = (h_ref[...] + ing_ref[...] + vec_ref[7:8, :]).astype(out_ref.dtype)
    grad = da_own_ref[...]
    for c in others:
        da_swap(c, c).wait_recv()
        grad = grad + da_all[c].astype(jnp.float32)
    gain, bias = vec_ref[0:1, :], vec_ref[1:2, :]
    _, normed, inverse = norm_parts(x_ref[mine].astype(jnp.float32), gain, bias)
    ing_ref[...] = dh_ref[...] + norm_back(grad, normed, inverse, gain)
    for away in range(1, lines):
        source = (line + away) % lines
        sums_to_line(source, source).wait_recv()
    total = sums_line[0]
    for by in range(1, lines):
        total = total + sums_line[by]
    total_ref[...] = total
    on_distance(0, slabs.along)
    tall = gq_ref.shape[1]
    gq_ref[...] = slab_sum[:shard, :tall]
    go_ref[...] = slab_sum[:shard, tall:]

    sums_to_core.wait_send()
    sums_to_side.wait_send()
    for c in others:
        sums_to_cycle(c, mine).wait_send()
        da_swap(c, mine).wait_send()
    for away in range(1, lines):
        sums_to_line((line + away) % lines, line).wait_send()
    branch.finish()
    slabs.finish()
    for chip in range(lines * COLUMNS):
        br_to_core(chip).wait_send()
        slab_to_core(mine, chip).wait_send()
        for c in others:
            slab_to_core(c, chip).wait_send()
            slab_to_cycle(c, chip, mine).wait_send()


def settle(slabs, branch, sums, da, da_own, dh, hidden, x, vectors, collective_id):
    cycle, peers, padded, size = slabs.shape
    rows, width = dh.shape
    lines = peers // (CORES * COLUMNS)
    chips = lines * COLUMNS
    shard = width // peers
    dma = pltpu.SemaphoreType.DMA
    f32, bf16 = jnp.float32, jnp.bfloat16

    def pieces(*lead):
        return pltpu.VMEM(lead + (padded, size), bf16)

    def blocks(*lead):
        return pltpu.VMEM(lead + (rows, width), bf16)

    def totals(*lead):
        return pltpu.VMEM(lead + sums.shape, f32)

    return pl.pallas_call(
        settle_kernel,
        out_shape=(
            jax.ShapeDtypeStruct((rows, width), bf16),
            jax.ShapeDtypeStruct((rows, width), f32),
            jax.ShapeDtypeStruct((shard, 3 * width // cycle), f32),
            jax.ShapeDtypeStruct((shard, width // cycle), f32),
            jax.ShapeDtypeStruct(sums.shape, f32),
        ),
        in_specs=whole_vmem(9),
        out_specs=tuple(whole_vmem(5)),
        scratch_shapes=[pieces(cycle, chips), pieces(cycle, chips)]
        + [pieces(lines)] * 3
        + [pltpu.VMEM((padded, size), f32)]
        + [blocks(chips)]
        + [blocks(lines)] * 3
        + [blocks(cycle), totals(3), totals(), totals(cycle), totals(), totals(lines)]
        + [dma((cycle, chips))] * 4
        + [dma((4, lines))] * 2
        + [dma((chips,))] * 2
        + [dma((4, lines))] * 2
        + [dma((cycle,))] * 2
        + [dma((2,))] * 2
        + [dma((cycle,))] * 2
        + [dma((lines,))] * 2,
        compiler_params=pltpu.CompilerParams(
            collective_id=collective_id, has_side_effects=True, vmem_limit_bytes=VMEM_LIMIT
        ),
    )(slabs, branch, sums, da, da_own, dh, hidden, x, vectors)


def per_device(
    block_in,
    cotangent,
    block_order,
    ln1_gain,
    ln1_bias,
    w_qkv,
    b_query,
    b_value,
    w_out,
    b_out,
    ln2_gain,
    ln2_bias,
    w_up,
    b_up,
    w_down,
    b_down,
):
    inputs = block_in[0]
    upstream = cotangent[0]
    row_count, width = inputs.shape
    peers = lax.axis_size("dp")
    cycle = lax.axis_size("ctx")
    mine = lax.axis_index("ctx")
    all_rows = row_count * cycle
    shard = width // peers
    padded = (shard // GROUP + 1) * GROUP

    vectors = [ln1_gain, ln1_bias, b_query, b_value, b_out, ln2_gain, ln2_bias, b_down]
    count = len(vectors)
    vectors = jnp.pad(jnp.concatenate(vectors), (0, 4 * width - count * shard))
    local = jnp.concatenate([w_qkv, w_out], axis=1)
    local = jnp.concatenate([local, vectors[None]], axis=0)
    local = jnp.pad(local, ((0, padded - shard - 1), (0, 0)))
    size = 4 * width // cycle
    local = jnp.stack([local[:, c * size : (c + 1) * size] for c in range(cycle)])
    weights, ups, rows = load(local, upstream, inputs, 0)
    vectors = weights[0, :, shard, : count * shard].reshape(peers, count, shard)
    vectors = jnp.transpose(vectors, (1, 0, 2)).reshape(count, width).astype(jnp.float32)
    weights = weights.reshape(cycle, peers * padded, size)

    slots = jnp.arange(all_rows, dtype=jnp.int32)
    block_rows = all_rows // block_order.shape[0]
    starts = jnp.repeat(block_order * block_rows, block_rows, total_repeat_length=all_rows)
    positions = starts + slots % block_rows
    key_pos = positions[None, :]
    query_pos = lax.dynamic_slice_in_dim(positions, mine * row_count, row_count)[:, None]

    spread, normed, q, k, v, o, o_spread, hidden, mid = forward(
        query_pos, key_pos, rows, weights, vectors
    )
    grad_mid, branch, g_up, g_down, g_bias_up = feed_forward(mid, ups, w_up, w_down, b_up, 1)
    slabs, sums, da, da_own, dh = backward(
        query_pos, key_pos, rows, weights, vectors, spread, normed,
        q, k, v, o, o_spread, hidden, upstream, grad_mid,
    )
    block_out, grad_input, g_qkv, g_out, sums = settle(
        slabs, branch, sums, da, da_own, dh, hidden, rows, vectors, 3
    )
    sums = lax.dynamic_slice_in_dim(sums, lax.axis_index("dp") * shard, shard, 1)
    return (
        block_out[None],
        grad_input[None],
        sums[0],
        sums[1],
        g_qkv,
        sums[2],
        sums[3],
        g_out,
        sums[4],
        sums[5],
        sums[6],
        g_up.T,
        g_bias_up[0],
        g_down,
        sums[7],
    )


def solution(mesh):
    in_specs = (
        P("dp", "ctx", None),
        P("dp", "ctx", None),
        P(),
        P("dp"),
        P("dp"),
        P("dp", None),
        P("dp"),
        P("dp"),
        P("dp", None),
        P("dp"),
        P("dp"),
        P("dp"),
        P(None, "dp"),
        P("dp"),
        P("dp", None),
        P("dp"),
    )
    out_specs = (
        P("dp", "ctx", None),
        P("dp", "ctx", None),
        P("dp"),
        P("dp"),
        P("dp", "ctx"),
        P("dp"),
        P("dp"),
        P("dp", "ctx"),
        P("dp"),
        P("dp"),
        P("dp"),
        P("ctx", "dp"),
        P("dp"),
        P("dp", "ctx"),
        P("dp"),
    )
    return jax.shard_map(
        per_device, mesh=mesh, in_specs=in_specs, out_specs=out_specs, check_vma=False
    )
```

```python
import functools
import types

import jax
import jax.numpy as jnp
from jax import lax
from jax.experimental import pallas as pl
from jax.experimental.pallas import tpu as pltpu
from jax.sharding import PartitionSpec as P

HD = 64
SCALE = 0.125


def norm_parts(values, gain_values, shift_values):
    average = jnp.mean(values, axis=-1, keepdims=True)
    centered = values - average
    inverse = lax.rsqrt(jnp.mean(centered * centered, axis=-1, keepdims=True) + 1e-05)
    normed = centered * inverse
    return normed * gain_values + shift_values, normed, inverse


def norm_back(upstream, normed, inverse, gain_values):
    scaled = upstream * gain_values
    return inverse * (
        scaled
        - jnp.mean(scaled, axis=-1, keepdims=True)
        - normed * jnp.mean(scaled * normed, axis=-1, keepdims=True)
    )


def contract_first(left, right):
    return lax.dot_general(
        left, right, (((0,), (0,)), ((), ())), preferred_element_type=jnp.float32
    )


def contract_last(left, right):
    return lax.dot_general(
        left, right, (((1,), (1,)), ((), ())), preferred_element_type=jnp.float32
    )


def head_groups(width):
    groups = [(start, 128) for start in range(0, width - width % 128, 128)]
    if width % 128:
        groups.append((width - width % 128, width % 128))
    return groups


def head_masks(lanes):
    if lanes == HD:
        return [None]
    lane = lax.broadcasted_iota(jnp.int32, (1, lanes), 1)
    return [
        jnp.where((lane >= first) & (lane < first + HD), 1.0, 0.0).astype(jnp.bfloat16)
        for first in range(0, lanes, HD)
    ]


def keep(array, mask):
    return array if mask is None else array * mask


MESH = pl.DeviceIdType.MESH
CORES = 2
COLUMNS = 2
VMEM_LIMIT = 63 * 1024 * 1024
UP, DOWN, ACROSS, PARTNER = range(4)
SIDES = ((1, UP), (-1, DOWN))
GROUP = 8
FUSED_LIMIT = 14 * 1024 * 1024


def place():
    index = lax.axis_index("dp")
    lines = lax.axis_size("dp") // (CORES * COLUMNS)
    core = index % CORES
    column = (index // CORES) % COLUMNS
    return index // (CORES * COLUMNS), column, core, lines


def device_at(line, column, core):
    return (line * COLUMNS + column) * CORES + core


def on_line(line, lines):
    return (line >= 0) & (line < lines)


def greet():
    line, column, core, lines = place()
    cycle = lax.axis_size("ctx")
    mine = lax.axis_index("ctx")
    barrier = pltpu.get_barrier_semaphore()
    peers = [{"dp": device_at((line + by) % lines, column, core)} for by in range(1, lines)]
    peers += [{"dp": device_at(line, 1 - column, core)}, {"dp": device_at(line, column, 1 - core)}]
    peers += [{"ctx": (mine + by) % cycle} for by in range(1, cycle)]
    for peer in peers:
        pl.semaphore_signal(barrier, inc=1, device_id=peer, device_id_type=MESH)
    pl.semaphore_wait(barrier, len(peers))


def remote(source, landing, send, recv, target):
    return pltpu.make_async_remote_copy(
        src_ref=source,
        dst_ref=landing,
        send_sem=send,
        recv_sem=recv,
        device_id=target,
        device_id_type=MESH,
    )


def on_distance(by, act):
    line, _, _, lines = place()
    if by == 0:
        act(line, 0)
        return
    for step in (1, -1):

        @pl.when(on_line(line + step * by, lines))
        def _():
            act(line + step * by, step)


def nearest(d):
    line, _, _, lines = place()
    toward = 1 - 2 * ((2 * line) // lines)
    return (line + toward * d + lines) % lines


def gather_stream(own, land, send, recv, balanced):
    line, column, core, lines = place()
    me = device_at(line, column, core)
    beside = device_at(line, 1 - column, core)
    partner = device_at(line, column, 1 - core)

    def push(shard, way, target, source=None):
        source = land(shard) if source is None else source
        remote(source, land(shard), send(way, shard), recv(shard), {"dp": target}).start()

    def arrived(shard):
        buffer = land(shard)
        remote(buffer, buffer, send(PARTNER, shard), recv(shard), {"dp": partner}).wait_recv()

    def sent(shard, way):
        buffer = land(shard)
        remote(buffer, buffer, send(way, shard), recv(shard), {"dp": partner}).wait_send()

    def start():
        push(me, ACROSS, beside, own)
        for step, way in SIDES:

            @pl.when(on_line(line + step, lines))
            def _():
                push(me, way, device_at(line + step, column, core), own)

        push(me, PARTNER, partner, own)

    def crosses(source, act):
        if balanced:

            @pl.when((source != 0) & (source != lines - 1))
            def _():
                act()

        else:
            act()

    def relay(by, seen=None):
        for step, way in SIDES:

            @pl.when(on_line(line - step * by, lines))
            def _():
                shard = device_at(line - step * by, column, core)
                arrived(shard)

                @pl.when(on_line(line + step, lines))
                def _():
                    push(shard, way, device_at(line + step, column, core))

                crosses(line - step * by, lambda: push(shard, ACROSS, beside))
                push(shard, PARTNER, partner)
                if seen is not None:
                    seen(shard)

    def through(source, act):
        if balanced:
            for step, way in SIDES:
                end = 0 if step > 0 else lines - 1

                @pl.when((source == end) & on_line(line + step, lines))
                def _():
                    act(way, device_at(line + step, column, core))

    def cross(source, seen=None):
        shard = device_at(source, 1 - column, core)
        arrived(shard)
        through(source, lambda way, target: push(shard, way, target))
        push(shard, PARTNER, partner)
        if seen is not None:
            seen(shard)

    def finish():
        def visit(source, step):
            shard = device_at(source, column, core)
            far = device_at(source, 1 - column, core)
            sent(shard, PARTNER)
            sent(far, PARTNER)
            if step:
                crosses(source, lambda: sent(shard, ACROSS))
            else:
                sent(shard, ACROSS)
            through(source, lambda way, target: sent(far, way))
            for along, way in SIDES:
                if step in (0, -along):

                    @pl.when(on_line(line + along, lines))
                    def _():
                        sent(shard, way)

        for by in range(lines):
            on_distance(by, visit)

    return types.SimpleNamespace(
        start=start, relay=relay, cross=cross, arrived=arrived, finish=finish
    )


def reduce_stream(have, buffers, send, recv, settle):
    line, column, core, lines = place()
    side_buf, up_buf, down_buf, stash = buffers
    beside = device_at(line, 1 - column, core)

    def landed(buffer, way, slot):
        copy = remote(buffer, buffer, send.at[way, slot], recv.at[way, slot], {"dp": beside})
        copy.wait_recv()
        return buffer[...].astype(jnp.float32)

    def to_beside(target, step):
        chip = target * COLUMNS + 1 - column
        buffer = stash(chip)
        buffer[...] = have(chip).astype(buffer.dtype)
        remote(
            buffer,
            side_buf.at[target],
            send.at[1, target],
            recv.at[1, target],
            {"dp": beside},
        ).start()

    def along(target, step):
        chip = target * COLUMNS + column
        total = have(chip)
        total = total + landed(side_buf.at[target], 1, target)
        if step == 0:
            for by, way, landing in ((1, 2, up_buf), (-1, 3, down_buf)):
                settle_from(total, by, way, landing)
            return
        way, landing = (2, up_buf) if step > 0 else (3, down_buf)
        buffer = stash(chip)
        buffer[...] = total.astype(buffer.dtype)

        @pl.when(on_line(line - step, lines))
        def _():
            more = landed(landing.at[target], way, target)
            buffer[...] = (total + more).astype(buffer.dtype)

        remote(
            buffer,
            landing.at[target],
            send.at[way, target],
            recv.at[way, target],
            {"dp": device_at(line + step, column, core)},
        ).start()

    def settle_from(total, by, way, landing):
        if way == 2:
            settle(total, True)

        @pl.when(on_line(line - by, lines))
        def _():
            settle(landed(landing.at[line], way, line), False)

    def finish():
        def visit(target, step):
            buffer = side_buf.at[target]
            slots = [(1, target)]
            if step:
                slots.append((2 if step > 0 else 3, target))
            for way, slot in slots:
                remote(
                    buffer, buffer, send.at[way, slot], recv.at[way, slot], {"dp": beside}
                ).wait_send()

        for by in range(lines):
            on_distance(by, visit)

    return types.SimpleNamespace(to_beside=to_beside, along=along, finish=finish)


def pack_weights(vec_ref, qkv_ref, out_ref, w_ref, row):
    count, shard = vec_ref.shape
    cycle, padded, size = w_ref.shape
    width = out_ref.shape[1]
    for c in range(cycle):
        first, last = c * size, (c + 1) * size
        split = min(max(3 * width - first, 0), size)
        if split:
            w_ref[c, :shard, :split] = qkv_ref[:, first : first + split]
        if split < size:
            w_ref[c, :shard, split:] = out_ref[:, first + split - 3 * width : last - 3 * width]
    row[...] = jnp.zeros_like(row)
    for i in range(count):
        row[0:1, i * shard : (i + 1) * shard] = vec_ref[i : i + 1, :].astype(jnp.float32)
    for c in range(cycle):
        w_ref[c, shard:padded, :] = row[: padded - shard, :].astype(jnp.bfloat16)


def load_kernel(
    vec_ref, qkv_ref, out_ref, u_t_ref, x_t_ref, w_all, u_all, x_all, w_ref, row, u_ref, x_ref,
    w_send, w_recv, part_send, cycle_send, u_send, u_recv, x_send, x_recv, local,
):
    line, column, core, lines = place()
    cycle = lax.axis_size("ctx")
    mine = lax.axis_index("ctx")
    me = device_at(line, column, core)
    partner = device_at(line, column, 1 - core)
    others = [(mine + by) % cycle for by in range(1, cycle)]
    pack_weights(vec_ref, qkv_ref, out_ref, w_ref, row)
    x_ref[...] = x_t_ref[...].T
    u_ref[...] = u_t_ref[...].T
    greet()

    weights = gather_stream(
        w_ref.at[mine],
        lambda shard: w_all.at[mine, shard],
        lambda way, shard: w_send.at[way, shard],
        lambda shard: w_recv.at[mine, shard],
        False,
    )
    ups = gather_stream(
        u_ref,
        lambda shard: u_all.at[shard],
        lambda way, shard: u_send.at[way, shard],
        lambda shard: u_recv.at[shard],
        True,
    )

    def part(c, shard, send, target, source=None):
        landing = w_all.at[c, shard]
        source = landing if source is None else source
        return remote(source, landing, send, w_recv.at[c, shard], target)

    def to_cycle(shard):
        for c in others:
            part(mine, shard, cycle_send.at[c, shard], {"ctx": c}).start()

    def from_cycle(shard):
        for c in others:
            copy = part(c, shard, part_send.at[c, shard], {"dp": partner})
            copy.wait_recv()
            copy.start()

    def swap(c, source):
        return remote(x_ref, x_all.at[source], x_send.at[c], x_recv.at[source], {"ctx": c})

    copies = [
        pltpu.make_async_copy(w_ref.at[c], w_all.at[c, me], local.at[c]) for c in range(cycle)
    ]
    copies.append(pltpu.make_async_copy(u_ref, u_all.at[me], local.at[cycle]))
    copies.append(pltpu.make_async_copy(x_ref, x_all.at[mine], local.at[cycle + 1]))
    weights.start()
    for c in others:
        swap(c, mine).start()
    ups.start()
    for c in others:
        part(c, me, part_send.at[c, me], {"dp": partner}, w_ref.at[c]).start()
    for copy in copies:
        copy.start()

    for d in range(lines):
        if d + 1 < lines:
            weights.relay(d + 1, to_cycle)
            ups.relay(d + 1)
        on_distance(d, lambda source, step: weights.cross(source, to_cycle))
        on_distance(d, lambda source, step: ups.cross(source))
        if d > 0:
            on_distance(d, lambda source, step: from_cycle(device_at(source, column, core)))
            on_distance(d - 1, lambda source, step: from_cycle(device_at(source, 1 - column, core)))
    on_distance(
        lines - 1, lambda source, step: from_cycle(device_at(source, 1 - column, core))
    )
    for chip in range(lines * COLUMNS):
        shard = chip * CORES + 1 - core
        weights.arrived(shard)
        ups.arrived(shard)
        for c in others:
            part(c, shard, part_send.at[c, shard], {"dp": partner}).wait_recv()
    weights.finish()
    ups.finish()
    for c in others:
        swap(c, c).wait_recv()
        swap(c, mine).wait_send()
        part(c, me, part_send.at[c, me], {"dp": partner}).wait_send()
    for d in range(lines):
        for across in (column, 1 - column):
            if d == 0 and across is column:
                continue
            shard = device_at(nearest(d), across, core)
            for c in others:
                part(c, shard, part_send.at[c, shard], {"dp": partner}).wait_send()
                part(mine, shard, cycle_send.at[c, shard], {"ctx": c}).wait_send()
    for copy in copies:
        copy.wait()


def load(vectors, w_qkv, w_out, ups_t, rows_t, collective_id):
    peers = lax.axis_size("dp")
    cycle = lax.axis_size("ctx")
    shard = w_out.shape[0]
    padded = (shard // GROUP + 1) * GROUP
    size = 4 * w_out.shape[1] // cycle
    block = ups_t.shape[::-1]
    bf16 = jnp.bfloat16
    dma = pltpu.SemaphoreType.DMA
    return pl.pallas_call(
        load_kernel,
        out_shape=(
            jax.ShapeDtypeStruct((cycle, peers, padded, size), bf16),
            jax.ShapeDtypeStruct((peers,) + block, bf16),
            jax.ShapeDtypeStruct((cycle,) + block, bf16),
        ),
        in_specs=whole_vmem(5),
        out_specs=tuple([pl.BlockSpec(memory_space=pl.ANY)] * 3),
        scratch_shapes=[
            pltpu.VMEM((cycle, padded, size), bf16),
            pltpu.VMEM((GROUP, size), jnp.float32),
            pltpu.VMEM(block, bf16),
            pltpu.VMEM(block, bf16),
            dma((4, peers)),
            dma((cycle, peers)),
            dma((cycle, peers)),
            dma((cycle, peers)),
            dma((4, peers)),
            dma((peers,)),
            dma((cycle,)),
            dma((cycle,)),
            dma((cycle + 2,)),
        ],
        compiler_params=pltpu.CompilerParams(collective_id=collective_id, has_side_effects=True),
    )(vectors, w_qkv, w_out, ups_t, rows_t)


def spreader(width, shard, padded):
    source = lax.broadcasted_iota(jnp.int32, (width, 1), 0).astype(jnp.float32)
    block = jnp.floor((source + 0.5) * (1.0 / shard))
    target = source + block * float(padded - shard)
    lanes = lax.broadcasted_iota(jnp.int32, (1, width // shard * padded), 1).astype(jnp.float32)
    return jnp.where(target == lanes, 1.0, 0.0).astype(jnp.bfloat16)


def visible_bias(order_ref, first, rows, keys):
    block = keys // order_ref.shape[0]

    def position(slot):
        where = slot
        for b in range(order_ref.shape[0]):
            inside = (slot >= b * block) & (slot < (b + 1) * block)
            where = jnp.where(inside, (order_ref[b] - b) * block + slot, where)
        return where

    query = position(first + lax.broadcasted_iota(jnp.int32, (rows, 1), 0))
    key = position(lax.broadcasted_iota(jnp.int32, (1, keys), 1))
    return jnp.where(query >= key, 0.0, -1e30)


def parts_over(first, last, size, count):
    return [c for c in range(count) if c * size < last and (c + 1) * size > first]


def forward_kernel(
    order_ref, x_ref, w_ref, vec_ref,
    spread_ref, normed_ref, q_ref, k_ref, v_ref, o_ref, o_spread_ref, h_ref, mid_ref,
    projected,
):
    cycle, rows, width = x_ref.shape
    shard = width // lax.axis_size("dp")
    mine = lax.axis_index("ctx")
    size = w_ref.shape[2]
    padded = w_ref.shape[1] // lax.axis_size("dp")
    spread_ref[...] = spreader(width, shard, padded)
    gain_one, shift_one, bias_q, bias_v, bias_o, gain_two, shift_two = [
        vec_ref[i : i + 1, :] for i in range(7)
    ]

    def project(left, first, last):
        for c in parts_over(first, last, size, cycle):
            projected[:, c * size : (c + 1) * size] = jnp.dot(
                left, w_ref[c], preferred_element_type=jnp.float32
            )

    def visit(c, carry):
        block = pl.ds(pl.multiple_of(c * rows, rows), rows)
        values, _, _ = norm_parts(x_ref[c].astype(jnp.float32), gain_one, shift_one)
        spread = jnp.dot(
            values.astype(jnp.bfloat16), spread_ref[...], preferred_element_type=jnp.float32
        ).astype(jnp.bfloat16)
        normed_ref[block, :] = spread
        project(spread, 0, 3 * width)
        k_ref[block, :] = projected[:, width : 2 * width].astype(jnp.bfloat16)
        v_ref[block, :] = (projected[:, 2 * width : 3 * width] + bias_v).astype(jnp.bfloat16)

        @pl.when(c == mine)
        def _():
            q_ref[...] = (projected[:, :width] + bias_q).astype(jnp.bfloat16)

        return carry

    lax.fori_loop(0, cycle, visit, 0)
    bias = visible_bias(order_ref, mine * rows, rows, cycle * rows)
    for start, lanes in head_groups(width):
        block = slice(start, start + lanes)
        q, k, v = q_ref[:, block], k_ref[:, block], v_ref[:, block]
        total = None
        for mask in head_masks(lanes):
            scores = contract_last(keep(q, mask), k) * SCALE + bias
            largest = jnp.max(scores, axis=-1, keepdims=True)
            exponent = jnp.exp(scores - largest)
            inverse = 1.0 / jnp.sum(exponent, axis=-1, keepdims=True)
            part = jnp.dot(
                exponent.astype(jnp.bfloat16), keep(v, mask), preferred_element_type=jnp.float32
            )
            part = part * inverse
            total = part if total is None else total + part
        o_ref[:, block] = total.astype(jnp.bfloat16)
    o_spread = jnp.dot(
        o_ref[...], spread_ref[...], preferred_element_type=jnp.float32
    ).astype(jnp.bfloat16)
    o_spread_ref[...] = o_spread
    project(o_spread, 3 * width, 4 * width)
    hidden = x_ref[mine].astype(jnp.float32) + projected[:, 3 * width : 4 * width] + bias_o
    h_ref[...] = hidden
    mid_ref[...] = norm_parts(hidden, gain_two, shift_two)[0].astype(jnp.bfloat16)


def ordered(count):
    return [pl.BlockSpec(memory_space=pltpu.SMEM)] + whole_vmem(count - 1)


def forward(order, x, w, vectors):
    cycle, rows, width = x.shape
    full = w.shape[1]

    def bf(*shape):
        return jax.ShapeDtypeStruct(shape, jnp.bfloat16)

    return pl.pallas_call(
        forward_kernel,
        out_shape=(
            bf(width, full),
            bf(cycle * rows, full),
            bf(rows, width),
            bf(cycle * rows, width),
            bf(cycle * rows, width),
            bf(rows, width),
            bf(rows, full),
            jax.ShapeDtypeStruct((rows, width), jnp.float32),
            bf(rows, width),
        ),
        in_specs=ordered(4),
        out_specs=tuple(whole_vmem(9)),
        scratch_shapes=[pltpu.VMEM((rows, 4 * width), jnp.float32)],
        compiler_params=pltpu.CompilerParams(vmem_limit_bytes=VMEM_LIMIT),
    )(order, x, w, vectors)


def weigh_slabs(slab_ref, normed_ref, wide, o_spread_ref, head_wide):
    cycle, peers, padded, _ = slab_ref.shape
    width = wide.shape[1] // 4
    tall, thin = 3 * width // cycle, width // cycle
    for c in range(cycle):
        grads = contract_first(normed_ref[...], wide[:, c * tall : (c + 1) * tall])
        for s in range(peers):
            slab_ref[c, s, :, :tall] = grads[s * padded : (s + 1) * padded].astype(jnp.bfloat16)
        start = 3 * width + c * thin
        grads = contract_first(o_spread_ref[...], head_wide[:, start : start + thin])
        for s in range(peers):
            slab_ref[c, s, :, tall:] = grads[s * padded : (s + 1) * padded].astype(jnp.bfloat16)


def weigh_kernel(normed_ref, wide_ref, o_spread_ref, head_wide_ref, slab_ref):
    weigh_slabs(slab_ref, normed_ref, wide_ref, o_spread_ref, head_wide_ref)


def backward_kernel(
    whole, order_ref, x_ref, w_ref, vec_ref, spread_ref, normed_ref,
    q_ref, k_ref, v_ref, o_ref, o_spread_ref, h_ref, up_t_ref, gm_ref,
    sums_ref, da_ref, da_own_ref, dh_ref, *rest
):
    if whole:
        slab_ref, wide, head_wide, do_ref = rest
    else:
        wide, head_wide, do_ref = rest
    cycle, rows, width = x_ref.shape
    peers = lax.axis_size("dp")
    mine = lax.axis_index("ctx")
    size = w_ref.shape[2]
    padded = w_ref.shape[1] // peers
    gain_one, shift_one, _, _, _, gain_two, shift_two = [vec_ref[i : i + 1, :] for i in range(7)]

    def column_sum(values):
        return jnp.sum(values, axis=0, keepdims=True)

    _, normed, inverse = norm_parts(h_ref[...], gain_two, shift_two)
    upstream = up_t_ref[...].T.astype(jnp.float32)
    grad_mid = gm_ref[...]
    sums_ref[0:2, :] = jnp.zeros((2, width), jnp.float32)
    sums_ref[5:6, :] = column_sum(grad_mid * normed)
    sums_ref[6:7, :] = column_sum(grad_mid)
    sums_ref[7:8, :] = column_sum(upstream)
    grad_hidden = upstream + norm_back(grad_mid, normed, inverse, gain_two)
    dh_ref[...] = grad_hidden
    sums_ref[4:5, :] = column_sum(grad_hidden)
    grad_hidden_b = grad_hidden.astype(jnp.bfloat16)
    head_wide[...] = jnp.zeros_like(head_wide)
    head_wide[:, 3 * width : 4 * width] = grad_hidden_b
    grad_ctx = None
    for c in parts_over(3 * width, 4 * width, size, cycle):
        more = contract_last(head_wide[:, c * size : (c + 1) * size], w_ref[c])
        grad_ctx = more if grad_ctx is None else grad_ctx + more
    do_ref[...] = contract_last(grad_ctx.astype(jnp.bfloat16), spread_ref[...]).astype(
        jnp.bfloat16
    )

    wide[...] = jnp.zeros_like(wide)
    own = pl.ds(pl.multiple_of(mine * rows, rows), rows)
    bias = visible_bias(order_ref, mine * rows, rows, cycle * rows)
    for start, lanes in head_groups(width):
        block = slice(start, start + lanes)
        q, k, v = q_ref[:, block], k_ref[:, block], v_ref[:, block]
        do, o = do_ref[:, block], o_ref[:, block]
        product = do.astype(jnp.float32) * o.astype(jnp.float32)
        dq = dk = dv = None
        for mask in head_masks(lanes):
            q_h, k_h, do_h = keep(q, mask), keep(k, mask), keep(do, mask)
            product_h = product if mask is None else product * mask.astype(jnp.float32)
            delta = jnp.sum(product_h, axis=-1, keepdims=True)
            scores = contract_last(q_h, k) * SCALE + bias
            largest = jnp.max(scores, axis=-1, keepdims=True)
            exponent = jnp.exp(scores - largest)
            p = exponent * (1.0 / jnp.sum(exponent, axis=-1, keepdims=True))
            dp = contract_last(do_h, v)
            ds = (p * (dp - delta)).astype(jnp.bfloat16)
            dv_h = contract_first(p.astype(jnp.bfloat16), do_h)
            dq_h = jnp.dot(ds, k_h, preferred_element_type=jnp.float32)
            dk_h = contract_first(ds, q_h)
            dq = dq_h if dq is None else dq + dq_h
            dk = dk_h if dk is None else dk + dk_h
            dv = dv_h if dv is None else dv + dv_h
        dq = dq * SCALE
        wide[own, start : start + lanes] = dq.astype(jnp.bfloat16)
        wide[:, width + start : width + start + lanes] = (dk * SCALE).astype(jnp.bfloat16)
        wide[:, 2 * width + start : 2 * width + start + lanes] = dv.astype(jnp.bfloat16)
        sums_ref[2:3, block] = column_sum(dq)
        sums_ref[3:4, block] = column_sum(dv)

    if whole:
        weigh_slabs(slab_ref, normed_ref, wide, o_spread_ref, head_wide)

    def visit(block, carry):
        span = pl.ds(pl.multiple_of(block * rows, rows), rows)
        total = None
        for c in parts_over(0, 3 * width, size, cycle):
            more = contract_last(wide[span, c * size : (c + 1) * size], w_ref[c])
            total = more if total is None else total + more
        high = total.astype(jnp.bfloat16)
        low = (total - high.astype(jnp.float32)).astype(jnp.bfloat16)
        grad = contract_last(high, spread_ref[...]) + contract_last(low, spread_ref[...])
        _, normed, _ = norm_parts(x_ref[block].astype(jnp.float32), gain_one, shift_one)
        sums_ref[0:1, :] += column_sum(grad * normed)
        sums_ref[1:2, :] += column_sum(grad)
        da_ref[block] = grad.astype(jnp.bfloat16)

        @pl.when(block == mine)
        def _():
            da_own_ref[...] = grad

        return carry

    lax.fori_loop(0, cycle, visit, 0)


def backward(*arrays):
    x, w = arrays[1], arrays[2]
    cycle, rows, width = x.shape
    peers = lax.axis_size("dp")
    size = w.shape[2]
    slabs = jax.ShapeDtypeStruct((cycle, peers, w.shape[1] // peers, size), jnp.bfloat16)
    kept = [((cycle * rows, 4 * width), jnp.bfloat16), ((rows, 4 * width), jnp.bfloat16)]
    whole = slabs.size + w.size + kept[0][0][0] * kept[0][0][1] < FUSED_LIMIT
    params = pltpu.CompilerParams(vmem_limit_bytes=VMEM_LIMIT)
    outs = [
        jax.ShapeDtypeStruct((8, width), jnp.float32),
        jax.ShapeDtypeStruct((cycle, rows, width), jnp.bfloat16),
        jax.ShapeDtypeStruct((rows, width), jnp.float32),
        jax.ShapeDtypeStruct((rows, width), jnp.float32),
    ]
    scratch = [pltpu.VMEM((rows, width), jnp.bfloat16)]
    if whole:
        outs += [slabs]
        scratch = [pltpu.VMEM(*entry) for entry in kept] + scratch
    else:
        outs += [jax.ShapeDtypeStruct(*entry) for entry in kept]
    sums, da, da_own, dh, *rest = pl.pallas_call(
        functools.partial(backward_kernel, whole),
        out_shape=tuple(outs),
        in_specs=ordered(len(arrays)),
        out_specs=tuple(whole_vmem(len(outs))),
        scratch_shapes=scratch,
        compiler_params=params,
    )(*arrays)
    if not whole:
        normed, o_spread = arrays[5], arrays[10]
        rest = [
            pl.pallas_call(
                weigh_kernel,
                out_shape=slabs,
                in_specs=whole_vmem(4),
                out_specs=whole_vmem(1)[0],
                compiler_params=params,
            )(normed, rest[0], o_spread, rest[1])
        ]
    return rest[0], sums, da, da_own, dh


def whole_vmem(count):
    return [pl.BlockSpec(memory_space=pltpu.VMEM)] * count


def ffn_kernel(
    mid_ref, ups_ref, w_up_t_ref, w_down_ref, b_up_ref,
    gm_ref, br_ref, gup_ref, gdown_ref, gb_ref,
    mids, parts, acts, grads, up_total, down_total, give, take, bias_part, bias_all,
    core_buf, side_buf, up_buf, down_buf,
    g_send, g_recv, c_send, c_recv, r_send, r_recv, y_send, y_recv, b_send, b_recv,
):
    line, column, core, lines = place()
    rows, width = mid_ref.shape
    cycle = lax.axis_size("ctx")
    mine = lax.axis_index("ctx")
    me = device_at(line, column, core)
    partner = device_at(line, column, 1 - core)
    greet()

    gather = gather_stream(
        mid_ref,
        lambda shard: mids.at[shard],
        lambda way, shard: g_send.at[way, shard],
        lambda shard: g_recv.at[shard],
        False,
    )
    gather.start()
    mids[me] = mid_ref[...]
    bias_part[...] = jnp.zeros_like(bias_part)

    def to_core(chip):
        return remote(
            parts.at[chip * CORES + 1 - core],
            core_buf.at[chip],
            c_send.at[chip],
            c_recv.at[chip],
            {"dp": partner},
        )

    def feed(chip):
        pair = pl.ds(chip * CORES, CORES)
        mid = mids[pair].reshape(CORES * rows, width)
        ups = ups_ref[pair].reshape(CORES * rows, width)
        pre = contract_last(mid, w_up_t_ref[...]) + b_up_ref[...]
        grad = contract_last(ups, w_down_ref[...])
        half = 0.5 * (1.0 + lax.erf(pre * 0.7071067811865476))
        act = (pre * half).astype(jnp.bfloat16)
        grad = grad * (half + pre * jnp.exp(-0.5 * pre * pre) * 0.3989422804014327)
        bias_part[...] += jnp.sum(grad, axis=0, keepdims=True)
        grad = grad.astype(jnp.bfloat16)
        acts[chip] = act
        grads[chip] = grad
        part = jnp.dot(grad, w_up_t_ref[...], preferred_element_type=jnp.float32)
        parts[pair] = part.astype(jnp.bfloat16).reshape(CORES, rows, width)
        to_core(chip).start()
        branch = jnp.dot(act, w_down_ref[...], preferred_element_type=jnp.float32)
        br_ref[pair] = branch.astype(jnp.bfloat16).reshape(CORES, rows, width)

    def visit(d, carry):
        @pl.when(d + 1 < lines)
        def _():
            gather.relay(d + 1)

        at = nearest(d)
        gather.arrived(device_at(at, column, 1 - core))
        feed(at * COLUMNS + column)
        gather.cross(at)
        gather.arrived(device_at(at, 1 - column, 1 - core))
        feed(at * COLUMNS + 1 - column)
        return carry

    lax.fori_loop(0, lines, visit, 0)

    def have(chip):
        to_core(chip).wait_recv()
        return core_buf[chip].astype(jnp.float32) + parts[chip * CORES + core].astype(jnp.float32)

    def settle(total, first):
        gm_ref[...] = total if first else gm_ref[...] + total

    reduce = reduce_stream(
        have,
        (side_buf, up_buf, down_buf, lambda chip: parts.at[chip * CORES + core]),
        r_send,
        r_recv,
        settle,
    )
    for by in range(lines - 1, -1, -1):
        on_distance(by, reduce.to_beside)

    def swap(c, source):
        return remote(give.at[c], take.at[source], y_send.at[c], y_recv.at[source], {"ctx": c})

    def swap_bias(c, source):
        landing = bias_all.at[source]
        return remote(bias_part, landing, b_send.at[c], b_recv.at[source], {"ctx": c})

    bias_all[mine] = bias_part[...]
    others = [(mine + by) % cycle for by in range(1, cycle)]
    for c in others:
        swap_bias(c, mine).start()
    up_total[...] = jnp.zeros_like(up_total)
    down_total[...] = jnp.zeros_like(down_total)

    def weigh(chip, carry):
        pair = pl.ds(chip * CORES, CORES)
        up_total[...] += contract_first(grads[chip], mids[pair].reshape(CORES * rows, width))
        down_total[...] += contract_first(acts[chip], ups_ref[pair].reshape(CORES * rows, width))
        return carry

    lax.fori_loop(0, lines * COLUMNS, weigh, 0)
    size = width // cycle
    for c in range(cycle):
        up_part = up_total[:, c * size : (c + 1) * size]
        down_part = down_total[:, c * size : (c + 1) * size]

        @pl.when(c == mine)
        def _():
            gup_ref[...] = up_part
            gdown_ref[...] = down_part

        @pl.when(c != mine)
        def _():
            give[c, 0] = up_part.astype(give.dtype)
            give[c, 1] = down_part.astype(give.dtype)
            swap(c, mine).start()

    for by in range(lines - 1, -1, -1):
        on_distance(by, reduce.along)
    for c in others:
        swap(c, c).wait_recv()
        gup_ref[...] += take[c, 0].astype(jnp.float32)
        gdown_ref[...] += take[c, 1].astype(jnp.float32)
        swap_bias(c, c).wait_recv()
    total = bias_all[0]
    for c in range(1, cycle):
        total = total + bias_all[c]
    gb_ref[...] = total
    for c in others:
        swap(c, mine).wait_send()
        swap_bias(c, mine).wait_send()
    for chip in range(lines * COLUMNS):
        to_core(chip).wait_send()
    reduce.finish()
    gather.finish()


def feed_forward(mid, ups, w_up, w_down, b_up, collective_id):
    peers = lax.axis_size("dp")
    cycle = lax.axis_size("ctx")
    lines = peers // (CORES * COLUMNS)
    chips = lines * COLUMNS
    rows, width = mid.shape
    hidden = w_up.shape[1]
    dma = pltpu.SemaphoreType.DMA

    def slabs(count):
        return pltpu.VMEM((count, rows, width), jnp.bfloat16)

    return pl.pallas_call(
        ffn_kernel,
        out_shape=(
            jax.ShapeDtypeStruct((rows, width), jnp.float32),
            jax.ShapeDtypeStruct((peers, rows, width), jnp.bfloat16),
            jax.ShapeDtypeStruct((hidden, width // cycle), jnp.float32),
            jax.ShapeDtypeStruct((hidden, width // cycle), jnp.float32),
            jax.ShapeDtypeStruct((1, hidden), jnp.float32),
        ),
        in_specs=whole_vmem(5),
        out_specs=tuple(whole_vmem(5)),
        scratch_shapes=[
            slabs(peers),
            slabs(peers),
            pltpu.VMEM((chips, CORES * rows, hidden), jnp.bfloat16),
            pltpu.VMEM((chips, CORES * rows, hidden), jnp.bfloat16),
            pltpu.VMEM((hidden, width), jnp.float32),
            pltpu.VMEM((hidden, width), jnp.float32),
            pltpu.VMEM((cycle, 2, hidden, width // cycle), jnp.bfloat16),
            pltpu.VMEM((cycle, 2, hidden, width // cycle), jnp.bfloat16),
            pltpu.VMEM((1, hidden), jnp.float32),
            pltpu.VMEM((cycle, 1, hidden), jnp.float32),
            slabs(chips),
            slabs(lines),
            slabs(lines),
            slabs(lines),
            dma((4, peers)),
            dma((peers,)),
            dma((chips,)),
            dma((chips,)),
            dma((4, lines)),
            dma((4, lines)),
            dma((cycle,)),
            dma((cycle,)),
            dma((cycle,)),
            dma((cycle,)),
        ],
        compiler_params=pltpu.CompilerParams(
            collective_id=collective_id, has_side_effects=True, vmem_limit_bytes=VMEM_LIMIT
        ),
    )(mid, ups, w_up.T, w_down, b_up.astype(jnp.float32)[None, :])


def settle_kernel(
    slab_ref, br_ref, sums_ref, da_ref, da_own_ref, dh_ref, h_ref, x_ref, vec_ref,
    out_t_ref, ing_t_ref, gq_ref, go_ref, total_ref,
    slab_core, slab_cycle, slab_side, slab_up, slab_down,
    slab_sum, branch_sum,
    br_core, br_side, br_up, br_down,
    da_all, stage, sums_core, sums_cycle, sums_side, sums_line,
    sc_send, sc_recv, sy_send, sy_recv, sr_send, sr_recv, bc_send, bc_recv, br_send, br_recv,
    a_send, a_recv, one_send, one_recv, cyc_send, cyc_recv, lin_send, lin_recv,
):
    line, column, core, lines = place()
    rows, width = dh_ref.shape
    shard = gq_ref.shape[0]
    cycle = lax.axis_size("ctx")
    mine = lax.axis_index("ctx")
    beside = device_at(line, 1 - column, core)
    partner = device_at(line, column, 1 - core)
    others = [(mine + by) % cycle for by in range(1, cycle)]
    greet()

    def slab_to_core(c, chip):
        return remote(
            slab_ref.at[c, chip * CORES + 1 - core],
            slab_core.at[c, chip],
            sc_send.at[c, chip],
            sc_recv.at[c, chip],
            {"dp": partner},
        )

    def slab_to_cycle(c, chip, source):
        return remote(
            slab_core.at[c, chip],
            slab_cycle.at[source, chip],
            sy_send.at[c, chip],
            sy_recv.at[source, chip],
            {"ctx": c},
        )

    def br_to_core(chip):
        return remote(
            br_ref.at[chip * CORES + 1 - core],
            br_core.at[chip],
            bc_send.at[chip],
            bc_recv.at[chip],
            {"dp": partner},
        )

    def da_swap(c, source):
        return remote(da_ref.at[c], da_all.at[source], a_send.at[c], a_recv.at[source], {"ctx": c})

    def both(act):
        def visit(target, step):
            act(target * COLUMNS + 1 - column)
            act(target * COLUMNS + column)

        return visit

    def far_first(act):
        for by in range(lines - 1, -1, -1):
            on_distance(by, act)

    sums_to_core = remote(sums_ref, sums_core, one_send.at[0], one_recv.at[0], {"dp": partner})
    sums_to_side = remote(stage.at[1], sums_side, one_send.at[1], one_recv.at[1], {"dp": beside})

    def sums_to_cycle(c, source):
        landing = sums_cycle.at[source]
        return remote(stage.at[0], landing, cyc_send.at[c], cyc_recv.at[source], {"ctx": c})

    def sums_to_line(to, source):
        target = {"dp": device_at(to, column, core)}
        return remote(
            stage.at[2], sums_line.at[source], lin_send.at[to], lin_recv.at[source], target
        )

    sums_to_core.start()

    def send_parts(chip):
        for c in others:
            slab_to_core(c, chip).start()

    far_first(both(send_parts))
    far_first(both(lambda chip: br_to_core(chip).start()))
    far_first(both(lambda chip: slab_to_core(mine, chip).start()))

    def cycle_sums(chip):
        for c in others:
            slab_to_core(c, chip).wait_recv()
            total = slab_core[c, chip].astype(jnp.float32)
            total = total + slab_ref[c, chip * CORES + core].astype(jnp.float32)
            slab_core[c, chip] = total.astype(slab_core.dtype)
            slab_to_cycle(c, chip, mine).start()

    def br_have(chip):
        br_to_core(chip).wait_recv()
        return br_core[chip].astype(jnp.float32) + br_ref[chip * CORES + core].astype(jnp.float32)

    def br_settle(total, first):
        if first:
            branch_sum[...] = total
        else:
            branch_sum[...] += total

    def slab_have(chip):
        slab_to_core(mine, chip).wait_recv()
        total = slab_core[mine, chip].astype(jnp.float32)
        total = total + slab_ref[mine, chip * CORES + core].astype(jnp.float32)
        for c in others:
            slab_to_cycle(c, chip, c).wait_recv()
            total = total + slab_cycle[c, chip].astype(jnp.float32)
        return total

    def slab_settle(total, first):
        slab_sum[...] = total if first else slab_sum[...] + total

    branch = reduce_stream(
        br_have, (br_side, br_up, br_down, lambda chip: br_core.at[chip]), br_send, br_recv, br_settle
    )
    slabs = reduce_stream(
        slab_have,
        (slab_side, slab_up, slab_down, lambda chip: slab_core.at[mine, chip]),
        sr_send,
        sr_recv,
        slab_settle,
    )

    def first_hop(target, step):
        both(cycle_sums)(target, step)
        branch.to_beside(target, step)

    sums_to_core.wait_recv()
    stage[0] = sums_ref[...] + sums_core[...]
    sums_cycle[mine] = stage[0]
    for c in others:
        sums_to_cycle(c, mine).start()
    on_distance(lines - 1, lambda target, step: both(cycle_sums)(target, step))
    for c in others:
        sums_to_cycle(c, c).wait_recv()
    total = sums_cycle[0]
    for c in range(1, cycle):
        total = total + sums_cycle[c]
    stage[1] = total
    sums_to_side.start()
    on_distance(lines - 1, branch.to_beside)
    for by in range(lines - 2, -1, -1):
        on_distance(by, first_hop)
    for c in others:
        da_swap(c, mine).start()
    sums_to_side.wait_recv()
    stage[2] = stage[1] + sums_side[...]
    sums_line[line] = stage[2]
    for away in range(1, lines):
        sums_to_line((line + away) % lines, line).start()

    for by in range(lines - 1, -1, -1):
        on_distance(by, slabs.to_beside)
        on_distance(by, branch.along)
        if by + 1 < lines:
            on_distance(by + 1, slabs.along)
    out_t_ref[...] = (h_ref[...] + branch_sum[...] + vec_ref[7:8, :]).astype(out_t_ref.dtype).T
    grad = da_own_ref[...]
    for c in others:
        da_swap(c, c).wait_recv()
        grad = grad + da_all[c].astype(jnp.float32)
    gain, bias = vec_ref[0:1, :], vec_ref[1:2, :]
    _, normed, inverse = norm_parts(x_ref[mine].astype(jnp.float32), gain, bias)
    ing_t_ref[...] = (dh_ref[...] + norm_back(grad, normed, inverse, gain)).T
    for away in range(1, lines):
        source = (line + away) % lines
        sums_to_line(source, source).wait_recv()
    total = sums_line[0]
    for by in range(1, lines):
        total = total + sums_line[by]
    total_ref[...] = total
    on_distance(0, slabs.along)
    tall = gq_ref.shape[1]
    gq_ref[...] = slab_sum[:shard, :tall]
    go_ref[...] = slab_sum[:shard, tall:]

    sums_to_core.wait_send()
    sums_to_side.wait_send()
    for c in others:
        sums_to_cycle(c, mine).wait_send()
        da_swap(c, mine).wait_send()
    for away in range(1, lines):
        sums_to_line((line + away) % lines, line).wait_send()
    branch.finish()
    slabs.finish()
    for chip in range(lines * COLUMNS):
        br_to_core(chip).wait_send()
        slab_to_core(mine, chip).wait_send()
        for c in others:
            slab_to_core(c, chip).wait_send()
            slab_to_cycle(c, chip, mine).wait_send()


def settle(slabs, branch, sums, da, da_own, dh, hidden, x, vectors, collective_id):
    cycle, peers, padded, size = slabs.shape
    rows, width = dh.shape
    lines = peers // (CORES * COLUMNS)
    chips = lines * COLUMNS
    shard = width // peers
    dma = pltpu.SemaphoreType.DMA
    f32, bf16 = jnp.float32, jnp.bfloat16

    def pieces(*lead):
        return pltpu.VMEM(lead + (padded, size), bf16)

    def blocks(*lead):
        return pltpu.VMEM(lead + (rows, width), bf16)

    def totals(*lead):
        return pltpu.VMEM(lead + sums.shape, f32)

    return pl.pallas_call(
        settle_kernel,
        out_shape=(
            jax.ShapeDtypeStruct((width, rows), bf16),
            jax.ShapeDtypeStruct((width, rows), f32),
            jax.ShapeDtypeStruct((shard, 3 * width // cycle), f32),
            jax.ShapeDtypeStruct((shard, width // cycle), f32),
            jax.ShapeDtypeStruct(sums.shape, f32),
        ),
        in_specs=whole_vmem(9),
        out_specs=tuple(whole_vmem(5)),
        scratch_shapes=[pieces(cycle, chips), pieces(cycle, chips)]
        + [pieces(lines)] * 3
        + [pltpu.VMEM((padded, size), f32), pltpu.VMEM((rows, width), f32)]
        + [blocks(chips)]
        + [blocks(lines)] * 3
        + [blocks(cycle), totals(3), totals(), totals(cycle), totals(), totals(lines)]
        + [dma((cycle, chips))] * 4
        + [dma((4, lines))] * 2
        + [dma((chips,))] * 2
        + [dma((4, lines))] * 2
        + [dma((cycle,))] * 2
        + [dma((2,))] * 2
        + [dma((cycle,))] * 2
        + [dma((lines,))] * 2,
        compiler_params=pltpu.CompilerParams(
            collective_id=collective_id, has_side_effects=True, vmem_limit_bytes=VMEM_LIMIT
        ),
    )(slabs, branch, sums, da, da_own, dh, hidden, x, vectors)


def per_device(
    block_in,
    cotangent,
    block_order,
    ln1_gain,
    ln1_bias,
    w_qkv,
    b_query,
    b_value,
    w_out,
    b_out,
    ln2_gain,
    ln2_bias,
    w_up,
    b_up,
    w_down,
    b_down,
):
    width, shard = w_out.shape[1], w_out.shape[0]
    peers = lax.axis_size("dp")
    rows_t, upstream_t = block_in[0].T, cotangent[0].T
    vectors = jnp.stack(
        [ln1_gain, ln1_bias, b_query, b_value, b_out, ln2_gain, ln2_bias, b_down]
    )
    count = vectors.shape[0]
    weights, ups, rows = load(vectors, w_qkv, w_out, upstream_t, rows_t, 0)
    vectors = weights[0, :, shard, : count * shard].reshape(peers, count, shard)
    vectors = jnp.transpose(vectors, (1, 0, 2)).reshape(count, width).astype(jnp.float32)
    weights = weights.reshape(weights.shape[0], -1, weights.shape[3])
    spread, normed, q, k, v, o, o_spread, hidden, mid = forward(
        block_order, rows, weights, vectors
    )
    grad_mid, branch, g_up, g_down, g_bias_up = feed_forward(mid, ups, w_up, w_down, b_up, 1)
    slabs, sums, da, da_own, dh = backward(
        block_order, rows, weights, vectors, spread, normed,
        q, k, v, o, o_spread, hidden, upstream_t, grad_mid,
    )
    block_out_t, grad_input_t, g_qkv, g_out, sums = settle(
        slabs, branch, sums, da, da_own, dh, hidden, rows, vectors, 3
    )
    sums = lax.dynamic_slice_in_dim(sums, lax.axis_index("dp") * shard, shard, 1)
    return (
        block_out_t.T[None],
        grad_input_t.T[None],
        sums[0],
        sums[1],
        g_qkv,
        sums[2],
        sums[3],
        g_out,
        sums[4],
        sums[5],
        sums[6],
        g_up.T,
        g_bias_up[0],
        g_down,
        sums[7],
    )


def solution(mesh):
    in_specs = (
        P("dp", "ctx", None),
        P("dp", "ctx", None),
        P(),
        P("dp"),
        P("dp"),
        P("dp", None),
        P("dp"),
        P("dp"),
        P("dp", None),
        P("dp"),
        P("dp"),
        P("dp"),
        P(None, "dp"),
        P("dp"),
        P("dp", None),
        P("dp"),
    )
    out_specs = (
        P("dp", "ctx", None),
        P("dp", "ctx", None),
        P("dp"),
        P("dp"),
        P("dp", "ctx"),
        P("dp"),
        P("dp"),
        P("dp", "ctx"),
        P("dp"),
        P("dp"),
        P("dp"),
        P("ctx", "dp"),
        P("dp"),
        P("dp", "ctx"),
        P("dp"),
    )
    return jax.shard_map(
        per_device, mesh=mesh, in_specs=in_specs, out_specs=out_specs, check_vma=False
    )
```

```python
import functools
import types

import jax
import jax.numpy as jnp
from jax import lax
from jax.experimental import pallas as pl
from jax.experimental.pallas import tpu as pltpu
from jax.sharding import PartitionSpec as P

HD = 64
SCALE = 0.125


def norm_parts(values, gain_values, shift_values):
    average = jnp.mean(values, axis=-1, keepdims=True)
    centered = values - average
    inverse = lax.rsqrt(jnp.mean(centered * centered, axis=-1, keepdims=True) + 1e-05)
    normed = centered * inverse
    return normed * gain_values + shift_values, normed, inverse


def norm_back(upstream, normed, inverse, gain_values):
    scaled = upstream * gain_values
    return inverse * (
        scaled
        - jnp.mean(scaled, axis=-1, keepdims=True)
        - normed * jnp.mean(scaled * normed, axis=-1, keepdims=True)
    )


def contract_first(left, right):
    return lax.dot_general(
        left, right, (((0,), (0,)), ((), ())), preferred_element_type=jnp.float32
    )


def contract_last(left, right):
    return lax.dot_general(
        left, right, (((1,), (1,)), ((), ())), preferred_element_type=jnp.float32
    )


def head_groups(width):
    groups = [(start, 128) for start in range(0, width - width % 128, 128)]
    if width % 128:
        groups.append((width - width % 128, width % 128))
    return groups


def head_masks(lanes):
    if lanes == HD:
        return [None]
    lane = lax.broadcasted_iota(jnp.int32, (1, lanes), 1)
    return [
        jnp.where((lane >= first) & (lane < first + HD), 1.0, 0.0).astype(jnp.bfloat16)
        for first in range(0, lanes, HD)
    ]


def keep(array, mask):
    return array if mask is None else array * mask


MESH = pl.DeviceIdType.MESH
CORES = 2
COLUMNS = 2
VMEM_LIMIT = 63 * 1024 * 1024
UP, DOWN, ACROSS, PARTNER = range(4)
SIDES = ((1, UP), (-1, DOWN))
GROUP = 8
FUSED_LIMIT = 9 * 1024 * 1024


def place():
    index = lax.axis_index("dp")
    lines = lax.axis_size("dp") // (CORES * COLUMNS)
    core = index % CORES
    column = (index // CORES) % COLUMNS
    return index // (CORES * COLUMNS), column, core, lines


def device_at(line, column, core):
    return (line * COLUMNS + column) * CORES + core


def on_line(line, lines):
    return (line >= 0) & (line < lines)


def greet():
    line, column, core, lines = place()
    cycle = lax.axis_size("ctx")
    mine = lax.axis_index("ctx")
    barrier = pltpu.get_barrier_semaphore()
    peers = [{"dp": device_at((line + by) % lines, column, core)} for by in range(1, lines)]
    peers += [{"dp": device_at(line, 1 - column, core)}, {"dp": device_at(line, column, 1 - core)}]
    peers += [{"ctx": (mine + by) % cycle} for by in range(1, cycle)]
    for peer in peers:
        pl.semaphore_signal(barrier, inc=1, device_id=peer, device_id_type=MESH)
    pl.semaphore_wait(barrier, len(peers))


def remote(source, landing, send, recv, target):
    return pltpu.make_async_remote_copy(
        src_ref=source,
        dst_ref=landing,
        send_sem=send,
        recv_sem=recv,
        device_id=target,
        device_id_type=MESH,
    )


def on_distance(by, act):
    line, _, _, lines = place()
    if by == 0:
        act(line, 0)
        return
    for step in (1, -1):

        @pl.when(on_line(line + step * by, lines))
        def _():
            act(line + step * by, step)


def nearest(d):
    line, _, _, lines = place()
    toward = 1 - 2 * ((2 * line) // lines)
    return (line + toward * d + lines) % lines


def gather_stream(own, land, send, recv, balanced):
    line, column, core, lines = place()
    me = device_at(line, column, core)
    beside = device_at(line, 1 - column, core)
    partner = device_at(line, column, 1 - core)

    def push(shard, way, target, source=None):
        source = land(shard) if source is None else source
        remote(source, land(shard), send(way, shard), recv(shard), {"dp": target}).start()

    def arrived(shard):
        buffer = land(shard)
        remote(buffer, buffer, send(PARTNER, shard), recv(shard), {"dp": partner}).wait_recv()

    def sent(shard, way):
        buffer = land(shard)
        remote(buffer, buffer, send(way, shard), recv(shard), {"dp": partner}).wait_send()

    def start():
        push(me, ACROSS, beside, own)
        for step, way in SIDES:

            @pl.when(on_line(line + step, lines))
            def _():
                push(me, way, device_at(line + step, column, core), own)

        push(me, PARTNER, partner, own)

    def crosses(source, act):
        if balanced:

            @pl.when((source != 0) & (source != lines - 1))
            def _():
                act()

        else:
            act()

    def relay(by, seen=None):
        for step, way in SIDES:

            @pl.when(on_line(line - step * by, lines))
            def _():
                shard = device_at(line - step * by, column, core)
                arrived(shard)

                @pl.when(on_line(line + step, lines))
                def _():
                    push(shard, way, device_at(line + step, column, core))

                crosses(line - step * by, lambda: push(shard, ACROSS, beside))
                push(shard, PARTNER, partner)
                if seen is not None:
                    seen(shard)

    def through(source, act):
        if balanced:
            for step, way in SIDES:
                end = 0 if step > 0 else lines - 1

                @pl.when((source == end) & on_line(line + step, lines))
                def _():
                    act(way, device_at(line + step, column, core))

    def cross(source, seen=None):
        shard = device_at(source, 1 - column, core)
        arrived(shard)
        through(source, lambda way, target: push(shard, way, target))
        push(shard, PARTNER, partner)
        if seen is not None:
            seen(shard)

    def finish():
        def visit(source, step):
            shard = device_at(source, column, core)
            far = device_at(source, 1 - column, core)
            sent(shard, PARTNER)
            sent(far, PARTNER)
            if step:
                crosses(source, lambda: sent(shard, ACROSS))
            else:
                sent(shard, ACROSS)
            through(source, lambda way, target: sent(far, way))
            for along, way in SIDES:
                if step in (0, -along):

                    @pl.when(on_line(line + along, lines))
                    def _():
                        sent(shard, way)

        for by in range(lines):
            on_distance(by, visit)

    return types.SimpleNamespace(
        start=start, relay=relay, cross=cross, arrived=arrived, finish=finish
    )


def reduce_stream(have, buffers, send, recv, settle):
    line, column, core, lines = place()
    side_buf, up_buf, down_buf, stash = buffers
    beside = device_at(line, 1 - column, core)

    def landed(buffer, way, slot):
        copy = remote(buffer, buffer, send.at[way, slot], recv.at[way, slot], {"dp": beside})
        copy.wait_recv()
        return buffer[...].astype(jnp.float32)

    def to_beside(target, step):
        chip = target * COLUMNS + 1 - column
        buffer = stash(chip)
        buffer[...] = have(chip).astype(buffer.dtype)
        remote(
            buffer,
            side_buf.at[target],
            send.at[1, target],
            recv.at[1, target],
            {"dp": beside},
        ).start()

    def along(target, step):
        chip = target * COLUMNS + column
        total = have(chip)
        total = total + landed(side_buf.at[target], 1, target)
        if step == 0:
            for by, way, landing in ((1, 2, up_buf), (-1, 3, down_buf)):
                settle_from(total, by, way, landing)
            return
        way, landing = (2, up_buf) if step > 0 else (3, down_buf)
        buffer = stash(chip)
        buffer[...] = total.astype(buffer.dtype)

        @pl.when(on_line(line - step, lines))
        def _():
            more = landed(landing.at[target], way, target)
            buffer[...] = (total + more).astype(buffer.dtype)

        remote(
            buffer,
            landing.at[target],
            send.at[way, target],
            recv.at[way, target],
            {"dp": device_at(line + step, column, core)},
        ).start()

    def settle_from(total, by, way, landing):
        if way == 2:
            settle(total, True)

        @pl.when(on_line(line - by, lines))
        def _():
            settle(landed(landing.at[line], way, line), False)

    def finish():
        def visit(target, step):
            buffer = side_buf.at[target]
            slots = [(1, target)]
            if step:
                slots.append((2 if step > 0 else 3, target))
            for way, slot in slots:
                remote(
                    buffer, buffer, send.at[way, slot], recv.at[way, slot], {"dp": beside}
                ).wait_send()

        for by in range(lines):
            on_distance(by, visit)

    return types.SimpleNamespace(to_beside=to_beside, along=along, finish=finish)


def pack_weights(vec_ref, qkv_ref, out_ref, w_ref, row):
    count, shard = vec_ref.shape
    cycle, padded, size = w_ref.shape
    width = out_ref.shape[1]
    for c in range(cycle):
        first, last = c * size, (c + 1) * size
        split = min(max(3 * width - first, 0), size)
        if split:
            w_ref[c, :shard, :split] = qkv_ref[:, first : first + split]
        if split < size:
            w_ref[c, :shard, split:] = out_ref[:, first + split - 3 * width : last - 3 * width]
    row[...] = jnp.zeros_like(row)
    for i in range(count):
        row[0:1, i * shard : (i + 1) * shard] = vec_ref[i : i + 1, :].astype(jnp.float32)
    for c in range(cycle):
        w_ref[c, shard:padded, :] = row[: padded - shard, :].astype(jnp.bfloat16)


def load_kernel(
    vec_ref, qkv_ref, out_ref, u_t_ref, x_t_ref, w_all, u_all, x_all, w_ref, row, u_ref, x_ref,
    w_send, w_recv, part_send, cycle_send, u_send, u_recv, x_send, x_recv, local,
):
    line, column, core, lines = place()
    cycle = lax.axis_size("ctx")
    mine = lax.axis_index("ctx")
    me = device_at(line, column, core)
    partner = device_at(line, column, 1 - core)
    others = [(mine + by) % cycle for by in range(1, cycle)]
    pack_weights(vec_ref, qkv_ref, out_ref, w_ref, row)
    x_ref[...] = x_t_ref[...].T
    u_ref[...] = u_t_ref[...].T
    greet()

    weights = gather_stream(
        w_ref.at[mine],
        lambda shard: w_all.at[mine, shard],
        lambda way, shard: w_send.at[way, shard],
        lambda shard: w_recv.at[mine, shard],
        False,
    )
    ups = gather_stream(
        u_ref,
        lambda shard: u_all.at[shard],
        lambda way, shard: u_send.at[way, shard],
        lambda shard: u_recv.at[shard],
        True,
    )

    def part(c, shard, send, target, source=None):
        landing = w_all.at[c, shard]
        source = landing if source is None else source
        return remote(source, landing, send, w_recv.at[c, shard], target)

    def to_cycle(shard):
        for c in others:
            part(mine, shard, cycle_send.at[c, shard], {"ctx": c}).start()

    def from_cycle(shard):
        for c in others:
            copy = part(c, shard, part_send.at[c, shard], {"dp": partner})
            copy.wait_recv()
            copy.start()

    def swap(c, source):
        return remote(x_ref, x_all.at[source], x_send.at[c], x_recv.at[source], {"ctx": c})

    copies = [
        pltpu.make_async_copy(w_ref.at[c], w_all.at[c, me], local.at[c]) for c in range(cycle)
    ]
    copies.append(pltpu.make_async_copy(u_ref, u_all.at[me], local.at[cycle]))
    copies.append(pltpu.make_async_copy(x_ref, x_all.at[mine], local.at[cycle + 1]))
    weights.start()
    for c in others:
        swap(c, mine).start()
    ups.start()
    for c in others:
        part(c, me, part_send.at[c, me], {"dp": partner}, w_ref.at[c]).start()
    for copy in copies:
        copy.start()

    for d in range(lines):
        if d + 1 < lines:
            weights.relay(d + 1, to_cycle)
            ups.relay(d + 1)
        on_distance(d, lambda source, step: weights.cross(source, to_cycle))
        on_distance(d, lambda source, step: ups.cross(source))
        if d > 0:
            on_distance(d, lambda source, step: from_cycle(device_at(source, column, core)))
            on_distance(d - 1, lambda source, step: from_cycle(device_at(source, 1 - column, core)))
    on_distance(
        lines - 1, lambda source, step: from_cycle(device_at(source, 1 - column, core))
    )
    for chip in range(lines * COLUMNS):
        shard = chip * CORES + 1 - core
        weights.arrived(shard)
        ups.arrived(shard)
        for c in others:
            part(c, shard, part_send.at[c, shard], {"dp": partner}).wait_recv()
    weights.finish()
    ups.finish()
    for c in others:
        swap(c, c).wait_recv()
        swap(c, mine).wait_send()
        part(c, me, part_send.at[c, me], {"dp": partner}).wait_send()
    for d in range(lines):
        for across in (column, 1 - column):
            if d == 0 and across is column:
                continue
            shard = device_at(nearest(d), across, core)
            for c in others:
                part(c, shard, part_send.at[c, shard], {"dp": partner}).wait_send()
                part(mine, shard, cycle_send.at[c, shard], {"ctx": c}).wait_send()
    for copy in copies:
        copy.wait()


def load(vectors, w_qkv, w_out, ups_t, rows_t, collective_id):
    peers = lax.axis_size("dp")
    cycle = lax.axis_size("ctx")
    shard = w_out.shape[0]
    padded = (shard // GROUP + 1) * GROUP
    size = 4 * w_out.shape[1] // cycle
    block = ups_t.shape[::-1]
    bf16 = jnp.bfloat16
    dma = pltpu.SemaphoreType.DMA
    return pl.pallas_call(
        load_kernel,
        out_shape=(
            jax.ShapeDtypeStruct((cycle, peers, padded, size), bf16),
            jax.ShapeDtypeStruct((peers,) + block, bf16),
            jax.ShapeDtypeStruct((cycle,) + block, bf16),
        ),
        in_specs=whole_vmem(5),
        out_specs=tuple([pl.BlockSpec(memory_space=pl.ANY)] * 3),
        scratch_shapes=[
            pltpu.VMEM((cycle, padded, size), bf16),
            pltpu.VMEM((GROUP, size), jnp.float32),
            pltpu.VMEM(block, bf16),
            pltpu.VMEM(block, bf16),
            dma((4, peers)),
            dma((cycle, peers)),
            dma((cycle, peers)),
            dma((cycle, peers)),
            dma((4, peers)),
            dma((peers,)),
            dma((cycle,)),
            dma((cycle,)),
            dma((cycle + 2,)),
        ],
        compiler_params=pltpu.CompilerParams(collective_id=collective_id, has_side_effects=True),
    )(vectors, w_qkv, w_out, ups_t, rows_t)


def spreader(width, shard, padded):
    source = lax.broadcasted_iota(jnp.int32, (width, 1), 0).astype(jnp.float32)
    block = jnp.floor((source + 0.5) * (1.0 / shard))
    target = source + block * float(padded - shard)
    lanes = lax.broadcasted_iota(jnp.int32, (1, width // shard * padded), 1).astype(jnp.float32)
    return jnp.where(target == lanes, 1.0, 0.0).astype(jnp.bfloat16)


def visible_bias(order_ref, first, rows, keys):
    block = keys // order_ref.shape[0]

    def position(slot):
        where = slot
        for b in range(order_ref.shape[0]):
            inside = (slot >= b * block) & (slot < (b + 1) * block)
            where = jnp.where(inside, (order_ref[b] - b) * block + slot, where)
        return where

    query = position(first + lax.broadcasted_iota(jnp.int32, (rows, 1), 0))
    key = position(lax.broadcasted_iota(jnp.int32, (1, keys), 1))
    return jnp.where(query >= key, 0.0, -1e30)


def parts_over(first, last, size, count):
    return [c for c in range(count) if c * size < last and (c + 1) * size > first]


def forward_kernel(
    order_ref, x_ref, w_ref, vec_ref,
    spread_ref, normed_ref, q_ref, k_ref, v_ref, o_ref, o_spread_ref, h_ref, mid_ref,
    projected,
):
    cycle, rows, width = x_ref.shape
    shard = width // lax.axis_size("dp")
    mine = lax.axis_index("ctx")
    size = w_ref.shape[2]
    padded = w_ref.shape[1] // lax.axis_size("dp")
    spread_ref[...] = spreader(width, shard, padded)
    gain_one, shift_one, bias_q, bias_v, bias_o, gain_two, shift_two = [
        vec_ref[i : i + 1, :] for i in range(7)
    ]

    def project(left, first, last):
        for c in parts_over(first, last, size, cycle):
            projected[:, c * size : (c + 1) * size] = jnp.dot(
                left, w_ref[c], preferred_element_type=jnp.float32
            )

    def visit(c, carry):
        block = pl.ds(pl.multiple_of(c * rows, rows), rows)
        values, _, _ = norm_parts(x_ref[c].astype(jnp.float32), gain_one, shift_one)
        spread = jnp.dot(
            values.astype(jnp.bfloat16), spread_ref[...], preferred_element_type=jnp.float32
        ).astype(jnp.bfloat16)
        normed_ref[block, :] = spread
        project(spread, 0, 3 * width)
        k_ref[block, :] = projected[:, width : 2 * width].astype(jnp.bfloat16)
        v_ref[block, :] = (projected[:, 2 * width : 3 * width] + bias_v).astype(jnp.bfloat16)

        @pl.when(c == mine)
        def _():
            q_ref[...] = (projected[:, :width] + bias_q).astype(jnp.bfloat16)

        return carry

    lax.fori_loop(0, cycle, visit, 0)
    bias = visible_bias(order_ref, mine * rows, rows, cycle * rows)
    for start, lanes in head_groups(width):
        block = slice(start, start + lanes)
        q, k, v = q_ref[:, block], k_ref[:, block], v_ref[:, block]
        total = None
        for mask in head_masks(lanes):
            scores = contract_last(keep(q, mask), k) * SCALE + bias
            largest = jnp.max(scores, axis=-1, keepdims=True)
            exponent = jnp.exp(scores - largest)
            inverse = 1.0 / jnp.sum(exponent, axis=-1, keepdims=True)
            part = jnp.dot(
                exponent.astype(jnp.bfloat16), keep(v, mask), preferred_element_type=jnp.float32
            )
            part = part * inverse
            total = part if total is None else total + part
        o_ref[:, block] = total.astype(jnp.bfloat16)
    o_spread = jnp.dot(
        o_ref[...], spread_ref[...], preferred_element_type=jnp.float32
    ).astype(jnp.bfloat16)
    o_spread_ref[...] = o_spread
    project(o_spread, 3 * width, 4 * width)
    hidden = x_ref[mine].astype(jnp.float32) + projected[:, 3 * width : 4 * width] + bias_o
    h_ref[...] = hidden
    mid_ref[...] = norm_parts(hidden, gain_two, shift_two)[0].astype(jnp.bfloat16)


def ordered(count):
    return [pl.BlockSpec(memory_space=pltpu.SMEM)] + whole_vmem(count - 1)


def forward(order, x, w, vectors):
    cycle, rows, width = x.shape
    full = w.shape[1]

    def bf(*shape):
        return jax.ShapeDtypeStruct(shape, jnp.bfloat16)

    return pl.pallas_call(
        forward_kernel,
        out_shape=(
            bf(width, full),
            bf(cycle * rows, full),
            bf(rows, width),
            bf(cycle * rows, width),
            bf(cycle * rows, width),
            bf(rows, width),
            bf(rows, full),
            jax.ShapeDtypeStruct((rows, width), jnp.float32),
            bf(rows, width),
        ),
        in_specs=ordered(4),
        out_specs=tuple(whole_vmem(9)),
        scratch_shapes=[pltpu.VMEM((rows, 4 * width), jnp.float32)],
        compiler_params=pltpu.CompilerParams(vmem_limit_bytes=VMEM_LIMIT),
    )(order, x, w, vectors)


def column_sum(values):
    return jnp.sum(values, axis=0, keepdims=True)


def store_owners(grads, ref, padded):
    for s in range(grads.shape[0] // padded):
        ref[s] = grads[s * padded : (s + 1) * padded].astype(ref.dtype)


def weigh_columns(slab_ref, c, normed_ref, wide):
    padded, tall = slab_ref.shape[2:]
    grads = contract_first(normed_ref[...], wide[:, c * tall : (c + 1) * tall])
    store_owners(grads, slab_ref.at[c], padded)


def weigh_kernel(normed_ref, wide_ref, slab_ref):
    for c in range(slab_ref.shape[0]):
        weigh_columns(slab_ref, c, normed_ref, wide_ref)


def back_norm(r):
    rows, width = r.hidden.shape
    gain, shift = r.vec[5:6, :], r.vec[6:7, :]
    _, normed, inverse = norm_parts(r.hidden[...], gain, shift)
    upstream = r.upstream_t[...].T.astype(jnp.float32)
    grad_mid = r.grad_mid[...]
    r.sums[0:2, :] = jnp.zeros((2, width), jnp.float32)
    r.sums[5:6, :] = column_sum(grad_mid * normed)
    r.sums[6:7, :] = column_sum(grad_mid)
    r.sums[7:8, :] = column_sum(upstream)
    grad_hidden = upstream + norm_back(grad_mid, normed, inverse, gain)
    r.dh[...] = grad_hidden
    r.sums[4:5, :] = column_sum(grad_hidden)
    grad_hidden_b = grad_hidden.astype(jnp.bfloat16)
    r.head_wide[...] = jnp.zeros_like(r.head_wide)
    r.head_wide[:, 3 * width : 4 * width] = grad_hidden_b
    grads = contract_first(r.o_spread[...], grad_hidden_b)
    store_owners(grads, r.out_slab, r.out_slab.shape[1])


def back_attend(r):
    cycle, rows, width = r.x.shape
    mine = lax.axis_index("ctx")
    size = r.w.shape[2]
    grad_ctx = None
    for c in parts_over(3 * width, 4 * width, size, cycle):
        more = contract_last(r.head_wide[:, c * size : (c + 1) * size], r.w[c])
        grad_ctx = more if grad_ctx is None else grad_ctx + more
    grad_ctx = contract_last(grad_ctx.astype(jnp.bfloat16), r.spread[...])
    r.do[...] = grad_ctx.astype(jnp.bfloat16)
    r.wide[...] = jnp.zeros_like(r.wide)
    own = pl.ds(pl.multiple_of(mine * rows, rows), rows)
    bias = visible_bias(r.order, mine * rows, rows, cycle * rows)
    for start, lanes in head_groups(width):
        block = slice(start, start + lanes)
        q, k, v = r.q[:, block], r.k[:, block], r.v[:, block]
        do, o = r.do[:, block], r.o[:, block]
        product = do.astype(jnp.float32) * o.astype(jnp.float32)
        dq = dk = dv = None
        for mask in head_masks(lanes):
            q_h, k_h, do_h = keep(q, mask), keep(k, mask), keep(do, mask)
            product_h = product if mask is None else product * mask.astype(jnp.float32)
            delta = jnp.sum(product_h, axis=-1, keepdims=True)
            scores = contract_last(q_h, k) * SCALE + bias
            largest = jnp.max(scores, axis=-1, keepdims=True)
            exponent = jnp.exp(scores - largest)
            p = exponent * (1.0 / jnp.sum(exponent, axis=-1, keepdims=True))
            dp = contract_last(do_h, v)
            ds = (p * (dp - delta)).astype(jnp.bfloat16)
            dv_h = contract_first(p.astype(jnp.bfloat16), do_h)
            dq_h = jnp.dot(ds, k_h, preferred_element_type=jnp.float32)
            dk_h = contract_first(ds, q_h)
            dq = dq_h if dq is None else dq + dq_h
            dk = dk_h if dk is None else dk + dk_h
            dv = dv_h if dv is None else dv + dv_h
        dq = dq * SCALE
        r.wide[own, start : start + lanes] = dq.astype(jnp.bfloat16)
        r.wide[:, width + start : width + start + lanes] = (dk * SCALE).astype(jnp.bfloat16)
        r.wide[:, 2 * width + start : 2 * width + start + lanes] = dv.astype(jnp.bfloat16)
        r.sums[2:3, block] = column_sum(dq)
        r.sums[3:4, block] = column_sum(dv)


def back_rows(r):
    cycle, rows, width = r.x.shape
    mine = lax.axis_index("ctx")
    size = r.w.shape[2]
    gain, shift = r.vec[0:1, :], r.vec[1:2, :]

    def visit(block, carry):
        span = pl.ds(pl.multiple_of(block * rows, rows), rows)
        total = None
        for c in parts_over(0, 3 * width, size, cycle):
            more = contract_last(r.wide[span, c * size : (c + 1) * size], r.w[c])
            total = more if total is None else total + more
        high = total.astype(jnp.bfloat16)
        low = (total - high.astype(jnp.float32)).astype(jnp.bfloat16)
        grad = contract_last(high, r.spread[...]) + contract_last(low, r.spread[...])
        _, normed, _ = norm_parts(r.x[block].astype(jnp.float32), gain, shift)
        r.sums[0:1, :] += column_sum(grad * normed)
        r.sums[1:2, :] += column_sum(grad)
        r.da[block] = grad.astype(jnp.bfloat16)

        @pl.when(block == mine)
        def _():
            r.da_own[...] = grad

        return carry

    lax.fori_loop(0, cycle, visit, 0)


BACK_INS = [
    "order", "x", "w", "vec", "spread", "normed", "q", "k", "v", "o", "o_spread", "hidden",
    "upstream_t", "grad_mid",
]
BACK_MADE = ["sums", "da", "da_own", "dh", "out_slab"]
BACK_KEPT = ["wide", "head_wide", "do"]


def back_kernel(*refs):
    r = types.SimpleNamespace(**dict(zip(BACK_INS + BACK_MADE + BACK_KEPT, refs)))
    back_norm(r)
    back_attend(r)
    back_rows(r)


def back_shapes(x, padded):
    cycle, rows, width = x.shape
    f32, bf16 = jnp.float32, jnp.bfloat16
    made = [
        ((8, width), f32),
        ((cycle, rows, width), bf16),
        ((rows, width), f32),
        ((rows, width), f32),
        ((lax.axis_size("dp"), padded, width), bf16),
    ]
    kept = [((cycle * rows, 4 * width), bf16), ((rows, 4 * width), bf16), ((rows, width), bf16)]
    return made, kept


def backward(arrays, padded):
    named = dict(zip(BACK_INS, arrays))
    cycle, rows, width = named["x"].shape
    made, kept = back_shapes(named["x"], padded)
    params = pltpu.CompilerParams(vmem_limit_bytes=VMEM_LIMIT)
    sums, da, da_own, dh, out_slab, wide = pl.pallas_call(
        back_kernel,
        out_shape=tuple(jax.ShapeDtypeStruct(*entry) for entry in made + kept[:1]),
        in_specs=ordered(len(arrays)),
        out_specs=tuple(whole_vmem(len(made) + 1)),
        scratch_shapes=[pltpu.VMEM(*entry) for entry in kept[1:]],
        compiler_params=params,
    )(*arrays)
    slab = pl.pallas_call(
        weigh_kernel,
        out_shape=jax.ShapeDtypeStruct(
            (cycle, out_slab.shape[0], padded, 3 * width // cycle), jnp.bfloat16
        ),
        in_specs=whole_vmem(2),
        out_specs=whole_vmem(1)[0],
        compiler_params=params,
    )(named["normed"], wide)
    return slab, sums, da, da_own, dh, out_slab


def whole_vmem(count):
    return [pl.BlockSpec(memory_space=pltpu.VMEM)] * count


def ffn_kernel(
    mid_ref, ups_ref, w_up_t_ref, w_down_ref, b_up_ref,
    gm_ref, br_ref, gup_ref, gdown_ref, gb_ref,
    mids, parts, acts, grads, up_total, down_total, give, take, bias_part, bias_all,
    core_buf, side_buf, up_buf, down_buf,
    g_send, g_recv, c_send, c_recv, r_send, r_recv, y_send, y_recv, b_send, b_recv,
):
    line, column, core, lines = place()
    rows, width = mid_ref.shape
    cycle = lax.axis_size("ctx")
    mine = lax.axis_index("ctx")
    me = device_at(line, column, core)
    partner = device_at(line, column, 1 - core)
    greet()

    gather = gather_stream(
        mid_ref,
        lambda shard: mids.at[shard],
        lambda way, shard: g_send.at[way, shard],
        lambda shard: g_recv.at[shard],
        False,
    )
    gather.start()
    mids[me] = mid_ref[...]
    bias_part[...] = jnp.zeros_like(bias_part)

    def to_core(chip):
        return remote(
            parts.at[chip * CORES + 1 - core],
            core_buf.at[chip],
            c_send.at[chip],
            c_recv.at[chip],
            {"dp": partner},
        )

    def feed(chip):
        pair = pl.ds(chip * CORES, CORES)
        mid = mids[pair].reshape(CORES * rows, width)
        ups = ups_ref[pair].reshape(CORES * rows, width)
        pre = contract_last(mid, w_up_t_ref[...]) + b_up_ref[...]
        grad = contract_last(ups, w_down_ref[...])
        half = 0.5 * (1.0 + lax.erf(pre * 0.7071067811865476))
        act = (pre * half).astype(jnp.bfloat16)
        grad = grad * (half + pre * jnp.exp(-0.5 * pre * pre) * 0.3989422804014327)
        bias_part[...] += jnp.sum(grad, axis=0, keepdims=True)
        grad = grad.astype(jnp.bfloat16)
        acts[chip] = act
        grads[chip] = grad
        part = jnp.dot(grad, w_up_t_ref[...], preferred_element_type=jnp.float32)
        parts[pair] = part.astype(jnp.bfloat16).reshape(CORES, rows, width)
        to_core(chip).start()
        branch = jnp.dot(act, w_down_ref[...], preferred_element_type=jnp.float32)
        br_ref[pair] = branch.astype(jnp.bfloat16).reshape(CORES, rows, width)

    def visit(d, carry):
        @pl.when(d + 1 < lines)
        def _():
            gather.relay(d + 1)

        at = nearest(d)
        gather.arrived(device_at(at, column, 1 - core))
        feed(at * COLUMNS + column)
        gather.cross(at)
        gather.arrived(device_at(at, 1 - column, 1 - core))
        feed(at * COLUMNS + 1 - column)
        return carry

    lax.fori_loop(0, lines, visit, 0)

    def have(chip):
        to_core(chip).wait_recv()
        return core_buf[chip].astype(jnp.float32) + parts[chip * CORES + core].astype(jnp.float32)

    def settle(total, first):
        gm_ref[...] = total if first else gm_ref[...] + total

    reduce = reduce_stream(
        have,
        (side_buf, up_buf, down_buf, lambda chip: parts.at[chip * CORES + core]),
        r_send,
        r_recv,
        settle,
    )
    for by in range(lines - 1, -1, -1):
        on_distance(by, reduce.to_beside)

    def swap(c, source):
        return remote(give.at[c], take.at[source], y_send.at[c], y_recv.at[source], {"ctx": c})

    def swap_bias(c, source):
        landing = bias_all.at[source]
        return remote(bias_part, landing, b_send.at[c], b_recv.at[source], {"ctx": c})

    bias_all[mine] = bias_part[...]
    others = [(mine + by) % cycle for by in range(1, cycle)]
    for c in others:
        swap_bias(c, mine).start()
    up_total[...] = jnp.zeros_like(up_total)
    down_total[...] = jnp.zeros_like(down_total)

    def weigh(chip, carry):
        pair = pl.ds(chip * CORES, CORES)
        up_total[...] += contract_first(grads[chip], mids[pair].reshape(CORES * rows, width))
        down_total[...] += contract_first(acts[chip], ups_ref[pair].reshape(CORES * rows, width))
        return carry

    lax.fori_loop(0, lines * COLUMNS, weigh, 0)
    size = width // cycle
    for c in range(cycle):
        up_part = up_total[:, c * size : (c + 1) * size]
        down_part = down_total[:, c * size : (c + 1) * size]

        @pl.when(c == mine)
        def _():
            gup_ref[...] = up_part
            gdown_ref[...] = down_part

        @pl.when(c != mine)
        def _():
            give[c, 0] = up_part.astype(give.dtype)
            give[c, 1] = down_part.astype(give.dtype)
            swap(c, mine).start()

    for by in range(lines - 1, -1, -1):
        on_distance(by, reduce.along)
    for c in others:
        swap(c, c).wait_recv()
        gup_ref[...] += take[c, 0].astype(jnp.float32)
        gdown_ref[...] += take[c, 1].astype(jnp.float32)
        swap_bias(c, c).wait_recv()
    total = bias_all[0]
    for c in range(1, cycle):
        total = total + bias_all[c]
    gb_ref[...] = total
    for c in others:
        swap(c, mine).wait_send()
        swap_bias(c, mine).wait_send()
    for chip in range(lines * COLUMNS):
        to_core(chip).wait_send()
    reduce.finish()
    gather.finish()


def feed_forward(mid, ups, w_up, w_down, b_up, collective_id):
    peers = lax.axis_size("dp")
    cycle = lax.axis_size("ctx")
    lines = peers // (CORES * COLUMNS)
    chips = lines * COLUMNS
    rows, width = mid.shape
    hidden = w_up.shape[1]
    dma = pltpu.SemaphoreType.DMA

    def slabs(count):
        return pltpu.VMEM((count, rows, width), jnp.bfloat16)

    return pl.pallas_call(
        ffn_kernel,
        out_shape=(
            jax.ShapeDtypeStruct((rows, width), jnp.float32),
            jax.ShapeDtypeStruct((peers, rows, width), jnp.bfloat16),
            jax.ShapeDtypeStruct((hidden, width // cycle), jnp.float32),
            jax.ShapeDtypeStruct((hidden, width // cycle), jnp.float32),
            jax.ShapeDtypeStruct((1, hidden), jnp.float32),
        ),
        in_specs=whole_vmem(5),
        out_specs=tuple(whole_vmem(5)),
        scratch_shapes=[
            slabs(peers),
            slabs(peers),
            pltpu.VMEM((chips, CORES * rows, hidden), jnp.bfloat16),
            pltpu.VMEM((chips, CORES * rows, hidden), jnp.bfloat16),
            pltpu.VMEM((hidden, width), jnp.float32),
            pltpu.VMEM((hidden, width), jnp.float32),
            pltpu.VMEM((cycle, 2, hidden, width // cycle), jnp.bfloat16),
            pltpu.VMEM((cycle, 2, hidden, width // cycle), jnp.bfloat16),
            pltpu.VMEM((1, hidden), jnp.float32),
            pltpu.VMEM((cycle, 1, hidden), jnp.float32),
            slabs(chips),
            slabs(lines),
            slabs(lines),
            slabs(lines),
            dma((4, peers)),
            dma((peers,)),
            dma((chips,)),
            dma((chips,)),
            dma((4, lines)),
            dma((4, lines)),
            dma((cycle,)),
            dma((cycle,)),
            dma((cycle,)),
            dma((cycle,)),
        ],
        compiler_params=pltpu.CompilerParams(
            collective_id=collective_id, has_side_effects=True, vmem_limit_bytes=VMEM_LIMIT
        ),
    )(mid, ups, w_up.T, w_down, b_up.astype(jnp.float32)[None, :])


def settle_body(r, early, middle, late):
    line, column, core, lines = place()
    rows, width = r.dh.shape
    cycle = lax.axis_size("ctx")
    mine = lax.axis_index("ctx")
    beside = device_at(line, 1 - column, core)
    partner = device_at(line, column, 1 - core)
    others = [(mine + by) % cycle for by in range(1, cycle)]
    chips = range(lines * COLUMNS)
    local = [
        pltpu.make_async_copy(
            r.br.at[chip * CORES + core], r.br_own.at[chip], r.local.at[chip]
        )
        for chip in chips
    ]
    for copy in local:
        copy.start()
    greet()

    def to_core(name, chip):
        source = getattr(r, name)
        sems = getattr(r, name + "_core_sems")
        return remote(
            source.at[chip * CORES + 1 - core],
            getattr(r, name + "_core").at[chip],
            sems.at[0, chip],
            sems.at[1, chip],
            {"dp": partner},
        )

    def slab_to_core(c, chip):
        return remote(
            r.slab.at[c, chip * CORES + 1 - core],
            r.slab_core.at[c, chip],
            r.slab_core_sems.at[0, c, chip],
            r.slab_core_sems.at[1, c, chip],
            {"dp": partner},
        )

    def slab_to_cycle(c, chip, source):
        return remote(
            r.slab_core.at[c, chip],
            r.slab_cycle.at[source, chip],
            r.slab_cycle_sems.at[0, c, chip],
            r.slab_cycle_sems.at[1, source, chip],
            {"ctx": c},
        )

    def swap(name, slot, c, source):
        sems = r.swap_sems
        return remote(
            getattr(r, name).at[c],
            getattr(r, name + "_all").at[source],
            sems.at[0, slot, c],
            sems.at[1, slot, source],
            {"ctx": c},
        )

    def both(act):
        def visit(target, step):
            act(target * COLUMNS + 1 - column)
            act(target * COLUMNS + column)

        return visit

    def far_first(act):
        for by in range(lines - 1, -1, -1):
            on_distance(by, act)

    one = r.one_sems
    sums_to_core = remote(r.sums, r.sums_core, one.at[0, 0], one.at[1, 0], {"dp": partner})
    sums_to_side = remote(r.stage.at[0], r.sums_side, one.at[0, 1], one.at[1, 1], {"dp": beside})

    def sums_to_line(to, source):
        return remote(
            r.stage.at[1],
            r.sums_line.at[source],
            r.line_sems.at[0, to],
            r.line_sems.at[1, source],
            {"dp": device_at(to, column, core)},
        )

    def sums_to_cycle(c, source):
        return remote(
            r.stage.at[2],
            r.sums_cycle.at[source],
            r.swap_sems.at[0, 2, c],
            r.swap_sems.at[1, 2, source],
            {"ctx": c},
        )

    def cycle_sums(chip):
        for c in others:
            slab_to_core(c, chip).wait_recv()
            total = r.slab_core[c, chip].astype(jnp.float32)
            total = total + r.slab[c, chip * CORES + core].astype(jnp.float32)
            r.slab_core[c, chip] = total.astype(r.slab_core.dtype)
            slab_to_cycle(c, chip, mine).start()

    def br_have(chip):
        to_core("br", chip).wait_recv()
        return r.br_core[chip].astype(jnp.float32) + r.br_own[chip].astype(jnp.float32)

    def out_have(chip):
        to_core("out_slab", chip).wait_recv()
        own = r.out_slab[chip * CORES + core].astype(jnp.float32)
        return r.out_slab_core[chip].astype(jnp.float32) + own

    def slab_have(chip):
        slab_to_core(mine, chip).wait_recv()
        total = r.slab_core[mine, chip].astype(jnp.float32)
        total = total + r.slab[mine, chip * CORES + core].astype(jnp.float32)
        for c in others:
            slab_to_cycle(c, chip, c).wait_recv()
            total = total + r.slab_cycle[c, chip].astype(jnp.float32)
        return total

    def into(ref):
        def settle(total, first):
            ref[...] = total if first else ref[...] + total

        return settle

    def stream(have, name, stash, ref):
        sems = getattr(r, name + "_sems")
        lanes = [getattr(r, name + "_lanes").at[i] for i in range(3)]
        return reduce_stream(have, (*lanes, stash), sems.at[0], sems.at[1], into(ref))

    branch = stream(br_have, "br", lambda chip: r.br_own.at[chip], r.branch_sum)
    heads = stream(out_have, "out_slab", lambda chip: r.out_slab_core.at[chip], r.out_sum)
    slabs = stream(slab_have, "slab", lambda chip: r.slab_core.at[mine, chip], r.slab_sum)

    far_first(both(lambda chip: to_core("br", chip).start()))
    early()
    for copy in local:
        copy.wait()
    far_first(both(lambda chip: to_core("out_slab", chip).start()))
    far_first(branch.to_beside)
    far_first(heads.to_beside)
    middle(True)
    for c in others:
        far_first(both(lambda chip: slab_to_core(c, chip).start()))
    on_distance(lines - 1, both(cycle_sums))
    middle(False)
    far_first(both(lambda chip: slab_to_core(mine, chip).start()))
    for by in range(lines - 2, -1, -1):
        on_distance(by, both(cycle_sums))
    on_distance(lines - 1, branch.along)
    late()
    sums_to_core.start()
    for c in others:
        swap("da", 0, c, mine).start()
    sums_to_core.wait_recv()
    r.stage[0] = r.sums[...] + r.sums_core[...]
    sums_to_side.start()

    for by in range(lines - 1, -1, -1):
        if by + 1 < lines:
            on_distance(by, branch.along)
        on_distance(by, slabs.to_beside)
        on_distance(by, heads.along)
        if by + 1 < lines:
            on_distance(by + 1, slabs.along)
        if by == min(1, lines - 1):
            sums_to_side.wait_recv()
            r.stage[1] = r.stage[0] + r.sums_side[...]
            r.sums_line[line] = r.stage[1]
            for away in range(1, lines):
                sums_to_line((line + away) % lines, line).start()
    thin = r.out_half.shape[1]
    for c in range(cycle):
        piece = r.out_sum[:, c * thin : (c + 1) * thin]

        @pl.when(c == mine)
        def _():
            r.out_half[...] = piece

        @pl.when(c != mine)
        def _():
            r.give[c] = piece.astype(r.give.dtype)
            swap("give", 1, c, mine).start()

    for away in range(1, lines):
        source = (line + away) % lines
        sums_to_line(source, source).wait_recv()
    total = r.sums_line[0]
    for by in range(1, lines):
        total = total + r.sums_line[by]
    r.stage[2] = total
    r.sums_cycle[mine] = total
    for c in others:
        sums_to_cycle(c, mine).start()
    r.out_t[...] = (r.hidden[...] + r.branch_sum[...] + r.vec[7:8, :]).astype(r.out_t.dtype).T
    grad = r.da_own[...]
    for c in others:
        swap("da", 0, c, c).wait_recv()
        grad = grad + r.da_all[c].astype(jnp.float32)
    gain, bias = r.vec[0:1, :], r.vec[1:2, :]
    _, normed, inverse = norm_parts(r.x[mine].astype(jnp.float32), gain, bias)
    r.ing_t[...] = (r.dh[...] + norm_back(grad, normed, inverse, gain)).T
    on_distance(0, slabs.along)
    for c in others:
        swap("give", 1, c, c).wait_recv()
        r.out_half[...] += r.give_all[c].astype(jnp.float32)
        sums_to_cycle(c, c).wait_recv()
    total = r.sums_cycle[0]
    for c in range(1, cycle):
        total = total + r.sums_cycle[c]
    r.total[...] = total

    sums_to_core.wait_send()
    sums_to_side.wait_send()
    for c in others:
        sums_to_cycle(c, mine).wait_send()
        swap("da", 0, c, mine).wait_send()
        swap("give", 1, c, mine).wait_send()
    for away in range(1, lines):
        sums_to_line((line + away) % lines, line).wait_send()
    branch.finish()
    heads.finish()
    slabs.finish()
    for chip in chips:
        to_core("br", chip).wait_send()
        to_core("out_slab", chip).wait_send()
        slab_to_core(mine, chip).wait_send()
        for c in others:
            slab_to_core(c, chip).wait_send()
            slab_to_cycle(c, chip, mine).wait_send()


SETTLE_OUTS = ["out_t", "ing_t", "slab_sum", "out_half", "total"]
SETTLE_KEPT = [
    "slab_core", "slab_cycle", "slab_lanes", "br_own", "br_core", "br_lanes", "out_slab_core",
    "out_slab_lanes", "out_sum", "branch_sum", "da_all", "give", "give_all", "stage", "sums_core",
    "sums_side", "sums_line", "sums_cycle", "local", "slab_core_sems", "slab_cycle_sems",
    "slab_sems", "br_core_sems", "br_sems", "out_slab_core_sems", "out_slab_sems", "swap_sems",
    "one_sems", "line_sems",
]


def nothing(*_):
    return None


def settle_kernel(names, *refs):
    r = types.SimpleNamespace(**dict(zip(names + SETTLE_OUTS + SETTLE_KEPT, refs)))
    settle_body(r, nothing, nothing, nothing)


def finish_kernel(names, *refs):
    names = names + SETTLE_OUTS + SETTLE_KEPT + BACK_MADE + BACK_KEPT + ["slab", "w", "w_sem"]
    r = types.SimpleNamespace(**dict(zip(names, refs)))
    cycle = r.w.shape[0]
    mine = lax.axis_index("ctx")
    copies = [
        pltpu.make_async_copy(r.w_far.at[c], r.w.at[c], r.w_sem.at[c])
        for c in range(cycle - 1, -1, -1)
    ]
    for copy in copies:
        copy.start()

    def middle(away):
        if away:
            for copy in copies:
                copy.wait()
            back_attend(r)
        for c in range(cycle):

            @pl.when((c != mine) if away else (c == mine))
            def _():
                weigh_columns(r.slab, c, r.normed, r.wide)

    settle_body(r, lambda: back_norm(r), middle, lambda: back_rows(r))


def settle_shapes(cycle, peers, padded, rows, width):
    lines = peers // (CORES * COLUMNS)
    chips = lines * COLUMNS
    tall, thin = 3 * width // cycle, width // cycle
    dma = pltpu.SemaphoreType.DMA
    f32, bf16 = jnp.float32, jnp.bfloat16

    def buffer(dtype, *shape):
        return pltpu.VMEM(shape, dtype)

    outs = [
        ((width, rows), bf16),
        ((width, rows), f32),
        ((padded, tall), f32),
        ((padded, thin), f32),
        ((8, width), f32),
    ]
    kept = [
        buffer(bf16, cycle, chips, padded, tall),
        buffer(bf16, cycle, chips, padded, tall),
        buffer(bf16, 3, lines, padded, tall),
        buffer(bf16, chips, rows, width),
        buffer(bf16, chips, rows, width),
        buffer(bf16, 3, lines, rows, width),
        buffer(bf16, chips, padded, width),
        buffer(bf16, 3, lines, padded, width),
        buffer(f32, padded, width),
        buffer(f32, rows, width),
        buffer(bf16, cycle, rows, width),
        buffer(bf16, cycle, padded, thin),
        buffer(bf16, cycle, padded, thin),
        buffer(f32, 3, 8, width),
        buffer(f32, 8, width),
        buffer(f32, 8, width),
        buffer(f32, lines, 8, width),
        buffer(f32, cycle, 8, width),
        dma((chips,)),
        dma((2, cycle, chips)),
        dma((2, cycle, chips)),
        dma((2, 4, lines)),
        dma((2, chips)),
        dma((2, 4, lines)),
        dma((2, chips)),
        dma((2, 4, lines)),
        dma((2, 3, cycle)),
        dma((2, 2)),
        dma((2, lines)),
    ]
    return outs, kept


def emit_kernel(count, out_t, ing_t, slab_sum, out_half, up_t, down, *refs):
    outs = refs[:count]
    shard = outs[2].shape[0]
    outs[0][...] = out_t[...]
    outs[1][...] = ing_t[...]
    outs[2][...] = slab_sum[:shard, :]
    outs[3][...] = out_half[:shard, :]
    outs[4][...] = up_t[...]
    outs[5][...] = down[...]


def emit(shard, *arrays):
    shapes = [a.shape for a in arrays]
    shapes[2:4] = [(shard, shape[1]) for shape in shapes[2:4]]
    return pl.pallas_call(
        functools.partial(emit_kernel, len(arrays)),
        out_shape=tuple(jax.ShapeDtypeStruct(t, a.dtype) for t, a in zip(shapes, arrays)),
        in_specs=whole_vmem(len(arrays)),
        out_specs=tuple(whole_vmem(len(arrays))),
    )(*arrays)


def finish(arrays, br, collective_id):
    named = dict(zip(BACK_INS, arrays))
    x, w = named["x"], named["w"]
    cycle, rows, width = x.shape
    peers = lax.axis_size("dp")
    padded = w.shape[1] // peers
    outs, kept = settle_shapes(cycle, peers, padded, rows, width)
    made, back_kept = back_shapes(x, padded)
    slab = ((cycle, peers, padded, 3 * width // cycle), jnp.bfloat16)
    params = pltpu.CompilerParams(
        collective_id=collective_id, has_side_effects=True, vmem_limit_bytes=VMEM_LIMIT
    )
    out_shape = tuple(jax.ShapeDtypeStruct(*entry) for entry in outs)
    far = pl.BlockSpec(memory_space=pl.ANY)
    if w.size + slab[0][0] * peers * padded * slab[0][3] < FUSED_LIMIT:
        names = ["w_far" if name == "w" else name for name in BACK_INS] + ["br"]
        specs = ordered(len(arrays))
        specs[BACK_INS.index("w")] = far
        extra = [pltpu.VMEM(*entry) for entry in made + back_kept + [slab]]
        extra += [pltpu.VMEM(w.shape, w.dtype), pltpu.SemaphoreType.DMA((cycle,))]
        return pl.pallas_call(
            functools.partial(finish_kernel, names),
            out_shape=out_shape,
            in_specs=specs + [far],
            out_specs=tuple(whole_vmem(len(outs))),
            scratch_shapes=kept + extra,
            compiler_params=params,
        )(*arrays, br)
    slabs, sums, da, da_own, dh, out_slab = backward(arrays, padded)
    names = ["slab", "sums", "da", "da_own", "dh", "out_slab", "hidden", "x", "vec", "br"]
    return pl.pallas_call(
        functools.partial(settle_kernel, names),
        out_shape=out_shape,
        in_specs=whole_vmem(9) + [far],
        out_specs=tuple(whole_vmem(len(outs))),
        scratch_shapes=kept,
        compiler_params=params,
    )(slabs, sums, da, da_own, dh, out_slab, named["hidden"], x, named["vec"], br)


def per_device(
    block_in,
    cotangent,
    block_order,
    ln1_gain,
    ln1_bias,
    w_qkv,
    b_query,
    b_value,
    w_out,
    b_out,
    ln2_gain,
    ln2_bias,
    w_up,
    b_up,
    w_down,
    b_down,
):
    width, shard = w_out.shape[1], w_out.shape[0]
    peers = lax.axis_size("dp")
    rows_t, upstream_t = block_in[0].T, cotangent[0].T
    vectors = jnp.stack(
        [ln1_gain, ln1_bias, b_query, b_value, b_out, ln2_gain, ln2_bias, b_down]
    )
    count = vectors.shape[0]
    weights, ups, rows = load(vectors, w_qkv, w_out, upstream_t, rows_t, 0)
    vectors = weights[0, :, shard, : count * shard].reshape(peers, count, shard)
    vectors = jnp.transpose(vectors, (1, 0, 2)).reshape(count, width).astype(jnp.float32)
    weights = weights.reshape(weights.shape[0], -1, weights.shape[3])
    spread, normed, q, k, v, o, o_spread, hidden, mid = forward(
        block_order, rows, weights, vectors
    )
    grad_mid, branch, g_up, g_down, g_bias_up = feed_forward(mid, ups, w_up, w_down, b_up, 1)
    arrays = (
        block_order, rows, weights, vectors, spread, normed,
        q, k, v, o, o_spread, hidden, upstream_t, grad_mid,
    )
    block_out_t, grad_input_t, g_qkv, g_out, sums = finish(arrays, branch, 3)
    block_out_t, grad_input_t, g_qkv, g_out, g_up, g_down = emit(
        shard, block_out_t, grad_input_t, g_qkv, g_out, g_up, g_down
    )
    sums = lax.dynamic_slice_in_dim(sums, lax.axis_index("dp") * shard, shard, 1)
    return (
        block_out_t.T[None],
        grad_input_t.T[None],
        sums[0],
        sums[1],
        g_qkv,
        sums[2],
        sums[3],
        g_out,
        sums[4],
        sums[5],
        sums[6],
        g_up.T,
        g_bias_up[0],
        g_down,
        sums[7],
    )


def solution(mesh):
    in_specs = (
        P("dp", "ctx", None),
        P("dp", "ctx", None),
        P(),
        P("dp"),
        P("dp"),
        P("dp", None),
        P("dp"),
        P("dp"),
        P("dp", None),
        P("dp"),
        P("dp"),
        P("dp"),
        P(None, "dp"),
        P("dp"),
        P("dp", None),
        P("dp"),
    )
    out_specs = (
        P("dp", "ctx", None),
        P("dp", "ctx", None),
        P("dp"),
        P("dp"),
        P("dp", "ctx"),
        P("dp"),
        P("dp"),
        P("dp", "ctx"),
        P("dp"),
        P("dp"),
        P("dp"),
        P("ctx", "dp"),
        P("dp"),
        P("dp", "ctx"),
        P("dp"),
    )
    return jax.shard_map(
        per_device, mesh=mesh, in_specs=in_specs, out_specs=out_specs, check_vma=False
    )
```

```python
import functools
import types

import jax
import jax.numpy as jnp
from jax import lax
from jax.experimental import pallas as pl
from jax.experimental.pallas import tpu as pltpu
from jax.sharding import PartitionSpec as P

HD = 64
SCALE = 0.125


def norm_parts(values, gain_values, shift_values):
    average = jnp.mean(values, axis=-1, keepdims=True)
    centered = values - average
    inverse = lax.rsqrt(jnp.mean(centered * centered, axis=-1, keepdims=True) + 1e-05)
    normed = centered * inverse
    return normed * gain_values + shift_values, normed, inverse


def norm_back(upstream, normed, inverse, gain_values):
    scaled = upstream * gain_values
    return inverse * (
        scaled
        - jnp.mean(scaled, axis=-1, keepdims=True)
        - normed * jnp.mean(scaled * normed, axis=-1, keepdims=True)
    )


def contract_first(left, right):
    return lax.dot_general(
        left, right, (((0,), (0,)), ((), ())), preferred_element_type=jnp.float32
    )


def contract_last(left, right):
    return lax.dot_general(
        left, right, (((1,), (1,)), ((), ())), preferred_element_type=jnp.float32
    )


def head_groups(width):
    groups = [(start, 128) for start in range(0, width - width % 128, 128)]
    if width % 128:
        groups.append((width - width % 128, width % 128))
    return groups


def head_masks(lanes):
    if lanes == HD:
        return [None]
    lane = lax.broadcasted_iota(jnp.int32, (1, lanes), 1)
    return [
        jnp.where((lane >= first) & (lane < first + HD), 1.0, 0.0).astype(jnp.bfloat16)
        for first in range(0, lanes, HD)
    ]


def keep(array, mask):
    return array if mask is None else array * mask


MESH = pl.DeviceIdType.MESH
CORES = 2
COLUMNS = 2
VMEM_LIMIT = 63 * 1024 * 1024
UP, DOWN, ACROSS, PARTNER = range(4)
SIDES = ((1, UP), (-1, DOWN))
GROUP = 8
FOLD = 2
FUSED_LIMIT = 9 * 1024 * 1024


def place():
    index = lax.axis_index("dp")
    lines = lax.axis_size("dp") // (CORES * COLUMNS)
    core = index % CORES
    column = (index // CORES) % COLUMNS
    return index // (CORES * COLUMNS), column, core, lines


def device_at(line, column, core):
    return (line * COLUMNS + column) * CORES + core


def on_line(line, lines):
    return (line >= 0) & (line < lines)


def greet():
    line, column, core, lines = place()
    cycle = lax.axis_size("ctx")
    mine = lax.axis_index("ctx")
    barrier = pltpu.get_barrier_semaphore()
    peers = [{"dp": device_at((line + by) % lines, column, core)} for by in range(1, lines)]
    peers += [{"dp": device_at(line, 1 - column, core)}, {"dp": device_at(line, column, 1 - core)}]
    peers += [{"ctx": (mine + by) % cycle} for by in range(1, cycle)]
    for peer in peers:
        pl.semaphore_signal(barrier, inc=1, device_id=peer, device_id_type=MESH)

    def met():
        pl.semaphore_wait(barrier, len(peers))

    return met


def remote(source, landing, send, recv, target):
    return pltpu.make_async_remote_copy(
        src_ref=source,
        dst_ref=landing,
        send_sem=send,
        recv_sem=recv,
        device_id=target,
        device_id_type=MESH,
    )


def fold(ref, values):
    half, width = values.shape[0] // FOLD, values.shape[1]
    for i in range(FOLD):
        part = values[i * half : (i + 1) * half]
        ref[:, i * width : (i + 1) * width] = part.astype(ref.dtype)


def fold_shape(rows, width):
    return rows // FOLD, FOLD * width


def unfold(values):
    width = values.shape[-1] // FOLD
    return [values[..., i * width : (i + 1) * width] for i in range(FOLD)]


def on_distance(by, act):
    line, _, _, lines = place()
    if by == 0:
        act(line, 0)
        return
    for step in (1, -1):

        @pl.when(on_line(line + step * by, lines))
        def _():
            act(line + step * by, step)


def nearest(d):
    line, _, _, lines = place()
    toward = 1 - 2 * ((2 * line) // lines)
    return (line + toward * d + lines) % lines


def gather_stream(own, land, send, recv, balanced):
    line, column, core, lines = place()
    me = device_at(line, column, core)
    beside = device_at(line, 1 - column, core)
    partner = device_at(line, column, 1 - core)

    def push(shard, way, target, source=None):
        source = land(shard) if source is None else source
        remote(source, land(shard), send(way, shard), recv(shard), {"dp": target}).start()

    def arrived(shard):
        buffer = land(shard)
        remote(buffer, buffer, send(PARTNER, shard), recv(shard), {"dp": partner}).wait_recv()

    def sent(shard, way):
        buffer = land(shard)
        remote(buffer, buffer, send(way, shard), recv(shard), {"dp": partner}).wait_send()

    def start():
        push(me, ACROSS, beside, own)
        for step, way in SIDES:

            @pl.when(on_line(line + step, lines))
            def _():
                push(me, way, device_at(line + step, column, core), own)

        push(me, PARTNER, partner, own)

    def crosses(source, act):
        if balanced:

            @pl.when((source != 0) & (source != lines - 1))
            def _():
                act()

        else:
            act()

    def relay(by, seen=None):
        for step, way in SIDES:

            @pl.when(on_line(line - step * by, lines))
            def _():
                shard = device_at(line - step * by, column, core)
                arrived(shard)

                @pl.when(on_line(line + step, lines))
                def _():
                    push(shard, way, device_at(line + step, column, core))

                crosses(line - step * by, lambda: push(shard, ACROSS, beside))
                push(shard, PARTNER, partner)
                if seen is not None:
                    seen(shard)

    def through(source, act):
        if balanced:
            for step, way in SIDES:
                end = 0 if step > 0 else lines - 1

                @pl.when((source == end) & on_line(line + step, lines))
                def _():
                    act(way, device_at(line + step, column, core))

    def cross(source, seen=None):
        shard = device_at(source, 1 - column, core)
        arrived(shard)
        through(source, lambda way, target: push(shard, way, target))
        push(shard, PARTNER, partner)
        if seen is not None:
            seen(shard)

    def finish():
        def visit(source, step):
            shard = device_at(source, column, core)
            far = device_at(source, 1 - column, core)
            sent(shard, PARTNER)
            sent(far, PARTNER)
            if step:
                crosses(source, lambda: sent(shard, ACROSS))
            else:
                sent(shard, ACROSS)
            through(source, lambda way, target: sent(far, way))
            for along, way in SIDES:
                if step in (0, -along):

                    @pl.when(on_line(line + along, lines))
                    def _():
                        sent(shard, way)

        for by in range(lines):
            on_distance(by, visit)

    return types.SimpleNamespace(
        start=start, relay=relay, cross=cross, arrived=arrived, finish=finish
    )


def reduce_stream(have, buffers, send, recv, settle):
    line, column, core, lines = place()
    side_buf, up_buf, down_buf, stash = buffers
    beside = device_at(line, 1 - column, core)

    def landed(buffer, way, slot):
        copy = remote(buffer, buffer, send.at[way, slot], recv.at[way, slot], {"dp": beside})
        copy.wait_recv()
        return buffer[...].astype(jnp.float32)

    def to_beside(target, step):
        chip = target * COLUMNS + 1 - column
        buffer = stash(chip)
        buffer[...] = have(chip).astype(buffer.dtype)
        remote(
            buffer,
            side_buf.at[target],
            send.at[1, target],
            recv.at[1, target],
            {"dp": beside},
        ).start()

    def along(target, step):
        chip = target * COLUMNS + column
        total = have(chip)
        total = total + landed(side_buf.at[target], 1, target)
        if step == 0:
            for by, way, landing in ((1, 2, up_buf), (-1, 3, down_buf)):
                settle_from(total, by, way, landing)
            return
        way, landing = (2, up_buf) if step > 0 else (3, down_buf)
        buffer = stash(chip)
        buffer[...] = total.astype(buffer.dtype)

        @pl.when(on_line(line - step, lines))
        def _():
            more = landed(landing.at[target], way, target)
            buffer[...] = (total + more).astype(buffer.dtype)

        remote(
            buffer,
            landing.at[target],
            send.at[way, target],
            recv.at[way, target],
            {"dp": device_at(line + step, column, core)},
        ).start()

    def settle_from(total, by, way, landing):
        if way == 2:
            settle(total, True)

        @pl.when(on_line(line - by, lines))
        def _():
            settle(landed(landing.at[line], way, line), False)

    def finish():
        def visit(target, step):
            buffer = side_buf.at[target]
            slots = [(1, target)]
            if step:
                slots.append((2 if step > 0 else 3, target))
            for way, slot in slots:
                remote(
                    buffer, buffer, send.at[way, slot], recv.at[way, slot], {"dp": beside}
                ).wait_send()

        for by in range(lines):
            on_distance(by, visit)

    return types.SimpleNamespace(to_beside=to_beside, along=along, finish=finish)


def pack_weights(vec_ref, qkv_ref, out_ref, w_ref, row):
    count, shard = vec_ref.shape
    cycle, padded, size = w_ref.shape
    width = out_ref.shape[1]
    for c in range(cycle):
        first, last = c * size, (c + 1) * size
        split = min(max(3 * width - first, 0), size)
        if split:
            w_ref[c, :shard, :split] = qkv_ref[:, first : first + split]
        if split < size:
            w_ref[c, :shard, split:] = out_ref[:, first + split - 3 * width : last - 3 * width]
    row[...] = jnp.zeros_like(row)
    for i in range(count):
        row[0:1, i * shard : (i + 1) * shard] = vec_ref[i : i + 1, :].astype(jnp.float32)
    for c in range(cycle):
        w_ref[c, shard:padded, :] = row[: padded - shard, :].astype(jnp.bfloat16)


def load_kernel(
    vec_ref, qkv_ref, out_ref, u_t_ref, x_t_ref, w_all, u_all, x_all, w_ref, row, u_ref, x_ref,
    w_send, w_recv, part_send, cycle_send, u_send, u_recv, x_send, x_recv, local,
):
    line, column, core, lines = place()
    cycle = lax.axis_size("ctx")
    mine = lax.axis_index("ctx")
    me = device_at(line, column, core)
    partner = device_at(line, column, 1 - core)
    others = [(mine + by) % cycle for by in range(1, cycle)]
    met = greet()
    pack_weights(vec_ref, qkv_ref, out_ref, w_ref, row)
    x_ref[...] = x_t_ref[...].T
    fold(u_ref, u_t_ref[...].astype(jnp.float32).T)
    met()

    weights = gather_stream(
        w_ref.at[mine],
        lambda shard: w_all.at[mine, shard],
        lambda way, shard: w_send.at[way, shard],
        lambda shard: w_recv.at[mine, shard],
        False,
    )
    ups = gather_stream(
        u_ref,
        lambda shard: u_all.at[shard],
        lambda way, shard: u_send.at[way, shard],
        lambda shard: u_recv.at[shard],
        True,
    )

    def part(c, shard, send, target, source=None):
        landing = w_all.at[c, shard]
        source = landing if source is None else source
        return remote(source, landing, send, w_recv.at[c, shard], target)

    def to_cycle(shard):
        for c in others:
            part(mine, shard, cycle_send.at[c, shard], {"ctx": c}).start()

    def from_cycle(shard):
        for c in others:
            copy = part(c, shard, part_send.at[c, shard], {"dp": partner})
            copy.wait_recv()
            copy.start()

    def swap(c, source):
        return remote(x_ref, x_all.at[source], x_send.at[c], x_recv.at[source], {"ctx": c})

    copies = [
        pltpu.make_async_copy(w_ref.at[c], w_all.at[c, me], local.at[c]) for c in range(cycle)
    ]
    copies.append(pltpu.make_async_copy(u_ref, u_all.at[me], local.at[cycle]))
    copies.append(pltpu.make_async_copy(x_ref, x_all.at[mine], local.at[cycle + 1]))
    weights.start()
    for c in others:
        swap(c, mine).start()
    ups.start()
    for c in others:
        part(c, me, part_send.at[c, me], {"dp": partner}, w_ref.at[c]).start()
    for copy in copies:
        copy.start()

    for d in range(lines):
        if d + 1 < lines:
            weights.relay(d + 1, to_cycle)
            ups.relay(d + 1)
        on_distance(d, lambda source, step: weights.cross(source, to_cycle))
        on_distance(d, lambda source, step: ups.cross(source))
        if d > 0:
            on_distance(d, lambda source, step: from_cycle(device_at(source, column, core)))
            on_distance(d - 1, lambda source, step: from_cycle(device_at(source, 1 - column, core)))
    on_distance(
        lines - 1, lambda source, step: from_cycle(device_at(source, 1 - column, core))
    )
    for chip in range(lines * COLUMNS):
        shard = chip * CORES + 1 - core
        weights.arrived(shard)
        ups.arrived(shard)
        for c in others:
            part(c, shard, part_send.at[c, shard], {"dp": partner}).wait_recv()
    weights.finish()
    ups.finish()
    for c in others:
        swap(c, c).wait_recv()
        swap(c, mine).wait_send()
        part(c, me, part_send.at[c, me], {"dp": partner}).wait_send()
    for d in range(lines):
        for across in (column, 1 - column):
            if d == 0 and across is column:
                continue
            shard = device_at(nearest(d), across, core)
            for c in others:
                part(c, shard, part_send.at[c, shard], {"dp": partner}).wait_send()
                part(mine, shard, cycle_send.at[c, shard], {"ctx": c}).wait_send()
    for copy in copies:
        copy.wait()


def load(vectors, w_qkv, w_out, ups_t, rows_t, collective_id):
    peers = lax.axis_size("dp")
    cycle = lax.axis_size("ctx")
    shard = w_out.shape[0]
    padded = (shard // GROUP + 1) * GROUP
    size = 4 * w_out.shape[1] // cycle
    block = ups_t.shape[::-1]
    bf16 = jnp.bfloat16
    dma = pltpu.SemaphoreType.DMA
    return pl.pallas_call(
        load_kernel,
        out_shape=(
            jax.ShapeDtypeStruct((cycle, peers, padded, size), bf16),
            jax.ShapeDtypeStruct((peers,) + fold_shape(*block), bf16),
            jax.ShapeDtypeStruct((cycle,) + block, bf16),
        ),
        in_specs=whole_vmem(5),
        out_specs=tuple([pl.BlockSpec(memory_space=pl.ANY)] * 3),
        scratch_shapes=[
            pltpu.VMEM((cycle, padded, size), bf16),
            pltpu.VMEM((GROUP, size), jnp.float32),
            pltpu.VMEM(fold_shape(*block), bf16),
            pltpu.VMEM(block, bf16),
            dma((4, peers)),
            dma((cycle, peers)),
            dma((cycle, peers)),
            dma((cycle, peers)),
            dma((4, peers)),
            dma((peers,)),
            dma((cycle,)),
            dma((cycle,)),
            dma((cycle + 2,)),
        ],
        compiler_params=pltpu.CompilerParams(collective_id=collective_id, has_side_effects=True),
    )(vectors, w_qkv, w_out, ups_t, rows_t)


def spreader(width, shard, padded):
    source = lax.broadcasted_iota(jnp.int32, (width, 1), 0).astype(jnp.float32)
    block = jnp.floor((source + 0.5) * (1.0 / shard))
    target = source + block * float(padded - shard)
    lanes = lax.broadcasted_iota(jnp.int32, (1, width // shard * padded), 1).astype(jnp.float32)
    return jnp.where(target == lanes, 1.0, 0.0).astype(jnp.bfloat16)


def visible_bias(order_ref, first, rows, keys):
    block = keys // order_ref.shape[0]

    def position(slot):
        where = slot
        for b in range(order_ref.shape[0]):
            inside = (slot >= b * block) & (slot < (b + 1) * block)
            where = jnp.where(inside, (order_ref[b] - b) * block + slot, where)
        return where

    query = position(first + lax.broadcasted_iota(jnp.int32, (rows, 1), 0))
    key = position(lax.broadcasted_iota(jnp.int32, (1, keys), 1))
    return jnp.where(query >= key, 0.0, -1e30)


def parts_over(first, last, size, count):
    return [c for c in range(count) if c * size < last and (c + 1) * size > first]


def forward_kernel(
    order_ref, x_ref, w_ref, vec_ref,
    spread_ref, normed_ref, q_ref, k_ref, v_ref, o_ref, o_spread_ref, h_ref, mid_ref,
    projected,
):
    cycle, rows, width = x_ref.shape
    shard = width // lax.axis_size("dp")
    mine = lax.axis_index("ctx")
    size = w_ref.shape[2]
    padded = w_ref.shape[1] // lax.axis_size("dp")
    spread_ref[...] = spreader(width, shard, padded)
    gain_one, shift_one, bias_q, bias_v, bias_o, gain_two, shift_two = [
        vec_ref[i : i + 1, :] for i in range(7)
    ]

    def project(left, first, last):
        for c in parts_over(first, last, size, cycle):
            projected[:, c * size : (c + 1) * size] = jnp.dot(
                left, w_ref[c], preferred_element_type=jnp.float32
            )

    def visit(c, carry):
        block = pl.ds(pl.multiple_of(c * rows, rows), rows)
        values, _, _ = norm_parts(x_ref[c].astype(jnp.float32), gain_one, shift_one)
        spread = jnp.dot(
            values.astype(jnp.bfloat16), spread_ref[...], preferred_element_type=jnp.float32
        ).astype(jnp.bfloat16)
        normed_ref[block, :] = spread
        project(spread, 0, 3 * width)
        k_ref[block, :] = projected[:, width : 2 * width].astype(jnp.bfloat16)
        v_ref[block, :] = (projected[:, 2 * width : 3 * width] + bias_v).astype(jnp.bfloat16)

        @pl.when(c == mine)
        def _():
            q_ref[...] = (projected[:, :width] + bias_q).astype(jnp.bfloat16)

        return carry

    lax.fori_loop(0, cycle, visit, 0)
    bias = visible_bias(order_ref, mine * rows, rows, cycle * rows)
    for start, lanes in head_groups(width):
        block = slice(start, start + lanes)
        q, k, v = q_ref[:, block], k_ref[:, block], v_ref[:, block]
        total = None
        for mask in head_masks(lanes):
            scores = contract_last(keep(q, mask), k) * SCALE + bias
            largest = jnp.max(scores, axis=-1, keepdims=True)
            exponent = jnp.exp(scores - largest)
            inverse = 1.0 / jnp.sum(exponent, axis=-1, keepdims=True)
            part = jnp.dot(
                exponent.astype(jnp.bfloat16), keep(v, mask), preferred_element_type=jnp.float32
            )
            part = part * inverse
            total = part if total is None else total + part
        o_ref[:, block] = total.astype(jnp.bfloat16)
    o_spread = jnp.dot(
        o_ref[...], spread_ref[...], preferred_element_type=jnp.float32
    ).astype(jnp.bfloat16)
    o_spread_ref[...] = o_spread
    project(o_spread, 3 * width, 4 * width)
    hidden = x_ref[mine].astype(jnp.float32) + projected[:, 3 * width : 4 * width] + bias_o
    h_ref[...] = hidden
    fold(mid_ref, norm_parts(hidden, gain_two, shift_two)[0])


def ordered(count):
    return [pl.BlockSpec(memory_space=pltpu.SMEM)] + whole_vmem(count - 1)


def forward(order, x, w, vectors):
    cycle, rows, width = x.shape
    full = w.shape[1]

    def bf(*shape):
        return jax.ShapeDtypeStruct(shape, jnp.bfloat16)

    return pl.pallas_call(
        forward_kernel,
        out_shape=(
            bf(width, full),
            bf(cycle * rows, full),
            bf(rows, width),
            bf(cycle * rows, width),
            bf(cycle * rows, width),
            bf(rows, width),
            bf(rows, full),
            jax.ShapeDtypeStruct((rows, width), jnp.float32),
            bf(*fold_shape(rows, width)),
        ),
        in_specs=ordered(4),
        out_specs=tuple(whole_vmem(9)),
        scratch_shapes=[pltpu.VMEM((rows, 4 * width), jnp.float32)],
        compiler_params=pltpu.CompilerParams(vmem_limit_bytes=VMEM_LIMIT),
    )(order, x, w, vectors)


def column_sum(values):
    return jnp.sum(values, axis=0, keepdims=True)


def store_owners(grads, ref, padded):
    for s in range(grads.shape[0] // padded):
        ref[s] = grads[s * padded : (s + 1) * padded].astype(ref.dtype)


def weigh_columns(slab_ref, c, normed_ref, wide):
    padded, tall = slab_ref.shape[2:]
    grads = contract_first(normed_ref[...], wide[:, c * tall : (c + 1) * tall])
    store_owners(grads, slab_ref.at[c], padded)


def weigh_kernel(normed_ref, wide_ref, slab_ref):
    for c in range(slab_ref.shape[0]):
        weigh_columns(slab_ref, c, normed_ref, wide_ref)


def back_norm(r):
    rows, width = r.hidden.shape
    gain, shift = r.vec[5:6, :], r.vec[6:7, :]
    _, normed, inverse = norm_parts(r.hidden[...], gain, shift)
    upstream = r.upstream_t[...].T.astype(jnp.float32)
    grad_mid = r.grad_mid[...]
    r.sums[0:2, :] = jnp.zeros((2, width), jnp.float32)
    r.sums[5:6, :] = column_sum(grad_mid * normed)
    r.sums[6:7, :] = column_sum(grad_mid)
    r.sums[7:8, :] = column_sum(upstream)
    grad_hidden = upstream + norm_back(grad_mid, normed, inverse, gain)
    r.dh[...] = grad_hidden
    r.sums[4:5, :] = column_sum(grad_hidden)
    grad_hidden_b = grad_hidden.astype(jnp.bfloat16)
    r.head_wide[...] = jnp.zeros_like(r.head_wide)
    r.head_wide[:, 3 * width : 4 * width] = grad_hidden_b
    grads = contract_first(r.o_spread[...], grad_hidden_b)
    store_owners(grads, r.out_slab, r.out_slab.shape[1])


def back_attend(r):
    cycle, rows, width = r.x.shape
    mine = lax.axis_index("ctx")
    size = r.w.shape[2]
    grad_ctx = None
    for c in parts_over(3 * width, 4 * width, size, cycle):
        more = contract_last(r.head_wide[:, c * size : (c + 1) * size], r.w[c])
        grad_ctx = more if grad_ctx is None else grad_ctx + more
    grad_ctx = contract_last(grad_ctx.astype(jnp.bfloat16), r.spread[...])
    r.do[...] = grad_ctx.astype(jnp.bfloat16)
    r.wide[...] = jnp.zeros_like(r.wide)
    own = pl.ds(pl.multiple_of(mine * rows, rows), rows)
    bias = visible_bias(r.order, mine * rows, rows, cycle * rows)
    for start, lanes in head_groups(width):
        block = slice(start, start + lanes)
        q, k, v = r.q[:, block], r.k[:, block], r.v[:, block]
        do, o = r.do[:, block], r.o[:, block]
        product = do.astype(jnp.float32) * o.astype(jnp.float32)
        dq = dk = dv = None
        for mask in head_masks(lanes):
            q_h, k_h, do_h = keep(q, mask), keep(k, mask), keep(do, mask)
            product_h = product if mask is None else product * mask.astype(jnp.float32)
            delta = jnp.sum(product_h, axis=-1, keepdims=True)
            scores = contract_last(q_h, k) * SCALE + bias
            largest = jnp.max(scores, axis=-1, keepdims=True)
            exponent = jnp.exp(scores - largest)
            p = exponent * (1.0 / jnp.sum(exponent, axis=-1, keepdims=True))
            dp = contract_last(do_h, v)
            ds = (p * (dp - delta)).astype(jnp.bfloat16)
            dv_h = contract_first(p.astype(jnp.bfloat16), do_h)
            dq_h = jnp.dot(ds, k_h, preferred_element_type=jnp.float32)
            dk_h = contract_first(ds, q_h)
            dq = dq_h if dq is None else dq + dq_h
            dk = dk_h if dk is None else dk + dk_h
            dv = dv_h if dv is None else dv + dv_h
        dq = dq * SCALE
        r.wide[own, start : start + lanes] = dq.astype(jnp.bfloat16)
        r.wide[:, width + start : width + start + lanes] = (dk * SCALE).astype(jnp.bfloat16)
        r.wide[:, 2 * width + start : 2 * width + start + lanes] = dv.astype(jnp.bfloat16)
        r.sums[2:3, block] = column_sum(dq)
        r.sums[3:4, block] = column_sum(dv)


def back_rows(r):
    cycle, rows, width = r.x.shape
    mine = lax.axis_index("ctx")
    size = r.w.shape[2]
    gain, shift = r.vec[0:1, :], r.vec[1:2, :]

    def visit(block, carry):
        span = pl.ds(pl.multiple_of(block * rows, rows), rows)
        total = None
        for c in parts_over(0, 3 * width, size, cycle):
            more = contract_last(r.wide[span, c * size : (c + 1) * size], r.w[c])
            total = more if total is None else total + more
        high = total.astype(jnp.bfloat16)
        low = (total - high.astype(jnp.float32)).astype(jnp.bfloat16)
        grad = contract_last(high, r.spread[...]) + contract_last(low, r.spread[...])
        _, normed, _ = norm_parts(r.x[block].astype(jnp.float32), gain, shift)
        r.sums[0:1, :] += column_sum(grad * normed)
        r.sums[1:2, :] += column_sum(grad)
        r.da[block] = grad.astype(jnp.bfloat16)

        @pl.when(block == mine)
        def _():
            r.da_own[...] = grad

        return carry

    lax.fori_loop(0, cycle, visit, 0)


BACK_INS = [
    "order", "x", "w", "vec", "spread", "normed", "q", "k", "v", "o", "o_spread", "hidden",
    "upstream_t", "grad_mid",
]
BACK_MADE = ["sums", "da", "da_own", "dh", "out_slab"]
BACK_KEPT = ["wide", "head_wide", "do"]


def back_kernel(*refs):
    r = types.SimpleNamespace(**dict(zip(BACK_INS + BACK_MADE + BACK_KEPT, refs)))
    back_norm(r)
    back_attend(r)
    back_rows(r)


def back_shapes(x, padded):
    cycle, rows, width = x.shape
    f32, bf16 = jnp.float32, jnp.bfloat16
    made = [
        ((8, width), f32),
        ((cycle, rows, width), bf16),
        ((rows, width), f32),
        ((rows, width), f32),
        ((lax.axis_size("dp"), padded, width), bf16),
    ]
    kept = [((cycle * rows, 4 * width), bf16), ((rows, 4 * width), bf16), ((rows, width), bf16)]
    return made, kept


def backward(arrays, padded):
    named = dict(zip(BACK_INS, arrays))
    cycle, rows, width = named["x"].shape
    made, kept = back_shapes(named["x"], padded)
    params = pltpu.CompilerParams(vmem_limit_bytes=VMEM_LIMIT)
    sums, da, da_own, dh, out_slab, wide = pl.pallas_call(
        back_kernel,
        out_shape=tuple(jax.ShapeDtypeStruct(*entry) for entry in made + kept[:1]),
        in_specs=ordered(len(arrays)),
        out_specs=tuple(whole_vmem(len(made) + 1)),
        scratch_shapes=[pltpu.VMEM(*entry) for entry in kept[1:]],
        compiler_params=params,
    )(*arrays)
    slab = pl.pallas_call(
        weigh_kernel,
        out_shape=jax.ShapeDtypeStruct(
            (cycle, out_slab.shape[0], padded, 3 * width // cycle), jnp.bfloat16
        ),
        in_specs=whole_vmem(2),
        out_specs=whole_vmem(1)[0],
        compiler_params=params,
    )(named["normed"], wide)
    return slab, sums, da, da_own, dh, out_slab


def whole_vmem(count):
    return [pl.BlockSpec(memory_space=pltpu.VMEM)] * count


def ffn_kernel(
    mid_ref, ups_far, w_up_t_ref, w_down_ref, b_up_ref,
    gm_ref, br_far, gup_ref, gdown_ref, gb_ref,
    ups_ref, br_ref, ups_sem, br_sem, mids, parts, acts, grads, up_total, down_total, give, take, bias_part, bias_all,
    core_buf, side_buf, up_buf, down_buf,
    g_send, g_recv, c_send, c_recv, r_send, r_recv, y_send, y_recv, b_send, b_recv,
):
    line, column, core, lines = place()
    rows, width = gm_ref.shape
    cycle = lax.axis_size("ctx")
    mine = lax.axis_index("ctx")
    me = device_at(line, column, core)
    partner = device_at(line, column, 1 - core)
    met = greet()
    ups_copy = pltpu.make_async_copy(ups_far, ups_ref, ups_sem)
    ups_copy.start()
    mids[me] = mid_ref[...]
    met()

    def br_copy(chip):
        pair = pl.ds(chip * CORES, CORES)
        return pltpu.make_async_copy(br_ref.at[pair], br_far.at[pair], br_sem.at[chip])

    def spread(ref, chip):
        pieces = unfold(ref[pl.ds(chip * CORES, CORES)])
        pieces = [piece.reshape(CORES * rows // FOLD, width) for piece in pieces]
        return jnp.concatenate(pieces, axis=0)

    def gather_rows(ref, chip, values):
        half = CORES * rows // FOLD
        for i in range(FOLD):
            piece = values[i * half : (i + 1) * half].astype(ref.dtype)
            piece = piece.reshape(CORES, rows // FOLD, width)
            ref[pl.ds(chip * CORES, CORES), :, i * width : (i + 1) * width] = piece

    gather = gather_stream(
        mid_ref,
        lambda shard: mids.at[shard],
        lambda way, shard: g_send.at[way, shard],
        lambda shard: g_recv.at[shard],
        False,
    )
    gather.start()
    bias_part[...] = jnp.zeros_like(bias_part)

    def to_core(chip):
        return remote(
            parts.at[chip * CORES + 1 - core],
            core_buf.at[chip],
            c_send.at[chip],
            c_recv.at[chip],
            {"dp": partner},
        )

    def feed(chip):
        mid = spread(mids, chip)
        ups = spread(ups_ref, chip)
        pre = contract_last(mid, w_up_t_ref[...]) + b_up_ref[...]
        grad = contract_last(ups, w_down_ref[...])
        half = 0.5 * (1.0 + lax.erf(pre * 0.7071067811865476))
        act = (pre * half).astype(jnp.bfloat16)
        grad = grad * (half + pre * jnp.exp(-0.5 * pre * pre) * 0.3989422804014327)
        bias_part[...] += jnp.sum(grad, axis=0, keepdims=True)
        grad = grad.astype(jnp.bfloat16)
        acts[chip] = act
        grads[chip] = grad
        part = jnp.dot(grad, w_up_t_ref[...], preferred_element_type=jnp.float32)
        gather_rows(parts, chip, part)
        to_core(chip).start()
        branch = jnp.dot(act, w_down_ref[...], preferred_element_type=jnp.float32)
        gather_rows(br_ref, chip, branch)
        br_copy(chip).start()

    def visit(d, carry):
        @pl.when(d + 1 < lines)
        def _():
            gather.relay(d + 1)

        at = nearest(d)
        gather.arrived(device_at(at, column, 1 - core))
        feed(at * COLUMNS + column)
        gather.cross(at)
        gather.arrived(device_at(at, 1 - column, 1 - core))
        feed(at * COLUMNS + 1 - column)
        return carry

    ups_copy.wait()
    lax.fori_loop(0, lines, visit, 0)

    def have(chip):
        to_core(chip).wait_recv()
        return core_buf[chip].astype(jnp.float32) + parts[chip * CORES + core].astype(jnp.float32)

    def settle(total, first):
        half = rows // FOLD
        for i, piece in enumerate(unfold(total)):
            span = slice(i * half, (i + 1) * half)
            gm_ref[span, :] = piece if first else gm_ref[span, :] + piece

    reduce = reduce_stream(
        have,
        (side_buf, up_buf, down_buf, lambda chip: parts.at[chip * CORES + core]),
        r_send,
        r_recv,
        settle,
    )
    for by in range(lines - 1, -1, -1):
        on_distance(by, reduce.to_beside)

    def swap(c, source):
        return remote(give.at[c], take.at[source], y_send.at[c], y_recv.at[source], {"ctx": c})

    def swap_bias(c, source):
        landing = bias_all.at[source]
        return remote(bias_part, landing, b_send.at[c], b_recv.at[source], {"ctx": c})

    bias_all[mine] = bias_part[...]
    others = [(mine + by) % cycle for by in range(1, cycle)]
    for c in others:
        swap_bias(c, mine).start()
    up_total[...] = jnp.zeros_like(up_total)
    down_total[...] = jnp.zeros_like(down_total)

    def weigh(chip, carry):
        up_total[...] += contract_first(grads[chip], spread(mids, chip))
        down_total[...] += contract_first(acts[chip], spread(ups_ref, chip))
        return carry

    lax.fori_loop(0, lines * COLUMNS, weigh, 0)
    size = width // cycle
    for c in range(cycle):
        up_part = up_total[:, c * size : (c + 1) * size]
        down_part = down_total[:, c * size : (c + 1) * size]

        @pl.when(c == mine)
        def _():
            gup_ref[...] = up_part
            gdown_ref[...] = down_part

        @pl.when(c != mine)
        def _():
            give[c, 0] = up_part.astype(give.dtype)
            give[c, 1] = down_part.astype(give.dtype)
            swap(c, mine).start()

    for by in range(lines - 1, -1, -1):
        on_distance(by, reduce.along)
    for c in others:
        swap(c, c).wait_recv()
        gup_ref[...] += take[c, 0].astype(jnp.float32)
        gdown_ref[...] += take[c, 1].astype(jnp.float32)
        swap_bias(c, c).wait_recv()
    total = bias_all[0]
    for c in range(1, cycle):
        total = total + bias_all[c]
    gb_ref[...] = total
    for c in others:
        swap(c, mine).wait_send()
        swap_bias(c, mine).wait_send()
    for chip in range(lines * COLUMNS):
        to_core(chip).wait_send()
        br_copy(chip).wait()
    reduce.finish()
    gather.finish()


def feed_forward(mid, ups, w_up, w_down, b_up, collective_id):
    peers = lax.axis_size("dp")
    cycle = lax.axis_size("ctx")
    lines = peers // (CORES * COLUMNS)
    chips = lines * COLUMNS
    rows, width = mid.shape[0] * FOLD, mid.shape[1] // FOLD
    hidden = w_up.shape[1]
    dma = pltpu.SemaphoreType.DMA
    near = pl.BlockSpec(memory_space=pltpu.VMEM)
    far = pl.BlockSpec(memory_space=pl.ANY)

    def slabs(count):
        return pltpu.VMEM((count,) + mid.shape, jnp.bfloat16)

    return pl.pallas_call(
        ffn_kernel,
        out_shape=(
            jax.ShapeDtypeStruct((rows, width), jnp.float32),
            jax.ShapeDtypeStruct((peers,) + mid.shape, jnp.bfloat16),
            jax.ShapeDtypeStruct((hidden, width // cycle), jnp.float32),
            jax.ShapeDtypeStruct((hidden, width // cycle), jnp.float32),
            jax.ShapeDtypeStruct((1, hidden), jnp.float32),
        ),
        in_specs=[near, far, near, near, near],
        out_specs=(near, far, near, near, near),
        scratch_shapes=[
            slabs(peers),
            slabs(peers),
            dma(()),
            dma((chips,)),
            slabs(peers),
            slabs(peers),
            pltpu.VMEM((chips, CORES * rows, hidden), jnp.bfloat16),
            pltpu.VMEM((chips, CORES * rows, hidden), jnp.bfloat16),
            pltpu.VMEM((hidden, width), jnp.float32),
            pltpu.VMEM((hidden, width), jnp.float32),
            pltpu.VMEM((cycle, 2, hidden, width // cycle), jnp.bfloat16),
            pltpu.VMEM((cycle, 2, hidden, width // cycle), jnp.bfloat16),
            pltpu.VMEM((1, hidden), jnp.float32),
            pltpu.VMEM((cycle, 1, hidden), jnp.float32),
            slabs(chips),
            slabs(lines),
            slabs(lines),
            slabs(lines),
            dma((4, peers)),
            dma((peers,)),
            dma((chips,)),
            dma((chips,)),
            dma((4, lines)),
            dma((4, lines)),
            dma((cycle,)),
            dma((cycle,)),
            dma((cycle,)),
            dma((cycle,)),
        ],
        compiler_params=pltpu.CompilerParams(
            collective_id=collective_id, has_side_effects=True, vmem_limit_bytes=VMEM_LIMIT
        ),
    )(mid, ups, w_up.T, w_down, b_up.astype(jnp.float32)[None, :])


def settle_body(r, early, middle, late):
    line, column, core, lines = place()
    rows, width = r.dh.shape
    cycle = lax.axis_size("ctx")
    mine = lax.axis_index("ctx")
    beside = device_at(line, 1 - column, core)
    partner = device_at(line, column, 1 - core)
    others = [(mine + by) % cycle for by in range(1, cycle)]
    chips = range(lines * COLUMNS)
    local = [
        pltpu.make_async_copy(
            r.br.at[chip * CORES + core], r.br_own.at[chip], r.local.at[chip]
        )
        for chip in chips
    ]
    met = greet()
    for copy in local:
        copy.start()
    met()

    def to_core(name, chip):
        source = getattr(r, name)
        sems = getattr(r, name + "_core_sems")
        return remote(
            source.at[chip * CORES + 1 - core],
            getattr(r, name + "_core").at[chip],
            sems.at[0, chip],
            sems.at[1, chip],
            {"dp": partner},
        )

    def slab_to_core(c, chip):
        return remote(
            r.slab.at[c, chip * CORES + 1 - core],
            r.slab_core.at[c, chip],
            r.slab_core_sems.at[0, c, chip],
            r.slab_core_sems.at[1, c, chip],
            {"dp": partner},
        )

    def slab_to_cycle(c, chip, source):
        return remote(
            r.slab_core.at[c, chip],
            r.slab_cycle.at[source, chip],
            r.slab_cycle_sems.at[0, c, chip],
            r.slab_cycle_sems.at[1, source, chip],
            {"ctx": c},
        )

    def swap(name, slot, c, source):
        sems = r.swap_sems
        return remote(
            getattr(r, name).at[c],
            getattr(r, name + "_all").at[source],
            sems.at[0, slot, c],
            sems.at[1, slot, source],
            {"ctx": c},
        )

    def both(act):
        def visit(target, step):
            act(target * COLUMNS + 1 - column)
            act(target * COLUMNS + column)

        return visit

    def far_first(act):
        for by in range(lines - 1, -1, -1):
            on_distance(by, act)

    one = r.one_sems
    sums_to_core = remote(r.sums, r.sums_core, one.at[0, 0], one.at[1, 0], {"dp": partner})
    sums_to_side = remote(r.stage.at[0], r.sums_side, one.at[0, 1], one.at[1, 1], {"dp": beside})

    def sums_to_line(to, source):
        return remote(
            r.stage.at[1],
            r.sums_line.at[source],
            r.line_sems.at[0, to],
            r.line_sems.at[1, source],
            {"dp": device_at(to, column, core)},
        )

    def sums_to_cycle(c, source):
        return remote(
            r.stage.at[2],
            r.sums_cycle.at[source],
            r.swap_sems.at[0, 2, c],
            r.swap_sems.at[1, 2, source],
            {"ctx": c},
        )

    def cycle_sums(chip):
        for c in others:
            slab_to_core(c, chip).wait_recv()
            total = r.slab_core[c, chip].astype(jnp.float32)
            total = total + r.slab[c, chip * CORES + core].astype(jnp.float32)
            r.slab_core[c, chip] = total.astype(r.slab_core.dtype)
            slab_to_cycle(c, chip, mine).start()

    def br_have(chip):
        to_core("br", chip).wait_recv()
        return r.br_core[chip].astype(jnp.float32) + r.br_own[chip].astype(jnp.float32)

    def out_have(chip):
        to_core("out_slab", chip).wait_recv()
        own = r.out_slab[chip * CORES + core].astype(jnp.float32)
        return r.out_slab_core[chip].astype(jnp.float32) + own

    def slab_have(chip):
        slab_to_core(mine, chip).wait_recv()
        total = r.slab_core[mine, chip].astype(jnp.float32)
        total = total + r.slab[mine, chip * CORES + core].astype(jnp.float32)
        for c in others:
            slab_to_cycle(c, chip, c).wait_recv()
            total = total + r.slab_cycle[c, chip].astype(jnp.float32)
        return total

    def into(ref):
        def settle(total, first):
            ref[...] = total if first else ref[...] + total

        return settle

    def stream(have, name, stash, ref):
        sems = getattr(r, name + "_sems")
        lanes = [getattr(r, name + "_lanes").at[i] for i in range(3)]
        return reduce_stream(have, (*lanes, stash), sems.at[0], sems.at[1], into(ref))

    branch = stream(br_have, "br", lambda chip: r.br_own.at[chip], r.branch_sum)
    heads = stream(out_have, "out_slab", lambda chip: r.out_slab_core.at[chip], r.out_sum)
    slabs = stream(slab_have, "slab", lambda chip: r.slab_core.at[mine, chip], r.slab_sum)

    for across in (1 - column, column):
        far_first(lambda target, step: to_core("br", target * COLUMNS + across).start())
    early()
    for copy in local:
        copy.wait()
    far_first(both(lambda chip: to_core("out_slab", chip).start()))
    far_first(branch.to_beside)
    middle(True)
    for c in others:
        far_first(both(lambda chip: slab_to_core(c, chip).start()))
    on_distance(lines - 1, both(cycle_sums))
    far_first(heads.to_beside)
    middle(False)
    far_first(both(lambda chip: slab_to_core(mine, chip).start()))
    for by in range(lines - 2, -1, -1):
        on_distance(by, both(cycle_sums))
    on_distance(lines - 1, branch.along)
    late()
    sums_to_core.start()
    for c in others:
        swap("da", 0, c, mine).start()
    sums_to_core.wait_recv()
    r.stage[0] = r.sums[...] + r.sums_core[...]
    sums_to_side.start()

    for by in range(lines - 1, -1, -1):
        if by + 1 < lines:
            on_distance(by, branch.along)
        on_distance(by, slabs.to_beside)
        on_distance(by, heads.along)
        if by + 1 < lines:
            on_distance(by + 1, slabs.along)
        if by == min(1, lines - 1):
            sums_to_side.wait_recv()
            r.stage[1] = r.stage[0] + r.sums_side[...]
            r.sums_line[line] = r.stage[1]
            for away in range(1, lines):
                sums_to_line((line + away) % lines, line).start()
    thin = r.out_half.shape[1]
    for c in range(cycle):
        piece = r.out_sum[:, c * thin : (c + 1) * thin]

        @pl.when(c == mine)
        def _():
            r.out_half[...] = piece

        @pl.when(c != mine)
        def _():
            r.give[c] = piece.astype(r.give.dtype)
            swap("give", 1, c, mine).start()

    for away in range(1, lines):
        source = (line + away) % lines
        sums_to_line(source, source).wait_recv()
    total = r.sums_line[0]
    for by in range(1, lines):
        total = total + r.sums_line[by]
    r.stage[2] = total
    r.sums_cycle[mine] = total
    for c in others:
        sums_to_cycle(c, mine).start()
    branch_rows = jnp.concatenate(unfold(r.branch_sum[...]), axis=0)
    r.out_t[...] = (r.hidden[...] + branch_rows + r.vec[7:8, :]).astype(r.out_t.dtype).T
    grad = r.da_own[...]
    for c in others:
        swap("da", 0, c, c).wait_recv()
        grad = grad + r.da_all[c].astype(jnp.float32)
    gain, bias = r.vec[0:1, :], r.vec[1:2, :]
    _, normed, inverse = norm_parts(r.x[mine].astype(jnp.float32), gain, bias)
    r.ing_t[...] = (r.dh[...] + norm_back(grad, normed, inverse, gain)).T
    on_distance(0, slabs.along)
    for c in others:
        swap("give", 1, c, c).wait_recv()
        r.out_half[...] += r.give_all[c].astype(jnp.float32)
        sums_to_cycle(c, c).wait_recv()
    total = r.sums_cycle[0]
    for c in range(1, cycle):
        total = total + r.sums_cycle[c]
    r.total[...] = total

    sums_to_core.wait_send()
    sums_to_side.wait_send()
    for c in others:
        sums_to_cycle(c, mine).wait_send()
        swap("da", 0, c, mine).wait_send()
        swap("give", 1, c, mine).wait_send()
    for away in range(1, lines):
        sums_to_line((line + away) % lines, line).wait_send()
    branch.finish()
    heads.finish()
    slabs.finish()
    for chip in chips:
        to_core("br", chip).wait_send()
        to_core("out_slab", chip).wait_send()
        slab_to_core(mine, chip).wait_send()
        for c in others:
            slab_to_core(c, chip).wait_send()
            slab_to_cycle(c, chip, mine).wait_send()


SETTLE_OUTS = ["out_t", "ing_t", "slab_sum", "out_half", "total"]
SETTLE_KEPT = [
    "slab_core", "slab_cycle", "slab_lanes", "br_own", "br_core", "br_lanes", "out_slab_core",
    "out_slab_lanes", "out_sum", "branch_sum", "da_all", "give", "give_all", "stage", "sums_core",
    "sums_side", "sums_line", "sums_cycle", "local", "slab_core_sems", "slab_cycle_sems",
    "slab_sems", "br_core_sems", "br_sems", "out_slab_core_sems", "out_slab_sems", "swap_sems",
    "one_sems", "line_sems",
]


def nothing(*_):
    return None


def settle_kernel(names, *refs):
    r = types.SimpleNamespace(**dict(zip(names + SETTLE_OUTS + SETTLE_KEPT, refs)))
    settle_body(r, nothing, nothing, nothing)


def finish_kernel(names, *refs):
    names = names + SETTLE_OUTS + SETTLE_KEPT + BACK_MADE + BACK_KEPT + ["slab", "w", "w_sem"]
    r = types.SimpleNamespace(**dict(zip(names, refs)))
    cycle = r.w.shape[0]
    mine = lax.axis_index("ctx")
    copies = [
        pltpu.make_async_copy(r.w_far.at[c], r.w.at[c], r.w_sem.at[c])
        for c in range(cycle - 1, -1, -1)
    ]
    for copy in copies:
        copy.start()

    def middle(away):
        if away:
            for copy in copies:
                copy.wait()
            back_attend(r)
        for c in range(cycle):

            @pl.when((c != mine) if away else (c == mine))
            def _():
                weigh_columns(r.slab, c, r.normed, r.wide)

    settle_body(r, lambda: back_norm(r), middle, lambda: back_rows(r))


def settle_shapes(cycle, peers, padded, rows, width):
    lines = peers // (CORES * COLUMNS)
    chips = lines * COLUMNS
    tall, thin = 3 * width // cycle, width // cycle
    folded = fold_shape(rows, width)
    dma = pltpu.SemaphoreType.DMA
    f32, bf16 = jnp.float32, jnp.bfloat16

    def buffer(dtype, *shape):
        return pltpu.VMEM(shape, dtype)

    outs = [
        ((width, rows), bf16),
        ((width, rows), f32),
        ((padded, tall), f32),
        ((padded, thin), f32),
        ((8, width), f32),
    ]
    kept = [
        buffer(bf16, cycle, chips, padded, tall),
        buffer(bf16, cycle, chips, padded, tall),
        buffer(bf16, 3, lines, padded, tall),
        buffer(bf16, chips, *folded),
        buffer(bf16, chips, *folded),
        buffer(bf16, 3, lines, *folded),
        buffer(bf16, chips, padded, width),
        buffer(bf16, 3, lines, padded, width),
        buffer(f32, padded, width),
        buffer(f32, *folded),
        buffer(bf16, cycle, rows, width),
        buffer(bf16, cycle, padded, thin),
        buffer(bf16, cycle, padded, thin),
        buffer(f32, 3, 8, width),
        buffer(f32, 8, width),
        buffer(f32, 8, width),
        buffer(f32, lines, 8, width),
        buffer(f32, cycle, 8, width),
        dma((chips,)),
        dma((2, cycle, chips)),
        dma((2, cycle, chips)),
        dma((2, 4, lines)),
        dma((2, chips)),
        dma((2, 4, lines)),
        dma((2, chips)),
        dma((2, 4, lines)),
        dma((2, 3, cycle)),
        dma((2, 2)),
        dma((2, lines)),
    ]
    return outs, kept


def emit_kernel(count, out_t, ing_t, slab_sum, out_half, up_t, down, *refs):
    outs = refs[:count]
    shard = outs[2].shape[0]
    outs[0][...] = out_t[...]
    outs[1][...] = ing_t[...]
    outs[2][...] = slab_sum[:shard, :]
    outs[3][...] = out_half[:shard, :]
    outs[4][...] = up_t[...]
    outs[5][...] = down[...]


def emit(shard, *arrays):
    shapes = [a.shape for a in arrays]
    shapes[2:4] = [(shard, shape[1]) for shape in shapes[2:4]]
    return pl.pallas_call(
        functools.partial(emit_kernel, len(arrays)),
        out_shape=tuple(jax.ShapeDtypeStruct(t, a.dtype) for t, a in zip(shapes, arrays)),
        in_specs=whole_vmem(len(arrays)),
        out_specs=tuple(whole_vmem(len(arrays))),
    )(*arrays)


def finish(arrays, br, collective_id):
    named = dict(zip(BACK_INS, arrays))
    x, w = named["x"], named["w"]
    cycle, rows, width = x.shape
    peers = lax.axis_size("dp")
    padded = w.shape[1] // peers
    outs, kept = settle_shapes(cycle, peers, padded, rows, width)
    made, back_kept = back_shapes(x, padded)
    slab = ((cycle, peers, padded, 3 * width // cycle), jnp.bfloat16)
    params = pltpu.CompilerParams(
        collective_id=collective_id, has_side_effects=True, vmem_limit_bytes=VMEM_LIMIT
    )
    out_shape = tuple(jax.ShapeDtypeStruct(*entry) for entry in outs)
    far = pl.BlockSpec(memory_space=pl.ANY)
    if w.size + slab[0][0] * peers * padded * slab[0][3] < FUSED_LIMIT:
        names = ["w_far" if name == "w" else name for name in BACK_INS] + ["br"]
        specs = ordered(len(arrays))
        specs[BACK_INS.index("w")] = far
        extra = [pltpu.VMEM(*entry) for entry in made + back_kept + [slab]]
        extra += [pltpu.VMEM(w.shape, w.dtype), pltpu.SemaphoreType.DMA((cycle,))]
        return pl.pallas_call(
            functools.partial(finish_kernel, names),
            out_shape=out_shape,
            in_specs=specs + [far],
            out_specs=tuple(whole_vmem(len(outs))),
            scratch_shapes=kept + extra,
            compiler_params=params,
        )(*arrays, br)
    slabs, sums, da, da_own, dh, out_slab = backward(arrays, padded)
    names = ["slab", "sums", "da", "da_own", "dh", "out_slab", "hidden", "x", "vec", "br"]
    return pl.pallas_call(
        functools.partial(settle_kernel, names),
        out_shape=out_shape,
        in_specs=whole_vmem(9) + [far],
        out_specs=tuple(whole_vmem(len(outs))),
        scratch_shapes=kept,
        compiler_params=params,
    )(slabs, sums, da, da_own, dh, out_slab, named["hidden"], x, named["vec"], br)


def per_device(
    block_in,
    cotangent,
    block_order,
    ln1_gain,
    ln1_bias,
    w_qkv,
    b_query,
    b_value,
    w_out,
    b_out,
    ln2_gain,
    ln2_bias,
    w_up,
    b_up,
    w_down,
    b_down,
):
    width, shard = w_out.shape[1], w_out.shape[0]
    peers = lax.axis_size("dp")
    rows_t, upstream_t = block_in[0].T, cotangent[0].T
    vectors = jnp.stack(
        [ln1_gain, ln1_bias, b_query, b_value, b_out, ln2_gain, ln2_bias, b_down]
    )
    count = vectors.shape[0]
    weights, ups, rows = load(vectors, w_qkv, w_out, upstream_t, rows_t, 0)
    vectors = weights[0, :, shard, : count * shard].reshape(peers, count, shard)
    vectors = jnp.transpose(vectors, (1, 0, 2)).reshape(count, width).astype(jnp.float32)
    weights = weights.reshape(weights.shape[0], -1, weights.shape[3])
    spread, normed, q, k, v, o, o_spread, hidden, mid = forward(
        block_order, rows, weights, vectors
    )
    grad_mid, branch, g_up, g_down, g_bias_up = feed_forward(mid, ups, w_up, w_down, b_up, 1)
    arrays = (
        block_order, rows, weights, vectors, spread, normed,
        q, k, v, o, o_spread, hidden, upstream_t, grad_mid,
    )
    block_out_t, grad_input_t, g_qkv, g_out, sums = finish(arrays, branch, 3)
    block_out_t, grad_input_t, g_qkv, g_out, g_up, g_down = emit(
        shard, block_out_t, grad_input_t, g_qkv, g_out, g_up, g_down
    )
    sums = lax.dynamic_slice_in_dim(sums, lax.axis_index("dp") * shard, shard, 1)
    return (
        block_out_t.T[None],
        grad_input_t.T[None],
        sums[0],
        sums[1],
        g_qkv,
        sums[2],
        sums[3],
        g_out,
        sums[4],
        sums[5],
        sums[6],
        g_up.T,
        g_bias_up[0],
        g_down,
        sums[7],
    )


def solution(mesh):
    in_specs = (
        P("dp", "ctx", None),
        P("dp", "ctx", None),
        P(),
        P("dp"),
        P("dp"),
        P("dp", None),
        P("dp"),
        P("dp"),
        P("dp", None),
        P("dp"),
        P("dp"),
        P("dp"),
        P(None, "dp"),
        P("dp"),
        P("dp", None),
        P("dp"),
    )
    out_specs = (
        P("dp", "ctx", None),
        P("dp", "ctx", None),
        P("dp"),
        P("dp"),
        P("dp", "ctx"),
        P("dp"),
        P("dp"),
        P("dp", "ctx"),
        P("dp"),
        P("dp"),
        P("dp"),
        P("ctx", "dp"),
        P("dp"),
        P("dp", "ctx"),
        P("dp"),
    )
    return jax.shard_map(
        per_device, mesh=mesh, in_specs=in_specs, out_specs=out_specs, check_vma=False
    )
```

```python
import functools
import types

import jax
import jax.numpy as jnp
from jax import lax
from jax.experimental import pallas as pl
from jax.experimental.pallas import tpu as pltpu
from jax.sharding import PartitionSpec as P

HD = 64
SCALE = 0.125


def norm_parts(values, gain_values, shift_values):
    average = jnp.mean(values, axis=-1, keepdims=True)
    centered = values - average
    inverse = lax.rsqrt(jnp.mean(centered * centered, axis=-1, keepdims=True) + 1e-05)
    normed = centered * inverse
    return normed * gain_values + shift_values, normed, inverse


def norm_back(upstream, normed, inverse, gain_values):
    scaled = upstream * gain_values
    return inverse * (
        scaled
        - jnp.mean(scaled, axis=-1, keepdims=True)
        - normed * jnp.mean(scaled * normed, axis=-1, keepdims=True)
    )


def contract_first(left, right):
    return lax.dot_general(
        left, right, (((0,), (0,)), ((), ())), preferred_element_type=jnp.float32
    )


def contract_last(left, right):
    return lax.dot_general(
        left, right, (((1,), (1,)), ((), ())), preferred_element_type=jnp.float32
    )


def head_groups(width):
    groups = [(start, 128) for start in range(0, width - width % 128, 128)]
    if width % 128:
        groups.append((width - width % 128, width % 128))
    return groups


def head_masks(lanes):
    if lanes == HD:
        return [None]
    lane = lax.broadcasted_iota(jnp.int32, (1, lanes), 1)
    return [
        jnp.where((lane >= first) & (lane < first + HD), 1.0, 0.0).astype(jnp.bfloat16)
        for first in range(0, lanes, HD)
    ]


def keep(array, mask):
    return array if mask is None else array * mask


MESH = pl.DeviceIdType.MESH
CORES = 2
COLUMNS = 2
VMEM_LIMIT = 63 * 1024 * 1024
UP, DOWN, ACROSS, PARTNER = range(4)
SIDES = ((1, UP), (-1, DOWN))
GROUP = 8
FOLD = 2
FUSED_LIMIT = 9 * 1024 * 1024


def place():
    index = lax.axis_index("dp")
    lines = lax.axis_size("dp") // (CORES * COLUMNS)
    core = index % CORES
    column = (index // CORES) % COLUMNS
    return index // (CORES * COLUMNS), column, core, lines


def device_at(line, column, core):
    return (line * COLUMNS + column) * CORES + core


def on_line(line, lines):
    return (line >= 0) & (line < lines)


def greet():
    line, column, core, lines = place()
    cycle = lax.axis_size("ctx")
    mine = lax.axis_index("ctx")
    barrier = pltpu.get_barrier_semaphore()
    peers = [{"dp": device_at((line + by) % lines, column, core)} for by in range(1, lines)]
    peers += [{"dp": device_at(line, 1 - column, core)}, {"dp": device_at(line, column, 1 - core)}]
    peers += [{"ctx": (mine + by) % cycle} for by in range(1, cycle)]
    for peer in peers:
        pl.semaphore_signal(barrier, inc=1, device_id=peer, device_id_type=MESH)

    def met():
        pl.semaphore_wait(barrier, len(peers))

    return met


def remote(source, landing, send, recv, target):
    return pltpu.make_async_remote_copy(
        src_ref=source,
        dst_ref=landing,
        send_sem=send,
        recv_sem=recv,
        device_id=target,
        device_id_type=MESH,
    )


def fold(ref, values):
    half, width = values.shape[0] // FOLD, values.shape[1]
    for i in range(FOLD):
        part = values[i * half : (i + 1) * half]
        ref[:, i * width : (i + 1) * width] = part.astype(ref.dtype)


def fold_shape(rows, width):
    return rows // FOLD, FOLD * width


def unfold(values):
    width = values.shape[-1] // FOLD
    return [values[..., i * width : (i + 1) * width] for i in range(FOLD)]


def on_distance(by, act):
    line, _, _, lines = place()
    if by == 0:
        act(line, 0)
        return
    for step in (1, -1):

        @pl.when(on_line(line + step * by, lines))
        def _():
            act(line + step * by, step)


def nearest(d):
    line, _, _, lines = place()
    toward = 1 - 2 * ((2 * line) // lines)
    return (line + toward * d + lines) % lines


def gather_stream(own, land, send, recv, balanced):
    line, column, core, lines = place()
    me = device_at(line, column, core)
    beside = device_at(line, 1 - column, core)
    partner = device_at(line, column, 1 - core)

    def push(shard, way, target, source=None):
        source = land(shard) if source is None else source
        remote(source, land(shard), send(way, shard), recv(shard), {"dp": target}).start()

    def arrived(shard):
        buffer = land(shard)
        remote(buffer, buffer, send(PARTNER, shard), recv(shard), {"dp": partner}).wait_recv()

    def sent(shard, way):
        buffer = land(shard)
        remote(buffer, buffer, send(way, shard), recv(shard), {"dp": partner}).wait_send()

    def start():
        push(me, ACROSS, beside, own)
        for step, way in SIDES:

            @pl.when(on_line(line + step, lines))
            def _():
                push(me, way, device_at(line + step, column, core), own)

        push(me, PARTNER, partner, own)

    def crosses(source, act):
        if balanced:

            @pl.when((source != 0) & (source != lines - 1))
            def _():
                act()

        else:
            act()

    def relay(by, seen=None):
        for step, way in SIDES:

            @pl.when(on_line(line - step * by, lines))
            def _():
                shard = device_at(line - step * by, column, core)
                arrived(shard)

                @pl.when(on_line(line + step, lines))
                def _():
                    push(shard, way, device_at(line + step, column, core))

                crosses(line - step * by, lambda: push(shard, ACROSS, beside))
                push(shard, PARTNER, partner)
                if seen is not None:
                    seen(shard)

    def through(source, act):
        if balanced:
            for step, way in SIDES:
                end = 0 if step > 0 else lines - 1

                @pl.when((source == end) & on_line(line + step, lines))
                def _():
                    act(way, device_at(line + step, column, core))

    def cross(source, seen=None):
        shard = device_at(source, 1 - column, core)
        arrived(shard)
        through(source, lambda way, target: push(shard, way, target))
        push(shard, PARTNER, partner)
        if seen is not None:
            seen(shard)

    def finish():
        def visit(source, step):
            shard = device_at(source, column, core)
            far = device_at(source, 1 - column, core)
            sent(shard, PARTNER)
            sent(far, PARTNER)
            if step:
                crosses(source, lambda: sent(shard, ACROSS))
            else:
                sent(shard, ACROSS)
            through(source, lambda way, target: sent(far, way))
            for along, way in SIDES:
                if step in (0, -along):

                    @pl.when(on_line(line + along, lines))
                    def _():
                        sent(shard, way)

        for by in range(lines):
            on_distance(by, visit)

    return types.SimpleNamespace(
        start=start, relay=relay, cross=cross, arrived=arrived, finish=finish
    )


def reduce_stream(have, buffers, send, recv, settle):
    line, column, core, lines = place()
    side_buf, up_buf, down_buf, stash = buffers
    beside = device_at(line, 1 - column, core)

    def landed(buffer, way, slot):
        copy = remote(buffer, buffer, send.at[way, slot], recv.at[way, slot], {"dp": beside})
        copy.wait_recv()
        return buffer[...].astype(jnp.float32)

    def to_beside(target, step):
        chip = target * COLUMNS + 1 - column
        buffer = stash(chip)
        buffer[...] = have(chip).astype(buffer.dtype)
        remote(
            buffer,
            side_buf.at[target],
            send.at[1, target],
            recv.at[1, target],
            {"dp": beside},
        ).start()

    def along(target, step):
        chip = target * COLUMNS + column
        total = have(chip)
        total = total + landed(side_buf.at[target], 1, target)
        if step == 0:
            for by, way, landing in ((1, 2, up_buf), (-1, 3, down_buf)):
                settle_from(total, by, way, landing)
            return
        way, landing = (2, up_buf) if step > 0 else (3, down_buf)
        buffer = stash(chip)
        buffer[...] = total.astype(buffer.dtype)

        @pl.when(on_line(line - step, lines))
        def _():
            more = landed(landing.at[target], way, target)
            buffer[...] = (total + more).astype(buffer.dtype)

        remote(
            buffer,
            landing.at[target],
            send.at[way, target],
            recv.at[way, target],
            {"dp": device_at(line + step, column, core)},
        ).start()

    def settle_from(total, by, way, landing):
        if way == 2:
            settle(total, True)

        @pl.when(on_line(line - by, lines))
        def _():
            settle(landed(landing.at[line], way, line), False)

    def finish():
        def visit(target, step):
            buffer = side_buf.at[target]
            slots = [(1, target)]
            if step:
                slots.append((2 if step > 0 else 3, target))
            for way, slot in slots:
                remote(
                    buffer, buffer, send.at[way, slot], recv.at[way, slot], {"dp": beside}
                ).wait_send()

        for by in range(lines):
            on_distance(by, visit)

    return types.SimpleNamespace(to_beside=to_beside, along=along, finish=finish)


def pack_weights(vec_ref, qkv_ref, out_ref, w_ref, row):
    count, shard = vec_ref.shape
    cycle, padded, size = w_ref.shape
    width = out_ref.shape[1]
    for c in range(cycle):
        first, last = c * size, (c + 1) * size
        split = min(max(3 * width - first, 0), size)
        if split:
            w_ref[c, :shard, :split] = qkv_ref[:, first : first + split]
        if split < size:
            w_ref[c, :shard, split:] = out_ref[:, first + split - 3 * width : last - 3 * width]
    row[...] = jnp.zeros_like(row)
    for i in range(count):
        row[0:1, i * shard : (i + 1) * shard] = vec_ref[i : i + 1, :].astype(jnp.float32)
    for c in range(cycle):
        w_ref[c, shard:padded, :] = row[: padded - shard, :].astype(jnp.bfloat16)


def load_kernel(
    vec_ref, qkv_ref, out_ref, u_t_ref, x_t_ref, w_all, u_all, x_all, w_ref, row, u_ref, x_ref,
    w_send, w_recv, part_send, cycle_send, u_send, u_recv, x_send, x_recv, local,
):
    line, column, core, lines = place()
    cycle = lax.axis_size("ctx")
    mine = lax.axis_index("ctx")
    me = device_at(line, column, core)
    partner = device_at(line, column, 1 - core)
    others = [(mine + by) % cycle for by in range(1, cycle)]
    met = greet()
    pack_weights(vec_ref, qkv_ref, out_ref, w_ref, row)
    x_ref[...] = x_t_ref[...].T
    fold(u_ref, u_t_ref[...].astype(jnp.float32).T)
    met()

    weights = gather_stream(
        w_ref.at[mine],
        lambda shard: w_all.at[mine, shard],
        lambda way, shard: w_send.at[way, shard],
        lambda shard: w_recv.at[mine, shard],
        False,
    )
    ups = gather_stream(
        u_ref,
        lambda shard: u_all.at[shard],
        lambda way, shard: u_send.at[way, shard],
        lambda shard: u_recv.at[shard],
        True,
    )

    def part(c, shard, send, target, source=None):
        landing = w_all.at[c, shard]
        source = landing if source is None else source
        return remote(source, landing, send, w_recv.at[c, shard], target)

    def to_cycle(shard):
        for c in others:
            part(mine, shard, cycle_send.at[c, shard], {"ctx": c}).start()

    def from_cycle(shard):
        for c in others:
            copy = part(c, shard, part_send.at[c, shard], {"dp": partner})
            copy.wait_recv()
            copy.start()

    def swap(c, source):
        return remote(x_ref, x_all.at[source], x_send.at[c], x_recv.at[source], {"ctx": c})

    copies = [
        pltpu.make_async_copy(w_ref.at[c], w_all.at[c, me], local.at[c]) for c in range(cycle)
    ]
    copies.append(pltpu.make_async_copy(u_ref, u_all.at[me], local.at[cycle]))
    copies.append(pltpu.make_async_copy(x_ref, x_all.at[mine], local.at[cycle + 1]))
    weights.start()
    for c in others:
        swap(c, mine).start()
    ups.start()
    for c in others:
        part(c, me, part_send.at[c, me], {"dp": partner}, w_ref.at[c]).start()
    for copy in copies:
        copy.start()

    for d in range(lines):
        if d + 1 < lines:
            weights.relay(d + 1, to_cycle)
            ups.relay(d + 1)
        on_distance(d, lambda source, step: weights.cross(source, to_cycle))
        on_distance(d, lambda source, step: ups.cross(source))
        if d > 0:
            on_distance(d, lambda source, step: from_cycle(device_at(source, column, core)))
            on_distance(d - 1, lambda source, step: from_cycle(device_at(source, 1 - column, core)))
    on_distance(
        lines - 1, lambda source, step: from_cycle(device_at(source, 1 - column, core))
    )
    for chip in range(lines * COLUMNS):
        shard = chip * CORES + 1 - core
        weights.arrived(shard)
        ups.arrived(shard)
        for c in others:
            part(c, shard, part_send.at[c, shard], {"dp": partner}).wait_recv()
    weights.finish()
    ups.finish()
    for c in others:
        swap(c, c).wait_recv()
        swap(c, mine).wait_send()
        part(c, me, part_send.at[c, me], {"dp": partner}).wait_send()
    for d in range(lines):
        for across in (column, 1 - column):
            if d == 0 and across is column:
                continue
            shard = device_at(nearest(d), across, core)
            for c in others:
                part(c, shard, part_send.at[c, shard], {"dp": partner}).wait_send()
                part(mine, shard, cycle_send.at[c, shard], {"ctx": c}).wait_send()
    for copy in copies:
        copy.wait()


def load(vectors, w_qkv, w_out, ups_t, rows_t, collective_id):
    peers = lax.axis_size("dp")
    cycle = lax.axis_size("ctx")
    shard = w_out.shape[0]
    padded = (shard // GROUP + 1) * GROUP
    size = 4 * w_out.shape[1] // cycle
    block = ups_t.shape[::-1]
    bf16 = jnp.bfloat16
    dma = pltpu.SemaphoreType.DMA
    return pl.pallas_call(
        load_kernel,
        out_shape=(
            jax.ShapeDtypeStruct((cycle, peers, padded, size), bf16),
            jax.ShapeDtypeStruct((peers,) + fold_shape(*block), bf16),
            jax.ShapeDtypeStruct((cycle,) + block, bf16),
        ),
        in_specs=whole_vmem(5),
        out_specs=tuple([pl.BlockSpec(memory_space=pl.ANY)] * 3),
        scratch_shapes=[
            pltpu.VMEM((cycle, padded, size), bf16),
            pltpu.VMEM((GROUP, size), jnp.float32),
            pltpu.VMEM(fold_shape(*block), bf16),
            pltpu.VMEM(block, bf16),
            dma((4, peers)),
            dma((cycle, peers)),
            dma((cycle, peers)),
            dma((cycle, peers)),
            dma((4, peers)),
            dma((peers,)),
            dma((cycle,)),
            dma((cycle,)),
            dma((cycle + 2,)),
        ],
        compiler_params=pltpu.CompilerParams(collective_id=collective_id, has_side_effects=True),
    )(vectors, w_qkv, w_out, ups_t, rows_t)


def nothing(*_):
    return None


def spreader(width, shard, padded):
    source = lax.broadcasted_iota(jnp.int32, (width, 1), 0).astype(jnp.float32)
    block = jnp.floor((source + 0.5) * (1.0 / shard))
    target = source + block * float(padded - shard)
    lanes = lax.broadcasted_iota(jnp.int32, (1, width // shard * padded), 1).astype(jnp.float32)
    return jnp.where(target == lanes, 1.0, 0.0).astype(jnp.bfloat16)


def visible_bias(order_ref, first, rows, keys):
    block = keys // order_ref.shape[0]

    def position(slot):
        where = slot
        for b in range(order_ref.shape[0]):
            inside = (slot >= b * block) & (slot < (b + 1) * block)
            where = jnp.where(inside, (order_ref[b] - b) * block + slot, where)
        return where

    query = position(first + lax.broadcasted_iota(jnp.int32, (rows, 1), 0))
    key = position(lax.broadcasted_iota(jnp.int32, (1, keys), 1))
    return jnp.where(query >= key, 0.0, -1e30)


def parts_over(first, last, size, count):
    return [c for c in range(count) if c * size < last and (c + 1) * size > first]


def forward_kernel(*refs):
    forward_body(nothing, *refs)


def forward_body(
    ready, order_ref, x_ref, w_ref, vec_ref,
    spread_ref, normed_ref, q_ref, k_ref, v_ref, o_ref, o_spread_ref, h_ref, mid_ref,
    projected,
):
    cycle, rows, width = x_ref.shape
    shard = width // lax.axis_size("dp")
    mine = lax.axis_index("ctx")
    size = w_ref.shape[2]
    padded = w_ref.shape[1] // lax.axis_size("dp")
    spread_ref[...] = spreader(width, shard, padded)
    gain_one, shift_one, bias_q, bias_v, bias_o, gain_two, shift_two = [
        vec_ref[i : i + 1, :] for i in range(7)
    ]

    def project(left, first, last):
        for c in parts_over(first, last, size, cycle):
            projected[:, c * size : (c + 1) * size] = jnp.dot(
                left, w_ref[c], preferred_element_type=jnp.float32
            )

    def visit(c, carry):
        block = pl.ds(pl.multiple_of(c * rows, rows), rows)
        values, _, _ = norm_parts(x_ref[c].astype(jnp.float32), gain_one, shift_one)
        spread = jnp.dot(
            values.astype(jnp.bfloat16), spread_ref[...], preferred_element_type=jnp.float32
        ).astype(jnp.bfloat16)
        normed_ref[block, :] = spread

        @pl.when(c == 0)
        def _():
            ready()

        project(spread, 0, 3 * width)
        k_ref[block, :] = projected[:, width : 2 * width].astype(jnp.bfloat16)
        v_ref[block, :] = (projected[:, 2 * width : 3 * width] + bias_v).astype(jnp.bfloat16)

        @pl.when(c == mine)
        def _():
            q_ref[...] = (projected[:, :width] + bias_q).astype(jnp.bfloat16)

        return carry

    lax.fori_loop(0, cycle, visit, 0)
    bias = visible_bias(order_ref, mine * rows, rows, cycle * rows)
    for start, lanes in head_groups(width):
        block = slice(start, start + lanes)
        q, k, v = q_ref[:, block], k_ref[:, block], v_ref[:, block]
        total = None
        for mask in head_masks(lanes):
            scores = contract_last(keep(q, mask), k) * SCALE + bias
            largest = jnp.max(scores, axis=-1, keepdims=True)
            exponent = jnp.exp(scores - largest)
            inverse = 1.0 / jnp.sum(exponent, axis=-1, keepdims=True)
            part = jnp.dot(
                exponent.astype(jnp.bfloat16), keep(v, mask), preferred_element_type=jnp.float32
            )
            part = part * inverse
            total = part if total is None else total + part
        o_ref[:, block] = total.astype(jnp.bfloat16)
    o_spread = jnp.dot(
        o_ref[...], spread_ref[...], preferred_element_type=jnp.float32
    ).astype(jnp.bfloat16)
    o_spread_ref[...] = o_spread
    project(o_spread, 3 * width, 4 * width)
    hidden = x_ref[mine].astype(jnp.float32) + projected[:, 3 * width : 4 * width] + bias_o
    h_ref[...] = hidden
    fold(mid_ref, norm_parts(hidden, gain_two, shift_two)[0])


def ordered(count):
    return [pl.BlockSpec(memory_space=pltpu.SMEM)] + whole_vmem(count - 1)


def forward_shapes(x, w):
    cycle, rows, width = x.shape
    full = w.shape[1]
    f32, bf16 = jnp.float32, jnp.bfloat16
    outs = [
        ((width, full), bf16),
        ((cycle * rows, full), bf16),
        ((rows, width), bf16),
        ((cycle * rows, width), bf16),
        ((cycle * rows, width), bf16),
        ((rows, width), bf16),
        ((rows, full), bf16),
        ((rows, width), f32),
    ]
    return outs, (fold_shape(rows, width), bf16), ((rows, 4 * width), f32)


def forward(order, x, w, vectors):
    outs, mid, projected = forward_shapes(x, w)
    return pl.pallas_call(
        forward_kernel,
        out_shape=tuple(jax.ShapeDtypeStruct(*entry) for entry in outs + [mid]),
        in_specs=ordered(4),
        out_specs=tuple(whole_vmem(len(outs) + 1)),
        scratch_shapes=[pltpu.VMEM(*projected)],
        compiler_params=pltpu.CompilerParams(vmem_limit_bytes=VMEM_LIMIT),
    )(order, x, w, vectors)


def column_sum(values):
    return jnp.sum(values, axis=0, keepdims=True)


def store_owners(grads, ref, padded):
    for s in range(grads.shape[0] // padded):
        ref[s] = grads[s * padded : (s + 1) * padded].astype(ref.dtype)


def weigh_columns(slab_ref, c, normed_ref, wide):
    padded, tall = slab_ref.shape[2:]
    grads = contract_first(normed_ref[...], wide[:, c * tall : (c + 1) * tall])
    store_owners(grads, slab_ref.at[c], padded)


def weigh_kernel(normed_ref, wide_ref, slab_ref):
    for c in range(slab_ref.shape[0]):
        weigh_columns(slab_ref, c, normed_ref, wide_ref)


def back_norm(r):
    rows, width = r.hidden.shape
    gain, shift = r.vec[5:6, :], r.vec[6:7, :]
    _, normed, inverse = norm_parts(r.hidden[...], gain, shift)
    upstream = r.upstream_t[...].T.astype(jnp.float32)
    grad_mid = r.grad_mid[...]
    r.sums[0:2, :] = jnp.zeros((2, width), jnp.float32)
    r.sums[5:6, :] = column_sum(grad_mid * normed)
    r.sums[6:7, :] = column_sum(grad_mid)
    r.sums[7:8, :] = column_sum(upstream)
    grad_hidden = upstream + norm_back(grad_mid, normed, inverse, gain)
    r.dh[...] = grad_hidden
    r.sums[4:5, :] = column_sum(grad_hidden)
    grad_hidden_b = grad_hidden.astype(jnp.bfloat16)
    r.head_wide[...] = jnp.zeros_like(r.head_wide)
    r.head_wide[:, 3 * width : 4 * width] = grad_hidden_b
    grads = contract_first(r.o_spread[...], grad_hidden_b)
    store_owners(grads, r.out_slab, r.out_slab.shape[1])


def back_attend(r):
    cycle, rows, width = r.x.shape
    mine = lax.axis_index("ctx")
    size = r.w.shape[2]
    grad_ctx = None
    for c in parts_over(3 * width, 4 * width, size, cycle):
        more = contract_last(r.head_wide[:, c * size : (c + 1) * size], r.w[c])
        grad_ctx = more if grad_ctx is None else grad_ctx + more
    grad_ctx = contract_last(grad_ctx.astype(jnp.bfloat16), r.spread[...])
    r.do[...] = grad_ctx.astype(jnp.bfloat16)
    r.wide[...] = jnp.zeros_like(r.wide)
    own = pl.ds(pl.multiple_of(mine * rows, rows), rows)
    bias = visible_bias(r.order, mine * rows, rows, cycle * rows)
    for start, lanes in head_groups(width):
        block = slice(start, start + lanes)
        q, k, v = r.q[:, block], r.k[:, block], r.v[:, block]
        do, o = r.do[:, block], r.o[:, block]
        product = do.astype(jnp.float32) * o.astype(jnp.float32)
        dq = dk = dv = None
        for mask in head_masks(lanes):
            q_h, k_h, do_h = keep(q, mask), keep(k, mask), keep(do, mask)
            product_h = product if mask is None else product * mask.astype(jnp.float32)
            delta = jnp.sum(product_h, axis=-1, keepdims=True)
            scores = contract_last(q_h, k) * SCALE + bias
            largest = jnp.max(scores, axis=-1, keepdims=True)
            exponent = jnp.exp(scores - largest)
            p = exponent * (1.0 / jnp.sum(exponent, axis=-1, keepdims=True))
            dp = contract_last(do_h, v)
            ds = (p * (dp - delta)).astype(jnp.bfloat16)
            dv_h = contract_first(p.astype(jnp.bfloat16), do_h)
            dq_h = jnp.dot(ds, k_h, preferred_element_type=jnp.float32)
            dk_h = contract_first(ds, q_h)
            dq = dq_h if dq is None else dq + dq_h
            dk = dk_h if dk is None else dk + dk_h
            dv = dv_h if dv is None else dv + dv_h
        dq = dq * SCALE
        r.wide[own, start : start + lanes] = dq.astype(jnp.bfloat16)
        r.wide[:, width + start : width + start + lanes] = (dk * SCALE).astype(jnp.bfloat16)
        r.wide[:, 2 * width + start : 2 * width + start + lanes] = dv.astype(jnp.bfloat16)
        r.sums[2:3, block] = column_sum(dq)
        r.sums[3:4, block] = column_sum(dv)


def back_rows(r):
    cycle, rows, width = r.x.shape
    mine = lax.axis_index("ctx")
    size = r.w.shape[2]
    gain, shift = r.vec[0:1, :], r.vec[1:2, :]

    def visit(block, carry):
        span = pl.ds(pl.multiple_of(block * rows, rows), rows)
        total = None
        for c in parts_over(0, 3 * width, size, cycle):
            more = contract_last(r.wide[span, c * size : (c + 1) * size], r.w[c])
            total = more if total is None else total + more
        high = total.astype(jnp.bfloat16)
        low = (total - high.astype(jnp.float32)).astype(jnp.bfloat16)
        grad = contract_last(high, r.spread[...]) + contract_last(low, r.spread[...])
        _, normed, _ = norm_parts(r.x[block].astype(jnp.float32), gain, shift)
        r.sums[0:1, :] += column_sum(grad * normed)
        r.sums[1:2, :] += column_sum(grad)
        r.da[block] = grad.astype(jnp.bfloat16)

        @pl.when(block == mine)
        def _():
            r.da_own[...] = grad

        return carry

    lax.fori_loop(0, cycle, visit, 0)


BACK_INS = [
    "order", "x", "w", "vec", "spread", "normed", "q", "k", "v", "o", "o_spread", "hidden",
    "upstream_t", "grad_mid",
]
BACK_MADE = ["sums", "da", "da_own", "dh", "out_slab"]
BACK_KEPT = ["wide", "head_wide", "do"]


def back_kernel(*refs):
    r = types.SimpleNamespace(**dict(zip(BACK_INS + BACK_MADE + BACK_KEPT, refs)))
    back_norm(r)
    back_attend(r)
    back_rows(r)


def back_shapes(x, padded):
    cycle, rows, width = x.shape
    f32, bf16 = jnp.float32, jnp.bfloat16
    made = [
        ((8, width), f32),
        ((cycle, rows, width), bf16),
        ((rows, width), f32),
        ((rows, width), f32),
        ((lax.axis_size("dp"), padded, width), bf16),
    ]
    kept = [((cycle * rows, 4 * width), bf16), ((rows, 4 * width), bf16), ((rows, width), bf16)]
    return made, kept


def backward(arrays, padded):
    named = dict(zip(BACK_INS, arrays))
    cycle, rows, width = named["x"].shape
    made, kept = back_shapes(named["x"], padded)
    params = pltpu.CompilerParams(vmem_limit_bytes=VMEM_LIMIT)
    sums, da, da_own, dh, out_slab, wide = pl.pallas_call(
        back_kernel,
        out_shape=tuple(jax.ShapeDtypeStruct(*entry) for entry in made + kept[:1]),
        in_specs=ordered(len(arrays)),
        out_specs=tuple(whole_vmem(len(made) + 1)),
        scratch_shapes=[pltpu.VMEM(*entry) for entry in kept[1:]],
        compiler_params=params,
    )(*arrays)
    slab = pl.pallas_call(
        weigh_kernel,
        out_shape=jax.ShapeDtypeStruct(
            (cycle, out_slab.shape[0], padded, 3 * width // cycle), jnp.bfloat16
        ),
        in_specs=whole_vmem(2),
        out_specs=whole_vmem(1)[0],
        compiler_params=params,
    )(named["normed"], wide)
    return slab, sums, da, da_own, dh, out_slab


def whole_vmem(count):
    return [pl.BlockSpec(memory_space=pltpu.VMEM)] * count


def ffn_kernel(*refs):
    ffn_body(nothing, *refs)


def middle_kernel(count, *refs):
    order, x, w_far, vec, ups, up_t, down, b_up = refs[:8]
    made, rest = refs[8 : 8 + count], refs[8 + count :]
    outs, (w, w_sem, mid, projected), kept = rest[:5], rest[5:9], rest[9:]
    copies = [
        pltpu.make_async_copy(w_far.at[c], w.at[c], w_sem.at[c]) for c in range(w.shape[0])
    ]

    def ready():
        for copy in copies:
            copy.wait()

    def before():
        for copy in copies:
            copy.start()
        forward_body(ready, order, x, w, vec, *made, mid, projected)

    ffn_body(before, mid, ups, up_t, down, b_up, *outs, *kept)


def ffn_body(
    before, mid_ref, ups_far, w_up_t_ref, w_down_ref, b_up_ref,
    gm_ref, br_far, gup_ref, gdown_ref, gb_ref,
    ups_ref, br_ref, ups_sem, br_sem, mids, parts, acts, grads, up_total, down_total, give, take, bias_part, bias_all,
    core_buf, side_buf, up_buf, down_buf,
    g_send, g_recv, c_send, c_recv, r_send, r_recv, y_send, y_recv, b_send, b_recv,
):
    line, column, core, lines = place()
    rows, width = gm_ref.shape
    cycle = lax.axis_size("ctx")
    mine = lax.axis_index("ctx")
    me = device_at(line, column, core)
    partner = device_at(line, column, 1 - core)
    met = greet()
    ups_copy = pltpu.make_async_copy(ups_far, ups_ref, ups_sem)
    ups_copy.start()
    before()
    mids[me] = mid_ref[...]
    met()

    def br_copy(chip):
        pair = pl.ds(chip * CORES, CORES)
        return pltpu.make_async_copy(br_ref.at[pair], br_far.at[pair], br_sem.at[chip])

    def spread(ref, chip):
        pieces = unfold(ref[pl.ds(chip * CORES, CORES)])
        pieces = [piece.reshape(CORES * rows // FOLD, width) for piece in pieces]
        return jnp.concatenate(pieces, axis=0)

    def gather_rows(ref, chip, values):
        half = CORES * rows // FOLD
        for i in range(FOLD):
            piece = values[i * half : (i + 1) * half].astype(ref.dtype)
            piece = piece.reshape(CORES, rows // FOLD, width)
            ref[pl.ds(chip * CORES, CORES), :, i * width : (i + 1) * width] = piece

    gather = gather_stream(
        mid_ref,
        lambda shard: mids.at[shard],
        lambda way, shard: g_send.at[way, shard],
        lambda shard: g_recv.at[shard],
        False,
    )
    gather.start()
    bias_part[...] = jnp.zeros_like(bias_part)

    def to_core(chip):
        return remote(
            parts.at[chip * CORES + 1 - core],
            core_buf.at[chip],
            c_send.at[chip],
            c_recv.at[chip],
            {"dp": partner},
        )

    def feed(chip):
        mid = spread(mids, chip)
        ups = spread(ups_ref, chip)
        pre = contract_last(mid, w_up_t_ref[...]) + b_up_ref[...]
        grad = contract_last(ups, w_down_ref[...])
        half = 0.5 * (1.0 + lax.erf(pre * 0.7071067811865476))
        act = (pre * half).astype(jnp.bfloat16)
        grad = grad * (half + pre * jnp.exp(-0.5 * pre * pre) * 0.3989422804014327)
        bias_part[...] += jnp.sum(grad, axis=0, keepdims=True)
        grad = grad.astype(jnp.bfloat16)
        acts[chip] = act
        grads[chip] = grad
        part = jnp.dot(grad, w_up_t_ref[...], preferred_element_type=jnp.float32)
        gather_rows(parts, chip, part)
        to_core(chip).start()
        branch = jnp.dot(act, w_down_ref[...], preferred_element_type=jnp.float32)
        gather_rows(br_ref, chip, branch)
        br_copy(chip).start()

    def visit(d, carry):
        @pl.when(d + 1 < lines)
        def _():
            gather.relay(d + 1)

        at = nearest(d)
        gather.arrived(device_at(at, column, 1 - core))
        feed(at * COLUMNS + column)
        gather.cross(at)
        gather.arrived(device_at(at, 1 - column, 1 - core))
        feed(at * COLUMNS + 1 - column)
        return carry

    ups_copy.wait()
    lax.fori_loop(0, lines, visit, 0)

    def have(chip):
        to_core(chip).wait_recv()
        return core_buf[chip].astype(jnp.float32) + parts[chip * CORES + core].astype(jnp.float32)

    def settle(total, first):
        half = rows // FOLD
        for i, piece in enumerate(unfold(total)):
            span = slice(i * half, (i + 1) * half)
            gm_ref[span, :] = piece if first else gm_ref[span, :] + piece

    reduce = reduce_stream(
        have,
        (side_buf, up_buf, down_buf, lambda chip: parts.at[chip * CORES + core]),
        r_send,
        r_recv,
        settle,
    )
    for by in range(lines - 1, -1, -1):
        on_distance(by, reduce.to_beside)

    def swap(c, source):
        return remote(give.at[c], take.at[source], y_send.at[c], y_recv.at[source], {"ctx": c})

    def swap_bias(c, source):
        landing = bias_all.at[source]
        return remote(bias_part, landing, b_send.at[c], b_recv.at[source], {"ctx": c})

    bias_all[mine] = bias_part[...]
    others = [(mine + by) % cycle for by in range(1, cycle)]
    for c in others:
        swap_bias(c, mine).start()
    up_total[...] = jnp.zeros_like(up_total)
    down_total[...] = jnp.zeros_like(down_total)

    def weigh(chip, carry):
        up_total[...] += contract_first(grads[chip], spread(mids, chip))
        down_total[...] += contract_first(acts[chip], spread(ups_ref, chip))
        return carry

    lax.fori_loop(0, lines * COLUMNS, weigh, 0)
    size = width // cycle
    for c in range(cycle):
        up_part = up_total[:, c * size : (c + 1) * size]
        down_part = down_total[:, c * size : (c + 1) * size]

        @pl.when(c == mine)
        def _():
            gup_ref[...] = up_part
            gdown_ref[...] = down_part

        @pl.when(c != mine)
        def _():
            give[c, 0] = up_part.astype(give.dtype)
            give[c, 1] = down_part.astype(give.dtype)
            swap(c, mine).start()

    for by in range(lines - 1, -1, -1):
        on_distance(by, reduce.along)
    for c in others:
        swap(c, c).wait_recv()
        gup_ref[...] += take[c, 0].astype(jnp.float32)
        gdown_ref[...] += take[c, 1].astype(jnp.float32)
        swap_bias(c, c).wait_recv()
    total = bias_all[0]
    for c in range(1, cycle):
        total = total + bias_all[c]
    gb_ref[...] = total
    for c in others:
        swap(c, mine).wait_send()
        swap_bias(c, mine).wait_send()
    for chip in range(lines * COLUMNS):
        to_core(chip).wait_send()
        br_copy(chip).wait()
    reduce.finish()
    gather.finish()


def ffn_shapes(rows, width, hidden):
    peers = lax.axis_size("dp")
    cycle = lax.axis_size("ctx")
    lines = peers // (CORES * COLUMNS)
    chips = lines * COLUMNS
    dma = pltpu.SemaphoreType.DMA
    f32, bf16 = jnp.float32, jnp.bfloat16
    thin = width // cycle

    def slabs(count):
        return pltpu.VMEM((count,) + fold_shape(rows, width), bf16)

    outs = [
        ((rows, width), f32),
        ((peers,) + fold_shape(rows, width), bf16),
        ((hidden, thin), f32),
        ((hidden, thin), f32),
        ((1, hidden), f32),
    ]
    kept = [
        slabs(peers),
        slabs(peers),
        dma(()),
        dma((chips,)),
        slabs(peers),
        slabs(peers),
        pltpu.VMEM((chips, CORES * rows, hidden), bf16),
        pltpu.VMEM((chips, CORES * rows, hidden), bf16),
        pltpu.VMEM((hidden, width), f32),
        pltpu.VMEM((hidden, width), f32),
        pltpu.VMEM((cycle, 2, hidden, thin), bf16),
        pltpu.VMEM((cycle, 2, hidden, thin), bf16),
        pltpu.VMEM((1, hidden), f32),
        pltpu.VMEM((cycle, 1, hidden), f32),
        slabs(chips),
        slabs(lines),
        slabs(lines),
        slabs(lines),
        dma((4, peers)),
        dma((peers,)),
        dma((chips,)),
        dma((chips,)),
        dma((4, lines)),
        dma((4, lines)),
        dma((cycle,)),
        dma((cycle,)),
        dma((cycle,)),
        dma((cycle,)),
    ]
    return outs, kept


def forward_and_feed(order, x, w, vectors, ups, w_up_t, w_down, b_up, collective_id):
    cycle, rows, width = x.shape
    hidden = w_down.shape[0]
    outs, kept = ffn_shapes(rows, width, hidden)
    made, mid, projected = forward_shapes(x, w)
    near = pl.BlockSpec(memory_space=pltpu.VMEM)
    far = pl.BlockSpec(memory_space=pl.ANY)
    out_specs = [near, far, near, near, near]
    params = pltpu.CompilerParams(
        collective_id=collective_id, has_side_effects=True, vmem_limit_bytes=VMEM_LIMIT
    )
    tail = (ups, w_up_t, w_down, b_up)
    shapes = [jax.ShapeDtypeStruct(*entry) for entry in outs]
    if w.size + ups.size < FUSED_LIMIT:
        scratch = [pltpu.VMEM(w.shape, w.dtype), pltpu.SemaphoreType.DMA((cycle,))]
        scratch += [pltpu.VMEM(*mid), pltpu.VMEM(*projected)]
        results = pl.pallas_call(
            functools.partial(middle_kernel, len(made)),
            out_shape=tuple([jax.ShapeDtypeStruct(*entry) for entry in made] + shapes),
            in_specs=ordered(2) + [far, near, far, near, near, near],
            out_specs=tuple(whole_vmem(len(made)) + out_specs),
            scratch_shapes=scratch + kept,
            compiler_params=params,
        )(order, x, w, vectors, *tail)
        return results[: len(made)], results[len(made) :]
    *made, mid = forward(order, x, w, vectors)
    return made, pl.pallas_call(
        ffn_kernel,
        out_shape=tuple(shapes),
        in_specs=[near, far, near, near, near],
        out_specs=tuple(out_specs),
        scratch_shapes=kept,
        compiler_params=params,
    )(mid, *tail)


def settle_body(r, early, middle, late):
    line, column, core, lines = place()
    rows, width = r.dh.shape
    cycle = lax.axis_size("ctx")
    mine = lax.axis_index("ctx")
    beside = device_at(line, 1 - column, core)
    partner = device_at(line, column, 1 - core)
    others = [(mine + by) % cycle for by in range(1, cycle)]
    chips = range(lines * COLUMNS)
    local = [
        pltpu.make_async_copy(
            r.br.at[chip * CORES + core], r.br_own.at[chip], r.local.at[chip]
        )
        for chip in chips
    ]
    met = greet()
    for copy in local:
        copy.start()
    met()

    def to_core(name, chip):
        source = getattr(r, name)
        sems = getattr(r, name + "_core_sems")
        return remote(
            source.at[chip * CORES + 1 - core],
            getattr(r, name + "_core").at[chip],
            sems.at[0, chip],
            sems.at[1, chip],
            {"dp": partner},
        )

    def slab_to_core(c, chip):
        return remote(
            r.slab.at[c, chip * CORES + 1 - core],
            r.slab_core.at[c, chip],
            r.slab_core_sems.at[0, c, chip],
            r.slab_core_sems.at[1, c, chip],
            {"dp": partner},
        )

    def slab_to_cycle(c, chip, source):
        return remote(
            r.slab_core.at[c, chip],
            r.slab_cycle.at[source, chip],
            r.slab_cycle_sems.at[0, c, chip],
            r.slab_cycle_sems.at[1, source, chip],
            {"ctx": c},
        )

    def swap(name, slot, c, source):
        sems = r.swap_sems
        return remote(
            getattr(r, name).at[c],
            getattr(r, name + "_all").at[source],
            sems.at[0, slot, c],
            sems.at[1, slot, source],
            {"ctx": c},
        )

    def both(act):
        def visit(target, step):
            act(target * COLUMNS + 1 - column)
            act(target * COLUMNS + column)

        return visit

    def far_first(act):
        for by in range(lines - 1, -1, -1):
            on_distance(by, act)

    one = r.one_sems
    sums_to_core = remote(r.sums, r.sums_core, one.at[0, 0], one.at[1, 0], {"dp": partner})
    sums_to_side = remote(r.stage.at[0], r.sums_side, one.at[0, 1], one.at[1, 1], {"dp": beside})

    def sums_to_line(to, source):
        return remote(
            r.stage.at[1],
            r.sums_line.at[source],
            r.line_sems.at[0, to],
            r.line_sems.at[1, source],
            {"dp": device_at(to, column, core)},
        )

    def sums_to_cycle(c, source):
        return remote(
            r.stage.at[2],
            r.sums_cycle.at[source],
            r.swap_sems.at[0, 2, c],
            r.swap_sems.at[1, 2, source],
            {"ctx": c},
        )

    def cycle_sums(chip):
        for c in others:
            slab_to_core(c, chip).wait_recv()
            total = r.slab_core[c, chip].astype(jnp.float32)
            total = total + r.slab[c, chip * CORES + core].astype(jnp.float32)
            r.slab_core[c, chip] = total.astype(r.slab_core.dtype)
            slab_to_cycle(c, chip, mine).start()

    def br_have(chip):
        to_core("br", chip).wait_recv()
        return r.br_core[chip].astype(jnp.float32) + r.br_own[chip].astype(jnp.float32)

    def out_have(chip):
        to_core("out_slab", chip).wait_recv()
        own = r.out_slab[chip * CORES + core].astype(jnp.float32)
        return r.out_slab_core[chip].astype(jnp.float32) + own

    def slab_have(chip):
        slab_to_core(mine, chip).wait_recv()
        total = r.slab_core[mine, chip].astype(jnp.float32)
        total = total + r.slab[mine, chip * CORES + core].astype(jnp.float32)
        for c in others:
            slab_to_cycle(c, chip, c).wait_recv()
            total = total + r.slab_cycle[c, chip].astype(jnp.float32)
        return total

    def into(ref):
        def settle(total, first):
            ref[...] = total if first else ref[...] + total

        return settle

    def stream(have, name, stash, ref):
        sems = getattr(r, name + "_sems")
        lanes = [getattr(r, name + "_lanes").at[i] for i in range(3)]
        return reduce_stream(have, (*lanes, stash), sems.at[0], sems.at[1], into(ref))

    branch = stream(br_have, "br", lambda chip: r.br_own.at[chip], r.branch_sum)
    heads = stream(out_have, "out_slab", lambda chip: r.out_slab_core.at[chip], r.out_sum)
    slabs = stream(slab_have, "slab", lambda chip: r.slab_core.at[mine, chip], r.slab_sum)

    for across in (1 - column, column):
        far_first(lambda target, step: to_core("br", target * COLUMNS + across).start())
    early()
    for copy in local:
        copy.wait()
    far_first(both(lambda chip: to_core("out_slab", chip).start()))
    far_first(branch.to_beside)
    middle(True)
    for c in others:
        far_first(both(lambda chip: slab_to_core(c, chip).start()))
    on_distance(lines - 1, both(cycle_sums))
    far_first(heads.to_beside)
    middle(False)
    far_first(both(lambda chip: slab_to_core(mine, chip).start()))
    for by in range(lines - 2, -1, -1):
        on_distance(by, both(cycle_sums))
    on_distance(lines - 1, branch.along)
    late()
    sums_to_core.start()
    for c in others:
        swap("da", 0, c, mine).start()
    sums_to_core.wait_recv()
    r.stage[0] = r.sums[...] + r.sums_core[...]
    sums_to_side.start()

    for by in range(lines - 1, -1, -1):
        if by + 1 < lines:
            on_distance(by, branch.along)
        on_distance(by, slabs.to_beside)
        on_distance(by, heads.along)
        if by + 1 < lines:
            on_distance(by + 1, slabs.along)
        if by == min(1, lines - 1):
            sums_to_side.wait_recv()
            r.stage[1] = r.stage[0] + r.sums_side[...]
            r.sums_line[line] = r.stage[1]
            for away in range(1, lines):
                sums_to_line((line + away) % lines, line).start()
    thin = r.out_half.shape[1]
    for c in range(cycle):
        piece = r.out_sum[:, c * thin : (c + 1) * thin]

        @pl.when(c == mine)
        def _():
            r.out_half[...] = piece

        @pl.when(c != mine)
        def _():
            r.give[c] = piece.astype(r.give.dtype)
            swap("give", 1, c, mine).start()

    for away in range(1, lines):
        source = (line + away) % lines
        sums_to_line(source, source).wait_recv()
    total = r.sums_line[0]
    for by in range(1, lines):
        total = total + r.sums_line[by]
    r.stage[2] = total
    r.sums_cycle[mine] = total
    for c in others:
        sums_to_cycle(c, mine).start()
    branch_rows = jnp.concatenate(unfold(r.branch_sum[...]), axis=0)
    r.out_t[...] = (r.hidden[...] + branch_rows + r.vec[7:8, :]).astype(r.out_t.dtype).T
    grad = r.da_own[...]
    for c in others:
        swap("da", 0, c, c).wait_recv()
        grad = grad + r.da_all[c].astype(jnp.float32)
    gain, bias = r.vec[0:1, :], r.vec[1:2, :]
    _, normed, inverse = norm_parts(r.x[mine].astype(jnp.float32), gain, bias)
    r.ing_t[...] = (r.dh[...] + norm_back(grad, normed, inverse, gain)).T
    on_distance(0, slabs.along)
    for c in others:
        swap("give", 1, c, c).wait_recv()
        r.out_half[...] += r.give_all[c].astype(jnp.float32)
        sums_to_cycle(c, c).wait_recv()
    total = r.sums_cycle[0]
    for c in range(1, cycle):
        total = total + r.sums_cycle[c]
    r.total[...] = total

    sums_to_core.wait_send()
    sums_to_side.wait_send()
    for c in others:
        sums_to_cycle(c, mine).wait_send()
        swap("da", 0, c, mine).wait_send()
        swap("give", 1, c, mine).wait_send()
    for away in range(1, lines):
        sums_to_line((line + away) % lines, line).wait_send()
    branch.finish()
    heads.finish()
    slabs.finish()
    for chip in chips:
        to_core("br", chip).wait_send()
        to_core("out_slab", chip).wait_send()
        slab_to_core(mine, chip).wait_send()
        for c in others:
            slab_to_core(c, chip).wait_send()
            slab_to_cycle(c, chip, mine).wait_send()


SETTLE_OUTS = ["out_t", "ing_t", "slab_sum", "out_half", "total"]
SETTLE_KEPT = [
    "slab_core", "slab_cycle", "slab_lanes", "br_own", "br_core", "br_lanes", "out_slab_core",
    "out_slab_lanes", "out_sum", "branch_sum", "da_all", "give", "give_all", "stage", "sums_core",
    "sums_side", "sums_line", "sums_cycle", "local", "slab_core_sems", "slab_cycle_sems",
    "slab_sems", "br_core_sems", "br_sems", "out_slab_core_sems", "out_slab_sems", "swap_sems",
    "one_sems", "line_sems",
]


def settle_kernel(names, *refs):
    r = types.SimpleNamespace(**dict(zip(names + SETTLE_OUTS + SETTLE_KEPT, refs)))
    settle_body(r, nothing, nothing, nothing)


LATE = ["w", "spread", "q", "k", "v", "o", "normed"]


def finish_kernel(names, *refs):
    names = names + SETTLE_OUTS + SETTLE_KEPT + BACK_MADE + BACK_KEPT + ["slab"] + LATE
    r = types.SimpleNamespace(**dict(zip(names + ["late_sems"], refs)))
    cycle = r.w.shape[0]
    mine = lax.axis_index("ctx")
    copies = [
        pltpu.make_async_copy(getattr(r, name + "_far"), getattr(r, name), r.late_sems.at[i])
        for i, name in enumerate(LATE)
    ]
    for copy in copies:
        copy.start()

    def middle(away):
        if away:
            for copy in copies:
                copy.wait()
            back_attend(r)
        for c in range(cycle):

            @pl.when((c != mine) if away else (c == mine))
            def _():
                weigh_columns(r.slab, c, r.normed, r.wide)

    settle_body(r, lambda: back_norm(r), middle, lambda: back_rows(r))


def settle_shapes(cycle, peers, padded, rows, width):
    lines = peers // (CORES * COLUMNS)
    chips = lines * COLUMNS
    tall, thin = 3 * width // cycle, width // cycle
    folded = fold_shape(rows, width)
    dma = pltpu.SemaphoreType.DMA
    f32, bf16 = jnp.float32, jnp.bfloat16

    def buffer(dtype, *shape):
        return pltpu.VMEM(shape, dtype)

    outs = [
        ((width, rows), bf16),
        ((width, rows), f32),
        ((padded, tall), f32),
        ((padded, thin), f32),
        ((8, width), f32),
    ]
    kept = [
        buffer(bf16, cycle, chips, padded, tall),
        buffer(bf16, cycle, chips, padded, tall),
        buffer(bf16, 3, lines, padded, tall),
        buffer(bf16, chips, *folded),
        buffer(bf16, chips, *folded),
        buffer(bf16, 3, lines, *folded),
        buffer(bf16, chips, padded, width),
        buffer(bf16, 3, lines, padded, width),
        buffer(f32, padded, width),
        buffer(f32, *folded),
        buffer(bf16, cycle, rows, width),
        buffer(bf16, cycle, padded, thin),
        buffer(bf16, cycle, padded, thin),
        buffer(f32, 3, 8, width),
        buffer(f32, 8, width),
        buffer(f32, 8, width),
        buffer(f32, lines, 8, width),
        buffer(f32, cycle, 8, width),
        dma((chips,)),
        dma((2, cycle, chips)),
        dma((2, cycle, chips)),
        dma((2, 4, lines)),
        dma((2, chips)),
        dma((2, 4, lines)),
        dma((2, chips)),
        dma((2, 4, lines)),
        dma((2, 3, cycle)),
        dma((2, 2)),
        dma((2, lines)),
    ]
    return outs, kept


def emit_kernel(count, out_t, ing_t, slab_sum, out_half, up_t, down, *refs):
    outs = refs[:count]
    shard = outs[2].shape[0]
    outs[0][...] = out_t[...]
    outs[1][...] = ing_t[...]
    outs[2][...] = slab_sum[:shard, :]
    outs[3][...] = out_half[:shard, :]
    outs[4][...] = up_t[...]
    outs[5][...] = down[...]


def emit(shard, *arrays):
    shapes = [a.shape for a in arrays]
    shapes[2:4] = [(shard, shape[1]) for shape in shapes[2:4]]
    return pl.pallas_call(
        functools.partial(emit_kernel, len(arrays)),
        out_shape=tuple(jax.ShapeDtypeStruct(t, a.dtype) for t, a in zip(shapes, arrays)),
        in_specs=whole_vmem(len(arrays)),
        out_specs=tuple(whole_vmem(len(arrays))),
    )(*arrays)


def finish(arrays, br, collective_id):
    named = dict(zip(BACK_INS, arrays))
    x, w = named["x"], named["w"]
    cycle, rows, width = x.shape
    peers = lax.axis_size("dp")
    padded = w.shape[1] // peers
    outs, kept = settle_shapes(cycle, peers, padded, rows, width)
    made, back_kept = back_shapes(x, padded)
    slab = ((cycle, peers, padded, 3 * width // cycle), jnp.bfloat16)
    params = pltpu.CompilerParams(
        collective_id=collective_id, has_side_effects=True, vmem_limit_bytes=VMEM_LIMIT
    )
    out_shape = tuple(jax.ShapeDtypeStruct(*entry) for entry in outs)
    far = pl.BlockSpec(memory_space=pl.ANY)
    if w.size + slab[0][0] * peers * padded * slab[0][3] < FUSED_LIMIT:
        names = [name + "_far" if name in LATE else name for name in BACK_INS] + ["br"]
        specs = ordered(len(arrays))
        for name in LATE:
            specs[BACK_INS.index(name)] = far
        extra = [pltpu.VMEM(*entry) for entry in made + back_kept + [slab]]
        extra += [pltpu.VMEM(named[name].shape, named[name].dtype) for name in LATE]
        extra += [pltpu.SemaphoreType.DMA((len(LATE),))]
        return pl.pallas_call(
            functools.partial(finish_kernel, names),
            out_shape=out_shape,
            in_specs=specs + [far],
            out_specs=tuple(whole_vmem(len(outs))),
            scratch_shapes=kept + extra,
            compiler_params=params,
        )(*arrays, br)
    slabs, sums, da, da_own, dh, out_slab = backward(arrays, padded)
    names = ["slab", "sums", "da", "da_own", "dh", "out_slab", "hidden", "x", "vec", "br"]
    return pl.pallas_call(
        functools.partial(settle_kernel, names),
        out_shape=out_shape,
        in_specs=whole_vmem(9) + [far],
        out_specs=tuple(whole_vmem(len(outs))),
        scratch_shapes=kept,
        compiler_params=params,
    )(slabs, sums, da, da_own, dh, out_slab, named["hidden"], x, named["vec"], br)


def per_device(
    block_in,
    cotangent,
    block_order,
    ln1_gain,
    ln1_bias,
    w_qkv,
    b_query,
    b_value,
    w_out,
    b_out,
    ln2_gain,
    ln2_bias,
    w_up,
    b_up,
    w_down,
    b_down,
):
    width, shard = w_out.shape[1], w_out.shape[0]
    peers = lax.axis_size("dp")
    rows_t, upstream_t = block_in[0].T, cotangent[0].T
    vectors = jnp.stack(
        [ln1_gain, ln1_bias, b_query, b_value, b_out, ln2_gain, ln2_bias, b_down]
    )
    count = vectors.shape[0]
    weights, ups, rows = load(vectors, w_qkv, w_out, upstream_t, rows_t, 0)
    vectors = weights[0, :, shard, : count * shard].reshape(peers, count, shard)
    vectors = jnp.transpose(vectors, (1, 0, 2)).reshape(count, width).astype(jnp.float32)
    weights = weights.reshape(weights.shape[0], -1, weights.shape[3])
    made, (grad_mid, branch, g_up, g_down, g_bias_up) = forward_and_feed(
        block_order, rows, weights, vectors, ups,
        w_up.T, w_down, b_up.astype(jnp.float32)[None, :], 1,
    )
    arrays = (block_order, rows, weights, vectors, *made, upstream_t, grad_mid)
    block_out_t, grad_input_t, g_qkv, g_out, sums = finish(arrays, branch, 3)
    block_out_t, grad_input_t, g_qkv, g_out, g_up, g_down = emit(
        shard, block_out_t, grad_input_t, g_qkv, g_out, g_up, g_down
    )
    sums = lax.dynamic_slice_in_dim(sums, lax.axis_index("dp") * shard, shard, 1)
    return (
        block_out_t.T[None],
        grad_input_t.T[None],
        sums[0],
        sums[1],
        g_qkv,
        sums[2],
        sums[3],
        g_out,
        sums[4],
        sums[5],
        sums[6],
        g_up.T,
        g_bias_up[0],
        g_down,
        sums[7],
    )


def solution(mesh):
    in_specs = (
        P("dp", "ctx", None),
        P("dp", "ctx", None),
        P(),
        P("dp"),
        P("dp"),
        P("dp", None),
        P("dp"),
        P("dp"),
        P("dp", None),
        P("dp"),
        P("dp"),
        P("dp"),
        P(None, "dp"),
        P("dp"),
        P("dp", None),
        P("dp"),
    )
    out_specs = (
        P("dp", "ctx", None),
        P("dp", "ctx", None),
        P("dp"),
        P("dp"),
        P("dp", "ctx"),
        P("dp"),
        P("dp"),
        P("dp", "ctx"),
        P("dp"),
        P("dp"),
        P("dp"),
        P("ctx", "dp"),
        P("dp"),
        P("dp", "ctx"),
        P("dp"),
    )
    return jax.shard_map(
        per_device, mesh=mesh, in_specs=in_specs, out_specs=out_specs, check_vma=False
    )
```

```python
import functools
import types

import jax
import jax.numpy as jnp
from jax import lax
from jax.experimental import pallas as pl
from jax.experimental.pallas import tpu as pltpu
from jax.sharding import PartitionSpec as P

HD = 64
SCALE = 0.125


def norm_parts(values, gain_values, shift_values):
    average = jnp.mean(values, axis=-1, keepdims=True)
    centered = values - average
    inverse = lax.rsqrt(jnp.mean(centered * centered, axis=-1, keepdims=True) + 1e-05)
    normed = centered * inverse
    return normed * gain_values + shift_values, normed, inverse


def norm_back(upstream, normed, inverse, gain_values):
    scaled = upstream * gain_values
    return inverse * (
        scaled
        - jnp.mean(scaled, axis=-1, keepdims=True)
        - normed * jnp.mean(scaled * normed, axis=-1, keepdims=True)
    )


def contract_first(left, right):
    return lax.dot_general(
        left, right, (((0,), (0,)), ((), ())), preferred_element_type=jnp.float32
    )


def contract_last(left, right):
    return lax.dot_general(
        left, right, (((1,), (1,)), ((), ())), preferred_element_type=jnp.float32
    )


def head_groups(width):
    groups = [(start, 128) for start in range(0, width - width % 128, 128)]
    if width % 128:
        groups.append((width - width % 128, width % 128))
    return groups


def head_masks(lanes):
    if lanes == HD:
        return [None]
    lane = lax.broadcasted_iota(jnp.int32, (1, lanes), 1)
    return [
        jnp.where((lane >= first) & (lane < first + HD), 1.0, 0.0).astype(jnp.bfloat16)
        for first in range(0, lanes, HD)
    ]


def keep(array, mask):
    return array if mask is None else array * mask


MESH = pl.DeviceIdType.MESH
CORES = 2
COLUMNS = 2
VMEM_LIMIT = 63 * 1024 * 1024
UP, DOWN, ACROSS, PARTNER = range(4)
SIDES = ((1, UP), (-1, DOWN))
GROUP = 8
FOLD = 2
FUSED_LIMIT = 9 * 1024 * 1024


def place():
    index = lax.axis_index("dp")
    lines = lax.axis_size("dp") // (CORES * COLUMNS)
    core = index % CORES
    column = (index // CORES) % COLUMNS
    return index // (CORES * COLUMNS), column, core, lines


def device_at(line, column, core):
    return (line * COLUMNS + column) * CORES + core


def on_line(line, lines):
    return (line >= 0) & (line < lines)


def greet():
    line, column, core, lines = place()
    cycle = lax.axis_size("ctx")
    mine = lax.axis_index("ctx")
    barrier = pltpu.get_barrier_semaphore()
    peers = [{"dp": device_at((line + by) % lines, column, core)} for by in range(1, lines)]
    peers += [{"dp": device_at(line, 1 - column, core)}, {"dp": device_at(line, column, 1 - core)}]
    peers += [{"ctx": (mine + by) % cycle} for by in range(1, cycle)]
    for peer in peers:
        pl.semaphore_signal(barrier, inc=1, device_id=peer, device_id_type=MESH)

    def met():
        pl.semaphore_wait(barrier, len(peers))

    return met


def remote(source, landing, send, recv, target):
    return pltpu.make_async_remote_copy(
        src_ref=source,
        dst_ref=landing,
        send_sem=send,
        recv_sem=recv,
        device_id=target,
        device_id_type=MESH,
    )


def fold(ref, values):
    half, width = values.shape[0] // FOLD, values.shape[1]
    for i in range(FOLD):
        part = values[i * half : (i + 1) * half]
        ref[:, i * width : (i + 1) * width] = part.astype(ref.dtype)


def fold_shape(rows, width):
    return rows // FOLD, FOLD * width


def unfold(values):
    width = values.shape[-1] // FOLD
    return [values[..., i * width : (i + 1) * width] for i in range(FOLD)]


def on_distance(by, act):
    line, _, _, lines = place()
    if by == 0:
        act(line, 0)
        return
    for step in (1, -1):

        @pl.when(on_line(line + step * by, lines))
        def _():
            act(line + step * by, step)


def nearest(d):
    line, _, _, lines = place()
    toward = 1 - 2 * ((2 * line) // lines)
    return (line + toward * d + lines) % lines


def gather_stream(own, land, send, recv, balanced):
    line, column, core, lines = place()
    me = device_at(line, column, core)
    beside = device_at(line, 1 - column, core)
    partner = device_at(line, column, 1 - core)

    def push(shard, way, target, source=None):
        source = land(shard) if source is None else source
        remote(source, land(shard), send(way, shard), recv(shard), {"dp": target}).start()

    def arrived(shard):
        buffer = land(shard)
        remote(buffer, buffer, send(PARTNER, shard), recv(shard), {"dp": partner}).wait_recv()

    def sent(shard, way):
        buffer = land(shard)
        remote(buffer, buffer, send(way, shard), recv(shard), {"dp": partner}).wait_send()

    def start():
        push(me, ACROSS, beside, own)
        for step, way in SIDES:

            @pl.when(on_line(line + step, lines))
            def _():
                push(me, way, device_at(line + step, column, core), own)

        push(me, PARTNER, partner, own)

    def crosses(source, act):
        if balanced:

            @pl.when((source != 0) & (source != lines - 1))
            def _():
                act()

        else:
            act()

    def relay(by, seen=None):
        for step, way in SIDES:

            @pl.when(on_line(line - step * by, lines))
            def _():
                shard = device_at(line - step * by, column, core)
                arrived(shard)

                @pl.when(on_line(line + step, lines))
                def _():
                    push(shard, way, device_at(line + step, column, core))

                crosses(line - step * by, lambda: push(shard, ACROSS, beside))
                push(shard, PARTNER, partner)
                if seen is not None:
                    seen(shard)

    def through(source, act):
        if balanced:
            for step, way in SIDES:
                end = 0 if step > 0 else lines - 1

                @pl.when((source == end) & on_line(line + step, lines))
                def _():
                    act(way, device_at(line + step, column, core))

    def cross(source, seen=None):
        shard = device_at(source, 1 - column, core)
        arrived(shard)
        through(source, lambda way, target: push(shard, way, target))
        push(shard, PARTNER, partner)
        if seen is not None:
            seen(shard)

    def finish():
        def visit(source, step):
            shard = device_at(source, column, core)
            far = device_at(source, 1 - column, core)
            sent(shard, PARTNER)
            sent(far, PARTNER)
            if step:
                crosses(source, lambda: sent(shard, ACROSS))
            else:
                sent(shard, ACROSS)
            through(source, lambda way, target: sent(far, way))
            for along, way in SIDES:
                if step in (0, -along):

                    @pl.when(on_line(line + along, lines))
                    def _():
                        sent(shard, way)

        for by in range(lines):
            on_distance(by, visit)

    return types.SimpleNamespace(
        start=start, relay=relay, cross=cross, arrived=arrived, finish=finish
    )


def reduce_stream(have, buffers, send, recv, settle):
    line, column, core, lines = place()
    side_buf, up_buf, down_buf, stash = buffers
    beside = device_at(line, 1 - column, core)

    def landed(buffer, way, slot):
        copy = remote(buffer, buffer, send.at[way, slot], recv.at[way, slot], {"dp": beside})
        copy.wait_recv()
        return buffer[...].astype(jnp.float32)

    def to_beside(target, step):
        chip = target * COLUMNS + 1 - column
        buffer = stash(chip)
        buffer[...] = have(chip).astype(buffer.dtype)
        remote(
            buffer,
            side_buf.at[target],
            send.at[1, target],
            recv.at[1, target],
            {"dp": beside},
        ).start()

    def along(target, step):
        chip = target * COLUMNS + column
        total = have(chip)
        total = total + landed(side_buf.at[target], 1, target)
        if step == 0:
            for by, way, landing in ((1, 2, up_buf), (-1, 3, down_buf)):
                settle_from(total, by, way, landing)
            return
        way, landing = (2, up_buf) if step > 0 else (3, down_buf)
        buffer = stash(chip)
        buffer[...] = total.astype(buffer.dtype)

        @pl.when(on_line(line - step, lines))
        def _():
            more = landed(landing.at[target], way, target)
            buffer[...] = (total + more).astype(buffer.dtype)

        remote(
            buffer,
            landing.at[target],
            send.at[way, target],
            recv.at[way, target],
            {"dp": device_at(line + step, column, core)},
        ).start()

    def settle_from(total, by, way, landing):
        if way == 2:
            settle(total, True)

        @pl.when(on_line(line - by, lines))
        def _():
            settle(landed(landing.at[line], way, line), False)

    def finish():
        def visit(target, step):
            buffer = side_buf.at[target]
            slots = [(1, target)]
            if step:
                slots.append((2 if step > 0 else 3, target))
            for way, slot in slots:
                remote(
                    buffer, buffer, send.at[way, slot], recv.at[way, slot], {"dp": beside}
                ).wait_send()

        for by in range(lines):
            on_distance(by, visit)

    return types.SimpleNamespace(to_beside=to_beside, along=along, finish=finish)


def pack_weights(vec_ref, qkv_ref, out_ref, w_ref, row):
    count, shard = vec_ref.shape
    cycle, padded, size = w_ref.shape
    width = out_ref.shape[1]
    for c in range(cycle):
        first, last = c * size, (c + 1) * size
        split = min(max(3 * width - first, 0), size)
        if split:
            w_ref[c, :shard, :split] = qkv_ref[:, first : first + split]
        if split < size:
            w_ref[c, :shard, split:] = out_ref[:, first + split - 3 * width : last - 3 * width]
    row[...] = jnp.zeros_like(row)
    for i in range(count):
        row[0:1, i * shard : (i + 1) * shard] = vec_ref[i : i + 1, :].astype(jnp.float32)
    for c in range(cycle):
        w_ref[c, shard:padded, :] = row[: padded - shard, :].astype(jnp.bfloat16)


def load_kernel(
    vec_ref, qkv_ref, out_ref, u_t_ref, x_t_ref, w_all, u_all, x_all, w_ref, row, u_ref, x_ref,
    w_send, w_recv, part_send, cycle_send, u_send, u_recv, x_send, x_recv, local,
):
    line, column, core, lines = place()
    cycle = lax.axis_size("ctx")
    mine = lax.axis_index("ctx")
    me = device_at(line, column, core)
    partner = device_at(line, column, 1 - core)
    others = [(mine + by) % cycle for by in range(1, cycle)]
    met = greet()
    pack_weights(vec_ref, qkv_ref, out_ref, w_ref, row)
    x_ref[...] = x_t_ref[...].T
    fold(u_ref, u_t_ref[...].astype(jnp.float32).T)
    met()

    weights = gather_stream(
        w_ref.at[mine],
        lambda shard: w_all.at[mine, shard],
        lambda way, shard: w_send.at[way, shard],
        lambda shard: w_recv.at[mine, shard],
        False,
    )
    ups = gather_stream(
        u_ref,
        lambda shard: u_all.at[shard],
        lambda way, shard: u_send.at[way, shard],
        lambda shard: u_recv.at[shard],
        True,
    )

    def part(c, shard, send, target, source=None):
        landing = w_all.at[c, shard]
        source = landing if source is None else source
        return remote(source, landing, send, w_recv.at[c, shard], target)

    def to_cycle(shard):
        for c in others:
            part(mine, shard, cycle_send.at[c, shard], {"ctx": c}).start()

    def from_cycle(shard):
        for c in others:
            copy = part(c, shard, part_send.at[c, shard], {"dp": partner})
            copy.wait_recv()
            copy.start()

    def swap(c, source):
        return remote(x_ref, x_all.at[source], x_send.at[c], x_recv.at[source], {"ctx": c})

    copies = [
        pltpu.make_async_copy(w_ref.at[c], w_all.at[c, me], local.at[c]) for c in range(cycle)
    ]
    copies.append(pltpu.make_async_copy(u_ref, u_all.at[me], local.at[cycle]))
    copies.append(pltpu.make_async_copy(x_ref, x_all.at[mine], local.at[cycle + 1]))
    weights.start()
    for c in others:
        swap(c, mine).start()
    ups.start()
    for c in others:
        part(c, me, part_send.at[c, me], {"dp": partner}, w_ref.at[c]).start()
    for copy in copies:
        copy.start()

    for d in range(lines):
        if d + 1 < lines:
            weights.relay(d + 1, to_cycle)
            ups.relay(d + 1)
        on_distance(d, lambda source, step: weights.cross(source, to_cycle))
        on_distance(d, lambda source, step: ups.cross(source))
        if d > 0:
            on_distance(d, lambda source, step: from_cycle(device_at(source, column, core)))
            on_distance(d - 1, lambda source, step: from_cycle(device_at(source, 1 - column, core)))
    on_distance(
        lines - 1, lambda source, step: from_cycle(device_at(source, 1 - column, core))
    )
    for chip in range(lines * COLUMNS):
        shard = chip * CORES + 1 - core
        weights.arrived(shard)
        ups.arrived(shard)
        for c in others:
            part(c, shard, part_send.at[c, shard], {"dp": partner}).wait_recv()
    weights.finish()
    ups.finish()
    for c in others:
        swap(c, c).wait_recv()
        swap(c, mine).wait_send()
        part(c, me, part_send.at[c, me], {"dp": partner}).wait_send()
    for d in range(lines):
        for across in (column, 1 - column):
            if d == 0 and across is column:
                continue
            shard = device_at(nearest(d), across, core)
            for c in others:
                part(c, shard, part_send.at[c, shard], {"dp": partner}).wait_send()
                part(mine, shard, cycle_send.at[c, shard], {"ctx": c}).wait_send()
    for copy in copies:
        copy.wait()


def load(vectors, w_qkv, w_out, ups_t, rows_t, collective_id):
    peers = lax.axis_size("dp")
    cycle = lax.axis_size("ctx")
    shard = w_out.shape[0]
    padded = (shard // GROUP + 1) * GROUP
    size = 4 * w_out.shape[1] // cycle
    block = ups_t.shape[::-1]
    bf16 = jnp.bfloat16
    dma = pltpu.SemaphoreType.DMA
    return pl.pallas_call(
        load_kernel,
        out_shape=(
            jax.ShapeDtypeStruct((cycle, peers, padded, size), bf16),
            jax.ShapeDtypeStruct((peers,) + fold_shape(*block), bf16),
            jax.ShapeDtypeStruct((cycle,) + block, bf16),
        ),
        in_specs=whole_vmem(5),
        out_specs=tuple([pl.BlockSpec(memory_space=pl.ANY)] * 3),
        scratch_shapes=[
            pltpu.VMEM((cycle, padded, size), bf16),
            pltpu.VMEM((GROUP, size), jnp.float32),
            pltpu.VMEM(fold_shape(*block), bf16),
            pltpu.VMEM(block, bf16),
            dma((4, peers)),
            dma((cycle, peers)),
            dma((cycle, peers)),
            dma((cycle, peers)),
            dma((4, peers)),
            dma((peers,)),
            dma((cycle,)),
            dma((cycle,)),
            dma((cycle + 2,)),
        ],
        compiler_params=pltpu.CompilerParams(collective_id=collective_id, has_side_effects=True),
    )(vectors, w_qkv, w_out, ups_t, rows_t)


def nothing(*_):
    return None


def spreader(width, shard, padded):
    source = lax.broadcasted_iota(jnp.int32, (width, 1), 0).astype(jnp.float32)
    block = jnp.floor((source + 0.5) * (1.0 / shard))
    target = source + block * float(padded - shard)
    lanes = lax.broadcasted_iota(jnp.int32, (1, width // shard * padded), 1).astype(jnp.float32)
    return jnp.where(target == lanes, 1.0, 0.0).astype(jnp.bfloat16)


def visible_bias(order_ref, first, rows, keys):
    block = keys // order_ref.shape[0]

    def position(slot):
        where = slot
        for b in range(order_ref.shape[0]):
            inside = (slot >= b * block) & (slot < (b + 1) * block)
            where = jnp.where(inside, (order_ref[b] - b) * block + slot, where)
        return where

    query = position(first + lax.broadcasted_iota(jnp.int32, (rows, 1), 0))
    key = position(lax.broadcasted_iota(jnp.int32, (1, keys), 1))
    return jnp.where(query >= key, 0.0, -1e30)


def parts_over(first, last, size, count):
    return [c for c in range(count) if c * size < last and (c + 1) * size > first]


def forward_kernel(*refs):
    forward_body(nothing, *refs)


def forward_body(
    ready, order_ref, x_ref, w_ref, vec_ref,
    spread_ref, normed_ref, q_ref, k_ref, v_ref, o_ref, o_spread_ref, h_ref, mid_ref,
    projected,
):
    cycle, rows, width = x_ref.shape
    shard = width // lax.axis_size("dp")
    mine = lax.axis_index("ctx")
    size = w_ref.shape[2]
    padded = w_ref.shape[1] // lax.axis_size("dp")
    spread_ref[...] = spreader(width, shard, padded)
    gain_one, shift_one, bias_q, bias_v, bias_o, gain_two, shift_two = [
        vec_ref[i : i + 1, :] for i in range(7)
    ]

    def project(left, first, last):
        for c in parts_over(first, last, size, cycle):
            projected[:, c * size : (c + 1) * size] = jnp.dot(
                left, w_ref[c], preferred_element_type=jnp.float32
            )

    def visit(c, carry):
        block = pl.ds(pl.multiple_of(c * rows, rows), rows)
        values, _, _ = norm_parts(x_ref[c].astype(jnp.float32), gain_one, shift_one)
        spread = jnp.dot(
            values.astype(jnp.bfloat16), spread_ref[...], preferred_element_type=jnp.float32
        ).astype(jnp.bfloat16)
        normed_ref[block, :] = spread

        @pl.when(c == 0)
        def _():
            ready()

        project(spread, 0, 3 * width)
        k_ref[block, :] = projected[:, width : 2 * width].astype(jnp.bfloat16)
        v_ref[block, :] = (projected[:, 2 * width : 3 * width] + bias_v).astype(jnp.bfloat16)

        @pl.when(c == mine)
        def _():
            q_ref[...] = (projected[:, :width] + bias_q).astype(jnp.bfloat16)

        return carry

    lax.fori_loop(0, cycle, visit, 0)
    bias = visible_bias(order_ref, mine * rows, rows, cycle * rows)
    for start, lanes in head_groups(width):
        block = slice(start, start + lanes)
        q, k, v = q_ref[:, block], k_ref[:, block], v_ref[:, block]
        total = None
        for mask in head_masks(lanes):
            scores = contract_last(keep(q, mask), k) * SCALE + bias
            largest = jnp.max(scores, axis=-1, keepdims=True)
            exponent = jnp.exp(scores - largest)
            inverse = 1.0 / jnp.sum(exponent, axis=-1, keepdims=True)
            part = jnp.dot(
                exponent.astype(jnp.bfloat16), keep(v, mask), preferred_element_type=jnp.float32
            )
            part = part * inverse
            total = part if total is None else total + part
        o_ref[:, block] = total.astype(jnp.bfloat16)
    o_spread = jnp.dot(
        o_ref[...], spread_ref[...], preferred_element_type=jnp.float32
    ).astype(jnp.bfloat16)
    o_spread_ref[...] = o_spread
    project(o_spread, 3 * width, 4 * width)
    hidden = x_ref[mine].astype(jnp.float32) + projected[:, 3 * width : 4 * width] + bias_o
    h_ref[...] = hidden
    fold(mid_ref, norm_parts(hidden, gain_two, shift_two)[0])


def ordered(count):
    return [pl.BlockSpec(memory_space=pltpu.SMEM)] + whole_vmem(count - 1)


def forward_shapes(x, w):
    cycle, rows, width = x.shape
    full = w.shape[1]
    f32, bf16 = jnp.float32, jnp.bfloat16
    outs = [
        ((width, full), bf16),
        ((cycle * rows, full), bf16),
        ((rows, width), bf16),
        ((cycle * rows, width), bf16),
        ((cycle * rows, width), bf16),
        ((rows, width), bf16),
        ((rows, full), bf16),
        ((rows, width), f32),
    ]
    return outs, (fold_shape(rows, width), bf16), ((rows, 4 * width), f32)


def forward(order, x, w, vectors):
    outs, mid, projected = forward_shapes(x, w)
    return pl.pallas_call(
        forward_kernel,
        out_shape=tuple(jax.ShapeDtypeStruct(*entry) for entry in outs + [mid]),
        in_specs=ordered(4),
        out_specs=tuple(whole_vmem(len(outs) + 1)),
        scratch_shapes=[pltpu.VMEM(*projected)],
        compiler_params=pltpu.CompilerParams(vmem_limit_bytes=VMEM_LIMIT),
    )(order, x, w, vectors)


def column_sum(values):
    return jnp.sum(values, axis=0, keepdims=True)


def store_owners(grads, ref, padded):
    for s in range(grads.shape[0] // padded):
        ref[s] = grads[s * padded : (s + 1) * padded].astype(ref.dtype)


def weigh_columns(slab_ref, c, normed_ref, wide):
    padded, tall = slab_ref.shape[2:]
    grads = contract_first(normed_ref[...], wide[:, c * tall : (c + 1) * tall])
    store_owners(grads, slab_ref.at[c], padded)


def weigh_kernel(normed_ref, wide_ref, slab_ref):
    for c in range(slab_ref.shape[0]):
        weigh_columns(slab_ref, c, normed_ref, wide_ref)


def back_norm(r):
    rows, width = r.hidden.shape
    gain, shift = r.vec[5:6, :], r.vec[6:7, :]
    _, normed, inverse = norm_parts(r.hidden[...], gain, shift)
    upstream = r.upstream_t[...].T.astype(jnp.float32)
    grad_mid = r.grad_mid[...]
    r.sums[0:2, :] = jnp.zeros((2, width), jnp.float32)
    r.sums[5:6, :] = column_sum(grad_mid * normed)
    r.sums[6:7, :] = column_sum(grad_mid)
    r.sums[7:8, :] = column_sum(upstream)
    grad_hidden = upstream + norm_back(grad_mid, normed, inverse, gain)
    r.dh[...] = grad_hidden
    r.sums[4:5, :] = column_sum(grad_hidden)
    grad_hidden_b = grad_hidden.astype(jnp.bfloat16)
    r.head_wide[...] = jnp.zeros_like(r.head_wide)
    r.head_wide[:, 3 * width : 4 * width] = grad_hidden_b
    grads = contract_first(r.o_spread[...], grad_hidden_b)
    store_owners(grads, r.out_slab, r.out_slab.shape[1])


def back_attend(r):
    cycle, rows, width = r.x.shape
    mine = lax.axis_index("ctx")
    size = r.w.shape[2]
    grad_ctx = None
    for c in parts_over(3 * width, 4 * width, size, cycle):
        more = contract_last(r.head_wide[:, c * size : (c + 1) * size], r.w[c])
        grad_ctx = more if grad_ctx is None else grad_ctx + more
    grad_ctx = contract_last(grad_ctx.astype(jnp.bfloat16), r.spread[...])
    r.do[...] = grad_ctx.astype(jnp.bfloat16)
    r.wide[...] = jnp.zeros_like(r.wide)
    own = pl.ds(pl.multiple_of(mine * rows, rows), rows)
    bias = visible_bias(r.order, mine * rows, rows, cycle * rows)
    for start, lanes in head_groups(width):
        block = slice(start, start + lanes)
        q, k, v = r.q[:, block], r.k[:, block], r.v[:, block]
        do, o = r.do[:, block], r.o[:, block]
        product = do.astype(jnp.float32) * o.astype(jnp.float32)
        dq = dk = dv = None
        for mask in head_masks(lanes):
            q_h, k_h, do_h = keep(q, mask), keep(k, mask), keep(do, mask)
            product_h = product if mask is None else product * mask.astype(jnp.float32)
            delta = jnp.sum(product_h, axis=-1, keepdims=True)
            scores = contract_last(q_h, k) * SCALE + bias
            largest = jnp.max(scores, axis=-1, keepdims=True)
            exponent = jnp.exp(scores - largest)
            p = exponent * (1.0 / jnp.sum(exponent, axis=-1, keepdims=True))
            dp = contract_last(do_h, v)
            ds = (p * (dp - delta)).astype(jnp.bfloat16)
            dv_h = contract_first(p.astype(jnp.bfloat16), do_h)
            dq_h = jnp.dot(ds, k_h, preferred_element_type=jnp.float32)
            dk_h = contract_first(ds, q_h)
            dq = dq_h if dq is None else dq + dq_h
            dk = dk_h if dk is None else dk + dk_h
            dv = dv_h if dv is None else dv + dv_h
        dq = dq * SCALE
        r.wide[own, start : start + lanes] = dq.astype(jnp.bfloat16)
        r.wide[:, width + start : width + start + lanes] = (dk * SCALE).astype(jnp.bfloat16)
        r.wide[:, 2 * width + start : 2 * width + start + lanes] = dv.astype(jnp.bfloat16)
        r.sums[2:3, block] = column_sum(dq)
        r.sums[3:4, block] = column_sum(dv)


def back_rows(r):
    cycle, rows, width = r.x.shape
    mine = lax.axis_index("ctx")
    size = r.w.shape[2]
    gain, shift = r.vec[0:1, :], r.vec[1:2, :]

    def visit(block, carry):
        span = pl.ds(pl.multiple_of(block * rows, rows), rows)
        total = None
        for c in parts_over(0, 3 * width, size, cycle):
            more = contract_last(r.wide[span, c * size : (c + 1) * size], r.w[c])
            total = more if total is None else total + more
        high = total.astype(jnp.bfloat16)
        low = (total - high.astype(jnp.float32)).astype(jnp.bfloat16)
        grad = contract_last(high, r.spread[...]) + contract_last(low, r.spread[...])
        _, normed, _ = norm_parts(r.x[block].astype(jnp.float32), gain, shift)
        r.sums[0:1, :] += column_sum(grad * normed)
        r.sums[1:2, :] += column_sum(grad)
        r.da[block] = grad.astype(jnp.bfloat16)

        @pl.when(block == mine)
        def _():
            r.da_own[...] = grad

        return carry

    lax.fori_loop(0, cycle, visit, 0)


BACK_INS = [
    "order", "x", "w", "vec", "spread", "normed", "q", "k", "v", "o", "o_spread", "hidden",
    "upstream_t", "grad_mid",
]
BACK_MADE = ["sums", "da", "da_own", "dh", "out_slab"]
BACK_KEPT = ["wide", "head_wide", "do"]


def back_kernel(*refs):
    r = types.SimpleNamespace(**dict(zip(BACK_INS + BACK_MADE + BACK_KEPT, refs)))
    back_norm(r)
    back_attend(r)
    back_rows(r)


def back_shapes(x, padded):
    cycle, rows, width = x.shape
    f32, bf16 = jnp.float32, jnp.bfloat16
    made = [
        ((8, width), f32),
        ((cycle, rows, width), bf16),
        ((rows, width), f32),
        ((rows, width), f32),
        ((lax.axis_size("dp"), padded, width), bf16),
    ]
    kept = [((cycle * rows, 4 * width), bf16), ((rows, 4 * width), bf16), ((rows, width), bf16)]
    return made, kept


def backward(arrays, padded):
    named = dict(zip(BACK_INS, arrays))
    cycle, rows, width = named["x"].shape
    made, kept = back_shapes(named["x"], padded)
    params = pltpu.CompilerParams(vmem_limit_bytes=VMEM_LIMIT)
    sums, da, da_own, dh, out_slab, wide = pl.pallas_call(
        back_kernel,
        out_shape=tuple(jax.ShapeDtypeStruct(*entry) for entry in made + kept[:1]),
        in_specs=ordered(len(arrays)),
        out_specs=tuple(whole_vmem(len(made) + 1)),
        scratch_shapes=[pltpu.VMEM(*entry) for entry in kept[1:]],
        compiler_params=params,
    )(*arrays)
    slab = pl.pallas_call(
        weigh_kernel,
        out_shape=jax.ShapeDtypeStruct(
            (cycle, out_slab.shape[0], padded, 3 * width // cycle), jnp.bfloat16
        ),
        in_specs=whole_vmem(2),
        out_specs=whole_vmem(1)[0],
        compiler_params=params,
    )(named["normed"], wide)
    return slab, sums, da, da_own, dh, out_slab


def whole_vmem(count):
    return [pl.BlockSpec(memory_space=pltpu.VMEM)] * count


def ffn_kernel(*refs):
    ffn_body(nothing, *refs)


def middle_kernel(count, *refs):
    order, x, w_far, vec, ups, up_t, down, b_up = refs[:8]
    made, rest = refs[8 : 8 + count], refs[8 + count :]
    outs, (w, w_sem, mid, projected), kept = rest[:5], rest[5:9], rest[9:]
    copies = [
        pltpu.make_async_copy(w_far.at[c], w.at[c], w_sem.at[c]) for c in range(w.shape[0])
    ]

    def ready():
        for copy in copies:
            copy.wait()

    def before():
        for copy in copies:
            copy.start()
        forward_body(ready, order, x, w, vec, *made, mid, projected)

    ffn_body(before, mid, ups, up_t, down, b_up, *outs, *kept)


def ffn_body(
    before, mid_ref, ups_far, w_up_t_ref, w_down_ref, b_up_ref,
    gm_ref, br_far, gup_ref, gdown_ref, gb_ref,
    ups_ref, br_ref, ups_sem, br_sem, mids, parts, acts, grads, up_total, down_total, give, take, bias_part, bias_all,
    core_buf, side_buf, up_buf, down_buf,
    g_send, g_recv, c_send, c_recv, r_send, r_recv, y_send, y_recv, b_send, b_recv,
):
    line, column, core, lines = place()
    rows, width = gm_ref.shape
    cycle = lax.axis_size("ctx")
    mine = lax.axis_index("ctx")
    me = device_at(line, column, core)
    partner = device_at(line, column, 1 - core)
    met = greet()
    ups_copy = pltpu.make_async_copy(ups_far, ups_ref, ups_sem)
    ups_copy.start()
    before()
    mids[me] = mid_ref[...]
    met()

    def br_copy(chip):
        pair = pl.ds(chip * CORES, CORES)
        return pltpu.make_async_copy(br_ref.at[pair], br_far.at[pair], br_sem.at[chip])

    def spread(ref, chip):
        pieces = unfold(ref[pl.ds(chip * CORES, CORES)])
        pieces = [piece.reshape(CORES * rows // FOLD, width) for piece in pieces]
        return jnp.concatenate(pieces, axis=0)

    def gather_rows(ref, chip, values):
        half = CORES * rows // FOLD
        for i in range(FOLD):
            piece = values[i * half : (i + 1) * half].astype(ref.dtype)
            piece = piece.reshape(CORES, rows // FOLD, width)
            ref[pl.ds(chip * CORES, CORES), :, i * width : (i + 1) * width] = piece

    gather = gather_stream(
        mid_ref,
        lambda shard: mids.at[shard],
        lambda way, shard: g_send.at[way, shard],
        lambda shard: g_recv.at[shard],
        False,
    )
    gather.start()
    bias_part[...] = jnp.zeros_like(bias_part)

    def to_core(chip):
        return remote(
            parts.at[chip * CORES + 1 - core],
            core_buf.at[chip],
            c_send.at[chip],
            c_recv.at[chip],
            {"dp": partner},
        )

    def feed(chip):
        mid = spread(mids, chip)
        ups = spread(ups_ref, chip)
        pre = contract_last(mid, w_up_t_ref[...]) + b_up_ref[...].astype(jnp.float32)
        grad = contract_last(ups, w_down_ref[...])
        half = 0.5 * (1.0 + lax.erf(pre * 0.7071067811865476))
        act = (pre * half).astype(jnp.bfloat16)
        grad = grad * (half + pre * jnp.exp(-0.5 * pre * pre) * 0.3989422804014327)
        bias_part[...] += jnp.sum(grad, axis=0, keepdims=True)
        grad = grad.astype(jnp.bfloat16)
        acts[chip] = act
        grads[chip] = grad
        part = jnp.dot(grad, w_up_t_ref[...], preferred_element_type=jnp.float32)
        gather_rows(parts, chip, part)
        to_core(chip).start()
        branch = jnp.dot(act, w_down_ref[...], preferred_element_type=jnp.float32)
        gather_rows(br_ref, chip, branch)
        br_copy(chip).start()

    def visit(d, carry):
        @pl.when(d + 1 < lines)
        def _():
            gather.relay(d + 1)

        at = nearest(d)
        gather.arrived(device_at(at, column, 1 - core))
        feed(at * COLUMNS + column)
        gather.cross(at)
        gather.arrived(device_at(at, 1 - column, 1 - core))
        feed(at * COLUMNS + 1 - column)
        return carry

    ups_copy.wait()
    lax.fori_loop(0, lines, visit, 0)

    def have(chip):
        to_core(chip).wait_recv()
        return core_buf[chip].astype(jnp.float32) + parts[chip * CORES + core].astype(jnp.float32)

    def settle(total, first):
        half = rows // FOLD
        for i, piece in enumerate(unfold(total)):
            span = slice(i * half, (i + 1) * half)
            gm_ref[span, :] = piece if first else gm_ref[span, :] + piece

    reduce = reduce_stream(
        have,
        (side_buf, up_buf, down_buf, lambda chip: parts.at[chip * CORES + core]),
        r_send,
        r_recv,
        settle,
    )
    for by in range(lines - 1, -1, -1):
        on_distance(by, reduce.to_beside)

    def swap(c, source):
        return remote(give.at[c], take.at[source], y_send.at[c], y_recv.at[source], {"ctx": c})

    def swap_bias(c, source):
        landing = bias_all.at[source]
        return remote(bias_part, landing, b_send.at[c], b_recv.at[source], {"ctx": c})

    bias_all[mine] = bias_part[...]
    others = [(mine + by) % cycle for by in range(1, cycle)]
    for c in others:
        swap_bias(c, mine).start()
    up_total[...] = jnp.zeros_like(up_total)
    down_total[...] = jnp.zeros_like(down_total)

    def weigh(chip, carry):
        up_total[...] += contract_first(grads[chip], spread(mids, chip))
        down_total[...] += contract_first(acts[chip], spread(ups_ref, chip))
        return carry

    lax.fori_loop(0, lines * COLUMNS, weigh, 0)
    size = width // cycle
    for c in range(cycle):
        up_part = up_total[:, c * size : (c + 1) * size]
        down_part = down_total[:, c * size : (c + 1) * size]

        @pl.when(c == mine)
        def _():
            gup_ref[...] = up_part
            gdown_ref[...] = down_part

        @pl.when(c != mine)
        def _():
            give[c, 0] = up_part.astype(give.dtype)
            give[c, 1] = down_part.astype(give.dtype)
            swap(c, mine).start()

    for by in range(lines - 1, -1, -1):
        on_distance(by, reduce.along)
    for c in others:
        swap(c, c).wait_recv()
        gup_ref[...] += take[c, 0].astype(jnp.float32)
        gdown_ref[...] += take[c, 1].astype(jnp.float32)
        swap_bias(c, c).wait_recv()
    total = bias_all[0]
    for c in range(1, cycle):
        total = total + bias_all[c]
    gb_ref[...] = total
    for c in others:
        swap(c, mine).wait_send()
        swap_bias(c, mine).wait_send()
    for chip in range(lines * COLUMNS):
        to_core(chip).wait_send()
        br_copy(chip).wait()
    reduce.finish()
    gather.finish()


def ffn_shapes(rows, width, hidden):
    peers = lax.axis_size("dp")
    cycle = lax.axis_size("ctx")
    lines = peers // (CORES * COLUMNS)
    chips = lines * COLUMNS
    dma = pltpu.SemaphoreType.DMA
    f32, bf16 = jnp.float32, jnp.bfloat16
    thin = width // cycle

    def slabs(count):
        return pltpu.VMEM((count,) + fold_shape(rows, width), bf16)

    outs = [
        ((rows, width), f32),
        ((peers,) + fold_shape(rows, width), bf16),
        ((hidden, thin), f32),
        ((hidden, thin), f32),
        ((1, hidden), f32),
    ]
    kept = [
        slabs(peers),
        slabs(peers),
        dma(()),
        dma((chips,)),
        slabs(peers),
        slabs(peers),
        pltpu.VMEM((chips, CORES * rows, hidden), bf16),
        pltpu.VMEM((chips, CORES * rows, hidden), bf16),
        pltpu.VMEM((hidden, width), f32),
        pltpu.VMEM((hidden, width), f32),
        pltpu.VMEM((cycle, 2, hidden, thin), bf16),
        pltpu.VMEM((cycle, 2, hidden, thin), bf16),
        pltpu.VMEM((1, hidden), f32),
        pltpu.VMEM((cycle, 1, hidden), f32),
        slabs(chips),
        slabs(lines),
        slabs(lines),
        slabs(lines),
        dma((4, peers)),
        dma((peers,)),
        dma((chips,)),
        dma((chips,)),
        dma((4, lines)),
        dma((4, lines)),
        dma((cycle,)),
        dma((cycle,)),
        dma((cycle,)),
        dma((cycle,)),
    ]
    return outs, kept


def forward_and_feed(order, x, w, vectors, ups, w_up_t, w_down, b_up, collective_id):
    cycle, rows, width = x.shape
    hidden = w_down.shape[0]
    outs, kept = ffn_shapes(rows, width, hidden)
    made, mid, projected = forward_shapes(x, w)
    near = pl.BlockSpec(memory_space=pltpu.VMEM)
    far = pl.BlockSpec(memory_space=pl.ANY)
    out_specs = [near, far, near, near, near]
    params = pltpu.CompilerParams(
        collective_id=collective_id, has_side_effects=True, vmem_limit_bytes=VMEM_LIMIT
    )
    tail = (ups, w_up_t, w_down, b_up)
    shapes = [jax.ShapeDtypeStruct(*entry) for entry in outs]
    if w.size + ups.size < FUSED_LIMIT:
        scratch = [pltpu.VMEM(w.shape, w.dtype), pltpu.SemaphoreType.DMA((cycle,))]
        scratch += [pltpu.VMEM(*mid), pltpu.VMEM(*projected)]
        results = pl.pallas_call(
            functools.partial(middle_kernel, len(made)),
            out_shape=tuple([jax.ShapeDtypeStruct(*entry) for entry in made] + shapes),
            in_specs=ordered(2) + [far, near, far, near, near, near],
            out_specs=tuple(whole_vmem(len(made)) + out_specs),
            scratch_shapes=scratch + kept,
            compiler_params=params,
        )(order, x, w, vectors, *tail)
        return results[: len(made)], results[len(made) :]
    *made, mid = forward(order, x, w, vectors)
    return made, pl.pallas_call(
        ffn_kernel,
        out_shape=tuple(shapes),
        in_specs=[near, far, near, near, near],
        out_specs=tuple(out_specs),
        scratch_shapes=kept,
        compiler_params=params,
    )(mid, *tail)


def settle_body(r, early, middle, late):
    line, column, core, lines = place()
    rows, width = r.dh.shape
    cycle = lax.axis_size("ctx")
    mine = lax.axis_index("ctx")
    beside = device_at(line, 1 - column, core)
    partner = device_at(line, column, 1 - core)
    others = [(mine + by) % cycle for by in range(1, cycle)]
    chips = range(lines * COLUMNS)
    local = [
        pltpu.make_async_copy(
            r.br.at[chip * CORES + core], r.br_own.at[chip], r.local.at[chip]
        )
        for chip in chips
    ]
    met = greet()
    for copy in local:
        copy.start()
    met()

    def to_core(name, chip):
        source = getattr(r, name)
        sems = getattr(r, name + "_core_sems")
        return remote(
            source.at[chip * CORES + 1 - core],
            getattr(r, name + "_core").at[chip],
            sems.at[0, chip],
            sems.at[1, chip],
            {"dp": partner},
        )

    def slab_to_core(c, chip):
        return remote(
            r.slab.at[c, chip * CORES + 1 - core],
            r.slab_core.at[c, chip],
            r.slab_core_sems.at[0, c, chip],
            r.slab_core_sems.at[1, c, chip],
            {"dp": partner},
        )

    def slab_to_cycle(c, chip, source):
        return remote(
            r.slab_core.at[c, chip],
            r.slab_cycle.at[source, chip],
            r.slab_cycle_sems.at[0, c, chip],
            r.slab_cycle_sems.at[1, source, chip],
            {"ctx": c},
        )

    def swap(name, slot, c, source):
        sems = r.swap_sems
        return remote(
            getattr(r, name).at[c],
            getattr(r, name + "_all").at[source],
            sems.at[0, slot, c],
            sems.at[1, slot, source],
            {"ctx": c},
        )

    def both(act):
        def visit(target, step):
            act(target * COLUMNS + 1 - column)
            act(target * COLUMNS + column)

        return visit

    def far_first(act):
        for by in range(lines - 1, -1, -1):
            on_distance(by, act)

    one = r.one_sems
    sums_to_core = remote(r.sums, r.sums_core, one.at[0, 0], one.at[1, 0], {"dp": partner})
    sums_to_side = remote(r.stage.at[0], r.sums_side, one.at[0, 1], one.at[1, 1], {"dp": beside})

    def sums_to_line(to, source):
        return remote(
            r.stage.at[1],
            r.sums_line.at[source],
            r.line_sems.at[0, to],
            r.line_sems.at[1, source],
            {"dp": device_at(to, column, core)},
        )

    def sums_to_cycle(c, source):
        return remote(
            r.stage.at[2],
            r.sums_cycle.at[source],
            r.swap_sems.at[0, 2, c],
            r.swap_sems.at[1, 2, source],
            {"ctx": c},
        )

    def cycle_sums(chip):
        for c in others:
            slab_to_core(c, chip).wait_recv()
            total = r.slab_core[c, chip].astype(jnp.float32)
            total = total + r.slab[c, chip * CORES + core].astype(jnp.float32)
            r.slab_core[c, chip] = total.astype(r.slab_core.dtype)
            slab_to_cycle(c, chip, mine).start()

    def br_have(chip):
        to_core("br", chip).wait_recv()
        return r.br_core[chip].astype(jnp.float32) + r.br_own[chip].astype(jnp.float32)

    def out_have(chip):
        to_core("out_slab", chip).wait_recv()
        own = r.out_slab[chip * CORES + core].astype(jnp.float32)
        return r.out_slab_core[chip].astype(jnp.float32) + own

    def slab_have(chip):
        slab_to_core(mine, chip).wait_recv()
        total = r.slab_core[mine, chip].astype(jnp.float32)
        total = total + r.slab[mine, chip * CORES + core].astype(jnp.float32)
        for c in others:
            slab_to_cycle(c, chip, c).wait_recv()
            total = total + r.slab_cycle[c, chip].astype(jnp.float32)
        return total

    def into(ref):
        def settle(total, first):
            ref[...] = total if first else ref[...] + total

        return settle

    def stream(have, name, stash, ref):
        sems = getattr(r, name + "_sems")
        lanes = [getattr(r, name + "_lanes").at[i] for i in range(3)]
        return reduce_stream(have, (*lanes, stash), sems.at[0], sems.at[1], into(ref))

    branch = stream(br_have, "br", lambda chip: r.br_own.at[chip], r.branch_sum)
    heads = stream(out_have, "out_slab", lambda chip: r.out_slab_core.at[chip], r.out_sum)
    slabs = stream(slab_have, "slab", lambda chip: r.slab_core.at[mine, chip], r.slab_sum)

    for across in (1 - column, column):
        far_first(lambda target, step: to_core("br", target * COLUMNS + across).start())
    early()
    for copy in local:
        copy.wait()
    far_first(both(lambda chip: to_core("out_slab", chip).start()))
    far_first(branch.to_beside)
    middle(True)
    for c in others:
        far_first(both(lambda chip: slab_to_core(c, chip).start()))
    ahead = range(lines - 1, max(lines - 3, -1), -1)
    for by in ahead:
        on_distance(by, both(cycle_sums))
    far_first(heads.to_beside)
    middle(False)
    far_first(both(lambda chip: slab_to_core(mine, chip).start()))
    for by in range(ahead[-1] - 1, -1, -1):
        on_distance(by, both(cycle_sums))
    on_distance(lines - 1, branch.along)
    late()
    sums_to_core.start()
    for c in others:
        swap("da", 0, c, mine).start()
    sums_to_core.wait_recv()
    r.stage[0] = r.sums[...] + r.sums_core[...]
    sums_to_side.start()

    for by in range(lines - 1, -1, -1):
        if by + 1 < lines:
            on_distance(by, branch.along)
        on_distance(by, slabs.to_beside)
        on_distance(by, heads.along)
        if by + 1 < lines:
            on_distance(by + 1, slabs.along)
        if by == min(1, lines - 1):
            sums_to_side.wait_recv()
            r.stage[1] = r.stage[0] + r.sums_side[...]
            r.sums_line[line] = r.stage[1]
            for away in range(1, lines):
                sums_to_line((line + away) % lines, line).start()
    thin = r.out_half.shape[1]
    for c in range(cycle):
        piece = r.out_sum[:, c * thin : (c + 1) * thin]

        @pl.when(c == mine)
        def _():
            r.out_half[...] = piece

        @pl.when(c != mine)
        def _():
            r.give[c] = piece.astype(r.give.dtype)
            swap("give", 1, c, mine).start()

    for away in range(1, lines):
        source = (line + away) % lines
        sums_to_line(source, source).wait_recv()
    total = r.sums_line[0]
    for by in range(1, lines):
        total = total + r.sums_line[by]
    r.stage[2] = total
    r.sums_cycle[mine] = total
    for c in others:
        sums_to_cycle(c, mine).start()
    branch_rows = jnp.concatenate(unfold(r.branch_sum[...]), axis=0)
    on_distance(0, slabs.along)
    r.out_t[...] = (r.hidden[...] + branch_rows + r.vec[7:8, :]).astype(r.out_t.dtype).T
    grad = r.da_own[...]
    for c in others:
        swap("da", 0, c, c).wait_recv()
        grad = grad + r.da_all[c].astype(jnp.float32)
    gain, bias = r.vec[0:1, :], r.vec[1:2, :]
    _, normed, inverse = norm_parts(r.x[mine].astype(jnp.float32), gain, bias)
    r.ing_t[...] = (r.dh[...] + norm_back(grad, normed, inverse, gain)).T
    for c in others:
        swap("give", 1, c, c).wait_recv()
        r.out_half[...] += r.give_all[c].astype(jnp.float32)
        sums_to_cycle(c, c).wait_recv()
    total = r.sums_cycle[0]
    for c in range(1, cycle):
        total = total + r.sums_cycle[c]
    r.total[...] = total

    sums_to_core.wait_send()
    sums_to_side.wait_send()
    for c in others:
        sums_to_cycle(c, mine).wait_send()
        swap("da", 0, c, mine).wait_send()
        swap("give", 1, c, mine).wait_send()
    for away in range(1, lines):
        sums_to_line((line + away) % lines, line).wait_send()
    branch.finish()
    heads.finish()
    slabs.finish()
    for chip in chips:
        to_core("br", chip).wait_send()
        to_core("out_slab", chip).wait_send()
        slab_to_core(mine, chip).wait_send()
        for c in others:
            slab_to_core(c, chip).wait_send()
            slab_to_cycle(c, chip, mine).wait_send()


SETTLE_OUTS = ["out_t", "ing_t", "slab_sum", "out_half", "total"]
SETTLE_KEPT = [
    "slab_core", "slab_cycle", "slab_lanes", "br_own", "br_core", "br_lanes", "out_slab_core",
    "out_slab_lanes", "out_sum", "branch_sum", "da_all", "give", "give_all", "stage", "sums_core",
    "sums_side", "sums_line", "sums_cycle", "local", "slab_core_sems", "slab_cycle_sems",
    "slab_sems", "br_core_sems", "br_sems", "out_slab_core_sems", "out_slab_sems", "swap_sems",
    "one_sems", "line_sems",
]


def settle_kernel(names, *refs):
    r = types.SimpleNamespace(**dict(zip(names + SETTLE_OUTS + SETTLE_KEPT, refs)))
    settle_body(r, nothing, nothing, nothing)


LATE = ["w", "spread", "q", "k", "v", "o", "normed"]


def finish_kernel(names, *refs):
    names = names + SETTLE_OUTS + SETTLE_KEPT + BACK_MADE + BACK_KEPT + ["slab"] + LATE
    r = types.SimpleNamespace(**dict(zip(names + ["late_sems"], refs)))
    cycle = r.w.shape[0]
    mine = lax.axis_index("ctx")
    copies = [
        pltpu.make_async_copy(getattr(r, name + "_far"), getattr(r, name), r.late_sems.at[i])
        for i, name in enumerate(LATE)
    ]
    for copy in copies:
        copy.start()

    def middle(away):
        if away:
            for copy in copies:
                copy.wait()
            back_attend(r)
        for c in range(cycle):

            @pl.when((c != mine) if away else (c == mine))
            def _():
                weigh_columns(r.slab, c, r.normed, r.wide)

    settle_body(r, lambda: back_norm(r), middle, lambda: back_rows(r))


def settle_shapes(cycle, peers, padded, rows, width):
    lines = peers // (CORES * COLUMNS)
    chips = lines * COLUMNS
    tall, thin = 3 * width // cycle, width // cycle
    folded = fold_shape(rows, width)
    dma = pltpu.SemaphoreType.DMA
    f32, bf16 = jnp.float32, jnp.bfloat16

    def buffer(dtype, *shape):
        return pltpu.VMEM(shape, dtype)

    outs = [
        ((width, rows), bf16),
        ((width, rows), f32),
        ((padded, tall), f32),
        ((padded, thin), f32),
        ((8, width), f32),
    ]
    kept = [
        buffer(bf16, cycle, chips, padded, tall),
        buffer(bf16, cycle, chips, padded, tall),
        buffer(bf16, 3, lines, padded, tall),
        buffer(bf16, chips, *folded),
        buffer(bf16, chips, *folded),
        buffer(bf16, 3, lines, *folded),
        buffer(bf16, chips, padded, width),
        buffer(bf16, 3, lines, padded, width),
        buffer(f32, padded, width),
        buffer(f32, *folded),
        buffer(bf16, cycle, rows, width),
        buffer(bf16, cycle, padded, thin),
        buffer(bf16, cycle, padded, thin),
        buffer(f32, 3, 8, width),
        buffer(f32, 8, width),
        buffer(f32, 8, width),
        buffer(f32, lines, 8, width),
        buffer(f32, cycle, 8, width),
        dma((chips,)),
        dma((2, cycle, chips)),
        dma((2, cycle, chips)),
        dma((2, 4, lines)),
        dma((2, chips)),
        dma((2, 4, lines)),
        dma((2, chips)),
        dma((2, 4, lines)),
        dma((2, 3, cycle)),
        dma((2, 2)),
        dma((2, lines)),
    ]
    return outs, kept


def emit_kernel(count, out_t, ing_t, slab_sum, out_half, up_t, down, *refs):
    outs = refs[:count]
    shard = outs[2].shape[0]
    outs[0][...] = out_t[...]
    outs[1][...] = ing_t[...]
    outs[2][...] = slab_sum[:shard, :]
    outs[3][...] = out_half[:shard, :]
    outs[4][...] = up_t[...]
    outs[5][...] = down[...]


def emit(shard, *arrays):
    shapes = [a.shape for a in arrays]
    shapes[2:4] = [(shard, shape[1]) for shape in shapes[2:4]]
    return pl.pallas_call(
        functools.partial(emit_kernel, len(arrays)),
        out_shape=tuple(jax.ShapeDtypeStruct(t, a.dtype) for t, a in zip(shapes, arrays)),
        in_specs=whole_vmem(len(arrays)),
        out_specs=tuple(whole_vmem(len(arrays))),
    )(*arrays)


def finish(arrays, br, collective_id):
    named = dict(zip(BACK_INS, arrays))
    x, w = named["x"], named["w"]
    cycle, rows, width = x.shape
    peers = lax.axis_size("dp")
    padded = w.shape[1] // peers
    outs, kept = settle_shapes(cycle, peers, padded, rows, width)
    made, back_kept = back_shapes(x, padded)
    slab = ((cycle, peers, padded, 3 * width // cycle), jnp.bfloat16)
    params = pltpu.CompilerParams(
        collective_id=collective_id, has_side_effects=True, vmem_limit_bytes=VMEM_LIMIT
    )
    out_shape = tuple(jax.ShapeDtypeStruct(*entry) for entry in outs)
    far = pl.BlockSpec(memory_space=pl.ANY)
    if w.size + slab[0][0] * peers * padded * slab[0][3] < FUSED_LIMIT:
        names = [name + "_far" if name in LATE else name for name in BACK_INS] + ["br"]
        specs = ordered(len(arrays))
        for name in LATE:
            specs[BACK_INS.index(name)] = far
        extra = [pltpu.VMEM(*entry) for entry in made + back_kept + [slab]]
        extra += [pltpu.VMEM(named[name].shape, named[name].dtype) for name in LATE]
        extra += [pltpu.SemaphoreType.DMA((len(LATE),))]
        return pl.pallas_call(
            functools.partial(finish_kernel, names),
            out_shape=out_shape,
            in_specs=specs + [far],
            out_specs=tuple(whole_vmem(len(outs))),
            scratch_shapes=kept + extra,
            compiler_params=params,
        )(*arrays, br)
    slabs, sums, da, da_own, dh, out_slab = backward(arrays, padded)
    names = ["slab", "sums", "da", "da_own", "dh", "out_slab", "hidden", "x", "vec", "br"]
    return pl.pallas_call(
        functools.partial(settle_kernel, names),
        out_shape=out_shape,
        in_specs=whole_vmem(9) + [far],
        out_specs=tuple(whole_vmem(len(outs))),
        scratch_shapes=kept,
        compiler_params=params,
    )(slabs, sums, da, da_own, dh, out_slab, named["hidden"], x, named["vec"], br)


def per_device(
    block_in,
    cotangent,
    block_order,
    ln1_gain,
    ln1_bias,
    w_qkv,
    b_query,
    b_value,
    w_out,
    b_out,
    ln2_gain,
    ln2_bias,
    w_up,
    b_up,
    w_down,
    b_down,
):
    width, shard = w_out.shape[1], w_out.shape[0]
    peers = lax.axis_size("dp")
    rows_t, upstream_t = block_in[0].T, cotangent[0].T
    vectors = jnp.stack(
        [ln1_gain, ln1_bias, b_query, b_value, b_out, ln2_gain, ln2_bias, b_down]
    )
    count = vectors.shape[0]
    weights, ups, rows = load(vectors, w_qkv, w_out, upstream_t, rows_t, 0)
    vectors = weights[0, :, shard, : count * shard].reshape(peers, count, shard)
    vectors = jnp.transpose(vectors, (1, 0, 2)).reshape(count, width).astype(jnp.float32)
    weights = weights.reshape(weights.shape[0], -1, weights.shape[3])
    made, (grad_mid, branch, g_up, g_down, g_bias_up) = forward_and_feed(
        block_order, rows, weights, vectors, ups,
        w_up.T, w_down, b_up[None, :], 1,
    )
    arrays = (block_order, rows, weights, vectors, *made, upstream_t, grad_mid)
    block_out_t, grad_input_t, g_qkv, g_out, sums = finish(arrays, branch, 3)
    block_out_t, grad_input_t, g_qkv, g_out, g_up, g_down = emit(
        shard, block_out_t, grad_input_t, g_qkv, g_out, g_up, g_down
    )
    sums = lax.dynamic_slice_in_dim(sums, lax.axis_index("dp") * shard, shard, 1)
    return (
        block_out_t.T[None],
        grad_input_t.T[None],
        sums[0],
        sums[1],
        g_qkv,
        sums[2],
        sums[3],
        g_out,
        sums[4],
        sums[5],
        sums[6],
        g_up.T,
        g_bias_up[0],
        g_down,
        sums[7],
    )


def solution(mesh):
    in_specs = (
        P("dp", "ctx", None),
        P("dp", "ctx", None),
        P(),
        P("dp"),
        P("dp"),
        P("dp", None),
        P("dp"),
        P("dp"),
        P("dp", None),
        P("dp"),
        P("dp"),
        P("dp"),
        P(None, "dp"),
        P("dp"),
        P("dp", None),
        P("dp"),
    )
    out_specs = (
        P("dp", "ctx", None),
        P("dp", "ctx", None),
        P("dp"),
        P("dp"),
        P("dp", "ctx"),
        P("dp"),
        P("dp"),
        P("dp", "ctx"),
        P("dp"),
        P("dp"),
        P("dp"),
        P("ctx", "dp"),
        P("dp"),
        P("dp", "ctx"),
        P("dp"),
    )
    return jax.shard_map(
        per_device, mesh=mesh, in_specs=in_specs, out_specs=out_specs, check_vma=False
    )
```
